32 devices in a mesh: sec: 4 (over x, core), row: 4 (over z), col: 2 (over y).
Axes of the slice: x: 2, y: 2, z: 4, core: 2. Of those that a mesh axis runs over, the one named last changes fastest.
Arguments:
- forcing: float32 [4, 8192, 128], P('sec', ('row', 'col')), may hold values from -6 to 6
- inverse_factor: bfloat16 [4, 2, 8192, 8192], P('sec', None, 'col', 'row'), as said below
- diag_inverse: float32 [4, 2, 8192], P('sec', None, 'col'), may hold values from -0.6 to 0.6
- coupling: float32 [4, 2, 8192], P('sec', None, ('row', 'col')), may hold values from -0.8 to 0.8
Outputs:
- section_fields: float32 [4, 8192, 128], P('sec', ('row', 'col'))
The draws below stay inside these ranges and needn't reach their ends.
Inputs may be any that keep to these rules, and one draw needn't show every extreme that they name: `inverse_factor`: each section's factor is lower triangular: entries above the diagonal are zero in both parts.
All inputs are finite; a program needn't handle non-finite values.
Results may differ from the reference program's by a relative error of at most 0.03.
Values may be sent and summed in bfloat16 or wider, within the bound.
A program may use at most 128 MiB of HBM per device.

```python
import jax
import jax.numpy as jnp
from jax import lax

F = 8192
R = 64
SECTIONS = 4
N_ROW = 4
N_COL = 2


def draw_inverse_factor(key, part):

    def one_section(index):
        section_key = jax.random.fold_in(key, index)
        values = jax.random.normal(section_key, (2, F, F), jnp.float32)
        rows = lax.broadcasted_iota(jnp.int32, (F, F), 0)
        cols = lax.broadcasted_iota(jnp.int32, (F, F), 1)
        lower = cols < rows
        diagonal = cols == rows
        reach = (rows - cols).astype(jnp.float32) / F
        spread = (0.3 + 2.4 * reach) / F ** 0.5
        real_part = jnp.where(lower, values[0] * spread, jnp.where(diagonal, 1.0, 0.0))
        imag_part = jnp.where(lower, values[1] * spread, jnp.where(diagonal, 0.5 * jnp.sin(values[1] * 3.0), 0.0))
        return jnp.stack([real_part, imag_part], axis=0).astype(jnp.bfloat16)
    return lax.map(one_section, jnp.arange(SECTIONS, dtype=jnp.int32))


def draw_forcing(key, part):
    value_key = jax.random.fold_in(key, 11)
    values = jnp.clip(jax.random.normal(value_key, (SECTIONS, F, 2 * R), jnp.float32), -6.0, 6.0)
    section = lax.broadcasted_iota(jnp.int32, (SECTIONS, 1, 1), 0)
    scale = jnp.where(section == 0, 1.0, 0.08)
    return (values * scale).astype(jnp.float32)


def draw_coupling(key, part):
    sign_key = jax.random.fold_in(key, 21)
    size_key = jax.random.fold_in(key, 22)
    signs = jnp.where(jax.random.uniform(sign_key, (SECTIONS, 2, F), jnp.float32) < 0.5, 1.0, -1.0)
    sizes = jax.random.uniform(size_key, (SECTIONS, 2, F), jnp.float32, 0.4, 0.8)
    return (signs * sizes).astype(jnp.float32)


def level_of(stream_key, dims, pieces, smallest, high):
    gain, own = 1.0, jax.random.fold_in(stream_key, 6)
    for position, parts in pieces:
        draws = jnp.exp(jax.random.uniform(jax.random.fold_in(own, position), (parts,), jnp.float32, smallest / len(pieces), high / len(pieces)))
        gain = gain * jnp.repeat(draws, dims[position] // parts).reshape([-1 if axis == position else 1 for axis in range(len(dims))])
    return gain


def setup_inputs(seed: int = 0) -> dict:
    arg_keys = jax.random.split(jax.random.key(seed), 5)
    forcing = draw_forcing(jax.random.fold_in(arg_keys[4], 71), 0)
    inverse_factor = draw_inverse_factor(jax.random.fold_in(arg_keys[4], 71), 0)
    diag_inverse = jnp.clip(jax.random.uniform(arg_keys[2], (SECTIONS, 2, F), jnp.float32, -0.6, 0.6) * level_of(arg_keys[2], (SECTIONS, 2, F), ((0, 4), (2, 2)), -0.4, 0.0), -0.6, 0.6)
    coupling = draw_coupling(jax.random.fold_in(arg_keys[4], 71), 0)
    return dict(forcing=forcing, inverse_factor=inverse_factor, diag_inverse=diag_inverse, coupling=coupling)


def complex_rows(coef_re, coef_im, values, half):
    v_re = values[:, :half]
    v_im = values[:, half:]
    out_re = coef_re[:, None] * v_re - coef_im[:, None] * v_im
    out_im = coef_re[:, None] * v_im + coef_im[:, None] * v_re
    return jnp.concatenate([out_re, out_im], axis=1)


def combine_parts(prod_re, prod_im, half):
    out_re = prod_re[:, :half] - prod_im[:, half:]
    out_im = prod_re[:, half:] + prod_im[:, :half]
    return jnp.concatenate([out_re, out_im], axis=1)


def forward_product(factor, source, half):
    width = factor.shape[2] // N_ROW
    total = jnp.zeros((factor.shape[1], source.shape[1]), jnp.float32)
    for block in range(N_ROW):
        lo = block * width
        piece = source[lo:lo + width]
        part_re = jnp.dot(factor[0][:, lo:lo + width], piece, preferred_element_type=jnp.float32)
        part_im = jnp.dot(factor[1][:, lo:lo + width], piece, preferred_element_type=jnp.float32)
        partial_sum = combine_parts(part_re, part_im, half).astype(jnp.bfloat16).astype(jnp.float32)
        total = total + partial_sum
    return total


def back_product(factor, scaled, half):
    width = factor.shape[1] // N_COL
    total = jnp.zeros((factor.shape[2], scaled.shape[1]), jnp.float32)
    for block in range(N_COL):
        lo = block * width
        piece = scaled[lo:lo + width]
        part_re = jnp.dot(factor[0][lo:lo + width].T, piece, preferred_element_type=jnp.float32)
        part_im = jnp.dot(factor[1][lo:lo + width].T, piece, preferred_element_type=jnp.float32)
        partial_sum = combine_parts(part_re, part_im, half).astype(jnp.bfloat16).astype(jnp.float32)
        total = total + partial_sum
    return total


def reference(forcing, inverse_factor, diag_inverse, coupling):
    half = forcing.shape[2] // 2
    previous = jnp.zeros(forcing.shape[1:], jnp.float32)
    results = []
    for section in range(SECTIONS):
        factor = inverse_factor[section]
        couple = coupling[section]
        source = (forcing[section] - complex_rows(couple[0], couple[1], previous, half)).astype(jnp.bfloat16)
        forward = forward_product(factor, source, half)
        dinv = diag_inverse[section]
        scaled = complex_rows(dinv[0], dinv[1], forward, half).astype(jnp.bfloat16)
        field = back_product(factor, scaled, half)
        results.append(field)
        previous = field
    return jnp.stack(results, axis=0)
```

```python
import functools

import jax
import jax.numpy as jnp
from jax import lax
from jax.experimental import pallas as pl
from jax.experimental.pallas import tpu as pltpu
from jax.sharding import PartitionSpec as P


def shifted(value, axis, steps):
    count = lax.axis_size(axis)
    initial, last = (max(0, -steps), min(count, count - steps))
    return lax.ppermute(value, axis, [(source, source + steps) for source in range(initial, last)])


def complex_rows(coef_re, coef_im, values, half):
    v_re = values[:, :half]
    v_im = values[:, half:]
    out_re = coef_re[:, None] * v_re - coef_im[:, None] * v_im
    out_im = coef_re[:, None] * v_im + coef_im[:, None] * v_re
    return jnp.concatenate([out_re, out_im], axis=1)


def combine_stack(product):
    half = product.shape[2] // 2
    out_re = product[0, :, :half] - product[1, :, half:]
    out_im = product[0, :, half:] + product[1, :, :half]
    return jnp.concatenate([out_re, out_im], axis=1)


def solve_section(source, factor, dinv):
    width = source.shape[1]
    product = jnp.einsum(
        "kij,jb->kib",
        factor,
        lax.all_gather(source, "col", axis=0, tiled=True),
        preferred_element_type=jnp.float32,
    )
    forward = combine_stack(product)
    share = lax.psum_scatter(
        forward.astype(jnp.bfloat16), "row", scatter_dimension=0, tiled=True
    ).astype(jnp.float32)
    share_rows = share.shape[0]
    local_dinv = lax.dynamic_slice_in_dim(dinv, lax.axis_index("row") * share_rows, share_rows, 1)
    scaled = complex_rows(local_dinv[0], local_dinv[1], share, width // 2).astype(jnp.bfloat16)
    product = jnp.einsum(
        "kij,ib->kjb",
        factor,
        lax.all_gather(scaled, "row", axis=0, tiled=True),
        preferred_element_type=jnp.float32,
    )
    back = combine_stack(product)
    return lax.psum_scatter(
        back.astype(jnp.bfloat16), "col", scatter_dimension=0, tiled=True
    ).astype(jnp.float32)


def local(forcing, inverse_factor, diag_inverse, coupling):
    sections = lax.axis_size("sec")
    section_id = lax.axis_index("sec")
    local_rhs = forcing[0]
    factor = inverse_factor[0]
    dinv = diag_inverse[0]
    couple = coupling[0]
    rows_here = local_rhs.shape[0]
    half = local_rhs.shape[1] // 2
    block_count = 1
    block_width = half // block_count
    rhs_blocks = local_rhs.reshape(rows_here, 2, block_count, block_width)
    results = jnp.zeros((rows_here, 2, block_count, block_width), jnp.float32)
    outgoing = jnp.zeros((rows_here, 2 * block_width), jnp.float32)
    for step_index in range(block_count + sections - 1):
        if step_index > 0:
            incoming = shifted(outgoing.astype(jnp.bfloat16), "sec", 1).astype(outgoing.dtype)
        else:
            incoming = jnp.zeros((rows_here, 2 * block_width), jnp.float32)
        block_index = step_index - section_id
        active = jnp.logical_and(block_index >= 0, block_index < block_count)
        safe_index = jnp.clip(block_index, 0, block_count - 1)
        current = lax.dynamic_index_in_dim(rhs_blocks, safe_index, 2, keepdims=False)
        current = current.reshape(rows_here, 2 * block_width)
        source = (current - complex_rows(couple[0], couple[1], incoming, block_width)).astype(
            jnp.bfloat16
        )
        field = solve_section(source, factor, dinv)
        updated = lax.dynamic_update_index_in_dim(
            results, field.reshape(rows_here, 2, block_width), safe_index, 2
        )
        results = jnp.where(active, updated, results)
        outgoing = field
    return results.reshape(1, rows_here, 2 * half)


MESH = pl.DeviceIdType.MESH

CHUNKS = 8
HALF = CHUNKS // 2
PARTS = 4
PLANS = {
    (1, 0): (0o04, 0o05, 0o06, 0o07, 0o00, 0o01, 0o02, 0o03, 0o30, 0o31, 0o32, 0o34, 0o35, 0o36, 0o37, 0o33),
    (1, 1): (0o00, 0o01, 0o04, 0o02, 0o20, 0o14, 0o05, 0o21, 0o15, 0o06, 0o16, 0o22, 0o07, 0o17, 0o24, 0o10, 0o03, 0o25, 0o11, 0o26, 0o12, 0o34, 0o27, 0o13, 0o30, 0o23, 0o35, 0o31, 0o36, 0o32, 0o37, 0o33),
    (1, 2): (0o00, 0o01, 0o04, 0o02, 0o24, 0o05, 0o25, 0o06, 0o26, 0o07, 0o27, 0o14, 0o03, 0o15, 0o34, 0o16, 0o35, 0o36, 0o17, 0o37, 0o30, 0o31, 0o32, 0o33),
    (1, 3): (0o04, 0o05, 0o06, 0o07, 0o34, 0o35, 0o36, 0o37),
    (0, 0): (0o04, 0o05, 0o06, 0o07, 0o00, 0o01, 0o02, 0o03, 0o30, 0o31, 0o32, 0o33, 0o34, 0o35, 0o36, 0o37),
    (0, 1): (0o04, 0o05, 0o06, 0o07, 0o34, 0o35, 0o36, 0o37),
}
PER_WORD = 6


def plan_words(codes):
    words = []
    for i in range(0, len(codes), PER_WORD):
        words.append(sum(code * 32**j for j, code in enumerate(codes[i : i + PER_WORD])))
    return len(codes), words


def sweep_kernel(
    n_sec, n_row, n_col, forcing, dinv, coupling, factor_hbm, out,
    factor, src_a, src_b, own, pre_in, suf_in, pre_out, suf_out,
    lhs, back, y_out, y_in, prev_out, prev_in, forcing_t, coupling_all,
    load_sem, src_send, src_recv, pre_send, pre_recv, suf_send, suf_recv,
    y_send, y_recv, prev_send, prev_recv,
    rhs_send, rhs_recv, coef_send, coef_recv,
):
    chunk = own.shape[1]
    half = own.shape[2] // 2
    share = forcing_t.shape[2]
    part = back.shape[2]
    s, r, c = lax.axis_index("sec"), lax.axis_index("row"), lax.axis_index("col")
    other = 1 - c
    ends = s == n_sec - 1
    active = r <= 2 * c + 1
    paired = r < 2

    def last(k):
        return 2 * c + k // HALF

    def chunk_rows(k):
        return pl.ds(pl.multiple_of(k * chunk, chunk), chunk)

    def load(k):
        rows = chunk_rows(k)
        return pltpu.make_async_copy(
            factor_hbm.at[0, :, rows, :], factor.at[:, rows, :], load_sem.at[k]
        )

    def half_rows(col):
        return pl.ds(pl.multiple_of(col * share, share), share)

    def remote(src, dst, send_sem, recv_sem, device):
        return pltpu.make_async_remote_copy(
            src_ref=src, dst_ref=dst, send_sem=send_sem, recv_sem=recv_sem,
            device_id=device, device_id_type=MESH,
        )

    here = (s, r, c)
    across = (s, r, other)
    after = (lax.rem(s + 1, n_sec), r, c)

    def send_source():
        rows = half_rows(c)
        return remote(src_a.at[rows], src_a.at[rows], src_send, src_recv, across)

    def send_rhs():
        return remote(forcing_t.at[c], forcing_t.at[c], rhs_send, rhs_recv, across)

    def send_coef():
        return remote(coupling_all.at[c], coupling_all.at[c], coef_send, coef_recv, across)

    def send_pre(k):
        return remote(
            pre_out.at[k], pre_in.at[k], pre_send.at[k], pre_recv.at[k],
            (s, lax.rem(r + 1, n_row), c),
        )

    def send_suf(k):
        return remote(
            suf_out.at[k], suf_in.at[k], suf_send.at[k], suf_recv.at[k],
            (s, lax.rem(r + n_row - 1, n_row), c),
        )

    def send_y(j):
        return remote(y_out.at[j], y_in.at[j], y_send.at[j], y_recv.at[j], across)

    def send_prev(j):
        return remote(prev_out.at[j], prev_in.at[j], prev_send.at[j], prev_recv.at[j], after)

    count = jnp.int32(0)
    words = [jnp.int32(0)] * max(len(plan_words(plan)[1]) for plan in PLANS.values())
    for (col, row), plan in PLANS.items():
        mine = jnp.logical_and(c == col, r == row)
        length, packed = plan_words(plan)
        count = jnp.where(mine, length, count)
        for i, word in enumerate(packed):
            words[i] = jnp.where(mine, word, words[i])

    inside = jnp.logical_and(c == 1, jnp.logical_or(r == 1, r == 2))
    for i, first in enumerate((0, 1, 4, 2, 5, 6, 7, 3)):
        k = jnp.where(inside, first, (i + HALF) % CHUNKS)

        @pl.when(r <= last(k))
        def _(k=k):
            load(k).start()

    barrier = pltpu.get_barrier_semaphore()
    for device in (
        (s, lax.rem(r + 1, n_row), c), (s, lax.rem(r + n_row - 1, n_row), c), across,
        after, (lax.rem(s + n_sec - 1, n_sec), r, c),
    ):
        pl.semaphore_signal(barrier, 1, device_id=device, device_id_type=MESH)
    pl.semaphore_wait(barrier, 5)

    def turned(value):
        return jnp.concatenate([-value[:, half:], value[:, :half]], axis=1)

    @pl.when(s == 0)
    def _():
        src_a[half_rows(c), :] = forcing[0].astype(jnp.bfloat16)
        send_source().start()
        src_b[half_rows(c), :] = turned(forcing[0].astype(jnp.bfloat16).astype(jnp.float32)).astype(
            jnp.bfloat16
        )
        back[...] = jnp.zeros_like(back)
        send_source().wait_recv()
        rows = half_rows(other)
        src_b[rows, :] = turned(src_a[rows, :].astype(jnp.float32)).astype(jnp.bfloat16)

    @pl.when(s > 0)
    def _():
        forcing_t[c] = forcing[0].T
        coupling_all[c] = coupling[0]
        send_rhs().start()
        send_coef().start()
        back[...] = jnp.zeros_like(back)
        send_rhs().wait_recv()
        send_coef().wait_recv()

        @pl.when(active)
        def _():
            for j in range(PARTS):
                send_prev(j).wait_recv()
                col, at = divmod(j * part, share)
                cols = slice(at, at + part)
                previous = prev_in[j].astype(jnp.float32)
                p_re, p_im = previous[:half], previous[half:]
                c_re, c_im = coupling_all[col, 0:1, cols], coupling_all[col, 1:2, cols]
                new_re = forcing_t[col, :half, cols] - (c_re * p_re - c_im * p_im)
                new_im = forcing_t[col, half:, cols] - (c_re * p_im + c_im * p_re)
                rows = slice(j * part, (j + 1) * part)
                src_a[rows, :] = jnp.concatenate([new_re, new_im], axis=0).T.astype(jnp.bfloat16)
                src_b[rows, :] = jnp.concatenate([-new_im, new_re], axis=0).T.astype(jnp.bfloat16)

    def forward_step(k):
        load(k).wait()
        rows = chunk_rows(k)
        total = jnp.dot(factor[0, rows, :], src_a[...], preferred_element_type=jnp.float32)
        total += jnp.dot(factor[1, rows, :], src_b[...], preferred_element_type=jnp.float32)
        own[k] = total

        @pl.when(jnp.logical_and(r == 0, last(k) > 0))
        def _():
            pre_out[k] = own[k].astype(jnp.bfloat16)
            send_pre(k).start()

        @pl.when(jnp.logical_and(r > 0, r == last(k)))
        def _():
            suf_out[k] = own[k].astype(jnp.bfloat16)
            send_suf(k).start()

    def relay_right(k):
        send_pre(k).wait_recv()
        pre_out[k] = (own[k] + pre_in[k].astype(jnp.float32)).astype(jnp.bfloat16)
        send_pre(k).start()

    def relay_left(k):
        send_suf(k).wait_recv()
        suf_out[k] = (own[k] + suf_in[k].astype(jnp.float32)).astype(jnp.bfloat16)
        send_suf(k).start()

    def back_step(k):
        @pl.when(r > 0)
        def _():
            @pl.when(r == last(k))
            def _():
                send_pre(k).wait_recv()

            own[k] += pre_in[k].astype(jnp.float32)

        @pl.when(r < last(k))
        def _():
            @pl.when(r == 0)
            def _():
                send_suf(k).wait_recv()

            own[k] += suf_in[k].astype(jnp.float32)

        rows = chunk_rows(k)
        forward = own[k].T
        d_re, d_im = dinv[0, 0:1, rows], dinv[0, 1:2, rows]
        f_re, f_im = forward[:half], forward[half:]
        s_re, s_im = d_re * f_re - d_im * f_im, d_re * f_im + d_im * f_re
        lhs[0] = jnp.concatenate([s_re, s_im], axis=0).astype(jnp.bfloat16)
        lhs[1] = jnp.concatenate([-s_im, s_re], axis=0).astype(jnp.bfloat16)
        total = jnp.dot(lhs[0], factor[0, rows, :], preferred_element_type=jnp.float32)
        total += jnp.dot(lhs[1], factor[1, rows, :], preferred_element_type=jnp.float32)
        for j in range(PARTS):
            back[j] += total[:, j * part : (j + 1) * part]

    @pl.loop(0, count)
    def _(e):
        at = e // PER_WORD
        word = words[0]
        for i in range(1, len(words)):
            word = jnp.where(at == i, words[i], word)
        code = lax.rem(lax.shift_right_logical(word, 5 * lax.rem(e, PER_WORD)), 32)
        k = lax.rem(code, CHUNKS)
        step = code // CHUNKS
        for i, action in enumerate((forward_step, relay_right, relay_left, back_step)):
            @pl.when(step == i)
            def _(action=action):
                action(k)

    def order(first, i):
        return (2 * first + i) % PARTS if isinstance(first, int) else lax.rem(2 * first + i, PARTS)

    def sends_y(i):
        wanted = jnp.logical_or(paired, c == 1) if i < 2 else paired
        return wanted if i < 2 else jnp.logical_and(wanted, jnp.logical_not(ends))

    def takes_y(i):
        wanted = jnp.logical_or(paired, c == 0) if i < 2 else paired
        return wanted if i < 2 else jnp.logical_and(wanted, jnp.logical_not(ends))

    for i in range(PARTS):
        j = order(other, i)

        @pl.when(sends_y(i))
        def _(j=j):
            y_out[j] = back[j].astype(jnp.bfloat16)
            send_y(j).start()

    passes = jnp.logical_and(active, jnp.logical_not(ends))
    for i in range(PARTS):
        j = order(c, i)

        @pl.when(takes_y(i))
        def _(j=j):
            send_y(j).wait_recv()
            back[j] += y_in[j].astype(jnp.float32)

        @pl.when(passes)
        def _(j=j):
            prev_out[j] = back[j].astype(jnp.bfloat16)
            send_prev(j).start()

    for i in range(2):
        out[0, i * part : (i + 1) * part, :] = back[order(c, i)].T

    @pl.when(s == 0)
    def _():
        send_source().wait_send()

    @pl.when(s > 0)
    def _():
        send_rhs().wait_send()
        send_coef().wait_send()

    for k in range(CHUNKS):
        @pl.when(r < last(k))
        def _(k=k):
            send_pre(k).wait_send()

        @pl.when(jnp.logical_and(r > 0, r <= last(k)))
        def _(k=k):
            send_suf(k).wait_send()

    for i in range(PARTS):
        @pl.when(sends_y(i))
        def _(i=i):
            send_y(order(other, i)).wait_send()

        @pl.when(passes)
        def _(i=i):
            send_prev(i).wait_send()


def sweep(n_sec, n_row, n_col, forcing, inverse_factor, diag_inverse, coupling):
    share, width = forcing.shape[1:]
    block_rows, block_cols = inverse_factor.shape[2:]
    chunk, part = block_rows // CHUNKS, block_cols // PARTS
    vmem = pl.BlockSpec(memory_space=pltpu.VMEM)
    bf16, f32 = jnp.bfloat16, jnp.float32
    dma = pltpu.SemaphoreType.DMA
    return pl.pallas_call(
        functools.partial(sweep_kernel, n_sec, n_row, n_col),
        out_shape=jax.ShapeDtypeStruct(forcing.shape, f32),
        in_specs=[vmem, vmem, vmem, pl.BlockSpec(memory_space=pl.ANY)],
        out_specs=vmem,
        scratch_shapes=[
            pltpu.VMEM((2, block_rows, block_cols), bf16),
            pltpu.VMEM((block_cols, width), bf16),
            pltpu.VMEM((block_cols, width), bf16),
            pltpu.VMEM((CHUNKS, chunk, width), f32),
            pltpu.VMEM((CHUNKS, chunk, width), bf16),
            pltpu.VMEM((CHUNKS, chunk, width), bf16),
            pltpu.VMEM((CHUNKS, chunk, width), bf16),
            pltpu.VMEM((CHUNKS, chunk, width), bf16),
            pltpu.VMEM((2, width, chunk), bf16),
            pltpu.VMEM((PARTS, width, part), f32),
            pltpu.VMEM((PARTS, width, part), bf16),
            pltpu.VMEM((PARTS, width, part), bf16),
            pltpu.VMEM((PARTS, width, part), bf16),
            pltpu.VMEM((PARTS, width, part), bf16),
            pltpu.VMEM((n_col, width, share), f32),
            pltpu.VMEM((n_col, 2, share), f32),
            dma((CHUNKS,)),
            dma, dma,
            dma((CHUNKS,)), dma((CHUNKS,)),
            dma((CHUNKS,)), dma((CHUNKS,)),
            dma((PARTS,)), dma((PARTS,)),
            dma((PARTS,)), dma((PARTS,)),
            dma, dma, dma, dma,
        ],
        compiler_params=pltpu.CompilerParams(
            collective_id=0, has_side_effects=True, vmem_limit_bytes=56 * 2**20
        ),
    )(forcing, diag_inverse, coupling, inverse_factor)


def solution(mesh):
    placed = (
        P("sec", ("row", "col"), None),
        P("sec", None, "col", "row"),
        P("sec", None, "col"),
        P("sec", None, ("row", "col")),
    )
    n_sec, n_row, n_col = (mesh.shape[axis] for axis in ("sec", "row", "col"))

    def body(forcing, inverse_factor, diag_inverse, coupling):
        share, width = forcing.shape[1:]
        fits = inverse_factor.size * 2 <= 32 * 2**20
        block = inverse_factor.shape[2] == 4 * share and inverse_factor.shape[3] == 2 * share
        if share % 256 or width % 128 or not fits or n_sec < 3 or (n_row, n_col) != (4, 2) or not block:
            return local(forcing, inverse_factor, diag_inverse, coupling)
        return sweep(n_sec, n_row, n_col, forcing, inverse_factor, diag_inverse, coupling)

    return jax.shard_map(
        body, mesh=mesh, in_specs=placed, out_specs=P("sec", ("row", "col"), None), check_vma=False
    )
```

```python
import functools

import jax
import jax.numpy as jnp
from jax import lax
from jax.experimental import pallas as pl
from jax.experimental.pallas import tpu as pltpu
from jax.sharding import PartitionSpec as P


def shifted(value, axis, steps):
    count = lax.axis_size(axis)
    initial, last = (max(0, -steps), min(count, count - steps))
    return lax.ppermute(value, axis, [(source, source + steps) for source in range(initial, last)])


def complex_rows(coef_re, coef_im, values, half):
    v_re = values[:, :half]
    v_im = values[:, half:]
    out_re = coef_re[:, None] * v_re - coef_im[:, None] * v_im
    out_im = coef_re[:, None] * v_im + coef_im[:, None] * v_re
    return jnp.concatenate([out_re, out_im], axis=1)


def combine_stack(product):
    half = product.shape[2] // 2
    out_re = product[0, :, :half] - product[1, :, half:]
    out_im = product[0, :, half:] + product[1, :, :half]
    return jnp.concatenate([out_re, out_im], axis=1)


def solve_section(source, factor, dinv):
    width = source.shape[1]
    product = jnp.einsum(
        "kij,jb->kib",
        factor,
        lax.all_gather(source, "col", axis=0, tiled=True),
        preferred_element_type=jnp.float32,
    )
    forward = combine_stack(product)
    share = lax.psum_scatter(
        forward.astype(jnp.bfloat16), "row", scatter_dimension=0, tiled=True
    ).astype(jnp.float32)
    share_rows = share.shape[0]
    local_dinv = lax.dynamic_slice_in_dim(dinv, lax.axis_index("row") * share_rows, share_rows, 1)
    scaled = complex_rows(local_dinv[0], local_dinv[1], share, width // 2).astype(jnp.bfloat16)
    product = jnp.einsum(
        "kij,ib->kjb",
        factor,
        lax.all_gather(scaled, "row", axis=0, tiled=True),
        preferred_element_type=jnp.float32,
    )
    back = combine_stack(product)
    return lax.psum_scatter(
        back.astype(jnp.bfloat16), "col", scatter_dimension=0, tiled=True
    ).astype(jnp.float32)


def local(forcing, inverse_factor, diag_inverse, coupling):
    sections = lax.axis_size("sec")
    section_id = lax.axis_index("sec")
    local_rhs = forcing[0]
    factor = inverse_factor[0]
    dinv = diag_inverse[0]
    couple = coupling[0]
    rows_here = local_rhs.shape[0]
    half = local_rhs.shape[1] // 2
    block_count = 1
    block_width = half // block_count
    rhs_blocks = local_rhs.reshape(rows_here, 2, block_count, block_width)
    results = jnp.zeros((rows_here, 2, block_count, block_width), jnp.float32)
    outgoing = jnp.zeros((rows_here, 2 * block_width), jnp.float32)
    for step_index in range(block_count + sections - 1):
        if step_index > 0:
            incoming = shifted(outgoing.astype(jnp.bfloat16), "sec", 1).astype(outgoing.dtype)
        else:
            incoming = jnp.zeros((rows_here, 2 * block_width), jnp.float32)
        block_index = step_index - section_id
        active = jnp.logical_and(block_index >= 0, block_index < block_count)
        safe_index = jnp.clip(block_index, 0, block_count - 1)
        current = lax.dynamic_index_in_dim(rhs_blocks, safe_index, 2, keepdims=False)
        current = current.reshape(rows_here, 2 * block_width)
        source = (current - complex_rows(couple[0], couple[1], incoming, block_width)).astype(
            jnp.bfloat16
        )
        field = solve_section(source, factor, dinv)
        updated = lax.dynamic_update_index_in_dim(
            results, field.reshape(rows_here, 2, block_width), safe_index, 2
        )
        results = jnp.where(active, updated, results)
        outgoing = field
    return results.reshape(1, rows_here, 2 * half)


MESH = pl.DeviceIdType.MESH

CHUNKS = 8
SUBS = 2
HALF = CHUNKS // 2
PARTS = 4
PLANS = {
    (1, 0): (
        0o40, 0o41, 0o42, 0o43, 0o04, 0o05, 0o06, 0o07, 0o00, 0o01, 0o02, 0o03, 0o30, 0o31, 0o34,
        0o32, 0o35, 0o36, 0o37, 0o33,
    ),
    (1, 1): (
        0o40, 0o41, 0o42, 0o43, 0o04, 0o05, 0o00, 0o20, 0o01, 0o14, 0o21, 0o15, 0o06, 0o24, 0o16,
        0o07, 0o17, 0o02, 0o22, 0o25, 0o10, 0o26, 0o11, 0o03, 0o27, 0o12, 0o34, 0o23, 0o13, 0o35,
        0o30, 0o36, 0o31, 0o37, 0o32, 0o33,
    ),
    (1, 2): (
        0o40, 0o41, 0o42, 0o43, 0o00, 0o04, 0o01, 0o05, 0o24, 0o02, 0o25, 0o06, 0o26, 0o07, 0o27,
        0o03, 0o14, 0o15, 0o34, 0o16, 0o35, 0o17, 0o36, 0o37, 0o30, 0o31, 0o32, 0o33,
    ),
    (1, 3): (
        0o40, 0o41, 0o42, 0o43, 0o04, 0o05, 0o06, 0o07, 0o34, 0o35, 0o36, 0o37,
    ),
    (0, 0): (
        0o40, 0o00, 0o41, 0o01, 0o42, 0o02, 0o43, 0o04, 0o05, 0o06, 0o07, 0o03, 0o34, 0o35, 0o36,
        0o37, 0o30, 0o31, 0o32, 0o33,
    ),
    (0, 1): (
        0o40, 0o04, 0o41, 0o05, 0o42, 0o06, 0o43, 0o07, 0o34, 0o35, 0o36, 0o37,
    ),
}
PER_WORD = 5


def plan_words(codes):
    words = []
    for i in range(0, len(codes), PER_WORD):
        words.append(sum(code * 64**j for j, code in enumerate(codes[i : i + PER_WORD])))
    return len(codes), words


def sweep_kernel(
    n_sec, n_row, n_col, forcing, dinv, coupling, factor_hbm, out,
    factor, src_a, src_b, own, pre_in, suf_in, pre_out, suf_out,
    lhs, back, y_out, y_in, prev_out, prev_in, forcing_t, coupling_all,
    load_sem, src_send, src_recv, pre_send, pre_recv, suf_send, suf_recv,
    y_send, y_recv, prev_send, prev_recv,
    rhs_send, rhs_recv, coef_send, coef_recv,
):
    chunk = own.shape[1]
    half = own.shape[2] // 2
    share = forcing_t.shape[2]
    part = back.shape[2]
    s, r, c = lax.axis_index("sec"), lax.axis_index("row"), lax.axis_index("col")
    other = 1 - c
    ends = s == n_sec - 1
    active = r <= 2 * c + 1
    paired = r < 2
    needed = jnp.logical_or(paired, c == 0)

    def last(k):
        return 2 * c + k // HALF

    def chunk_rows(k):
        return pl.ds(pl.multiple_of(k * chunk, chunk), chunk)

    def load(k):
        rows = chunk_rows(k)
        return pltpu.make_async_copy(
            factor_hbm.at[0, :, rows, :], factor.at[:, rows, :], load_sem.at[k]
        )

    def half_rows(col):
        return pl.ds(pl.multiple_of(col * share, share), share)

    def remote(src, dst, send_sem, recv_sem, device):
        return pltpu.make_async_remote_copy(
            src_ref=src, dst_ref=dst, send_sem=send_sem, recv_sem=recv_sem,
            device_id=device, device_id_type=MESH,
        )

    here = (s, r, c)
    across = (s, r, other)
    after = (lax.rem(s + 1, n_sec), r, c)

    def part_rows(j):
        return pl.ds(pl.multiple_of(j * part, part), part)

    def send_source(j):
        rows = part_rows(j)
        at = lax.rem(j, 2)
        return remote(src_a.at[rows], src_a.at[rows], src_send.at[at], src_recv.at[at], across)

    def send_rhs():
        return remote(forcing_t.at[c], forcing_t.at[c], rhs_send, rhs_recv, across)

    def send_coef():
        return remote(coupling_all.at[c], coupling_all.at[c], coef_send, coef_recv, across)

    def send_pre(k, h):
        rows = pl.ds(h * (chunk // SUBS), chunk // SUBS)
        at = k * SUBS + h
        return remote(
            pre_out.at[k, rows], pre_in.at[k, rows], pre_send.at[at], pre_recv.at[at],
            (s, lax.rem(r + 1, n_row), c),
        )

    def send_suf(k, h):
        rows = pl.ds(h * (chunk // SUBS), chunk // SUBS)
        at = k * SUBS + h
        return remote(
            suf_out.at[k, rows], suf_in.at[k, rows], suf_send.at[at], suf_recv.at[at],
            (s, lax.rem(r + n_row - 1, n_row), c),
        )

    def send_y(j):
        return remote(y_out.at[j], y_in.at[j], y_send.at[j], y_recv.at[j], across)

    def send_prev(j):
        return remote(prev_out.at[j], prev_in.at[j], prev_send.at[j], prev_recv.at[j], after)

    count = jnp.int32(0)
    words = [jnp.int32(0)] * max(len(plan_words(plan)[1]) for plan in PLANS.values())
    for (col, row), plan in PLANS.items():
        mine = jnp.logical_and(c == col, r == row)
        length, packed = plan_words(plan)
        count = jnp.where(mine, length, count)
        for i, word in enumerate(packed):
            words[i] = jnp.where(mine, word, words[i])

    for i in range(CHUNKS):
        k = (i + HALF) % CHUNKS

        @pl.when(r <= last(k))
        def _(k=k):
            load(k).start()

    barrier = pltpu.get_barrier_semaphore()
    for device in (
        (s, lax.rem(r + 1, n_row), c), (s, lax.rem(r + n_row - 1, n_row), c), across,
        after, (lax.rem(s + n_sec - 1, n_sec), r, c),
    ):
        pl.semaphore_signal(barrier, 1, device_id=device, device_id_type=MESH)

    def turned(value):
        return jnp.concatenate([-value[:, half:], value[:, :half]], axis=1)

    @pl.when(s == 0)
    def _():
        src_a[half_rows(c), :] = forcing[0].astype(jnp.bfloat16)

    @pl.when(s > 0)
    def _():
        forcing_t[c] = forcing[0].T
        coupling_all[c] = coupling[0]

    def product(k, cols):
        rows = chunk_rows(k)
        total = jnp.dot(factor[0, rows, cols], src_a[cols, :], preferred_element_type=jnp.float32)
        return total + jnp.dot(
            factor[1, rows, cols], src_b[cols, :], preferred_element_type=jnp.float32
        )

    pl.semaphore_wait(barrier, 5)

    @pl.when(s == 0)
    def _():
        @pl.when(needed)
        def _():
            for i in range(2):
                send_source(2 * c + i).start()

        src_b[half_rows(c), :] = turned(src_a[half_rows(c), :].astype(jnp.float32)).astype(
            jnp.bfloat16
        )
        back[...] = jnp.zeros_like(back)

        @pl.loop(0, CHUNKS)
        def _(i):
            k = lax.rem(i + HALF, CHUNKS)

            @pl.when(r < last(k))
            def _():
                load(k).wait()
                own[k] = product(k, half_rows(c))

    @pl.when(s > 0)
    def _():
        send_rhs().start()
        send_coef().start()
        back[...] = jnp.zeros_like(back)
        send_rhs().wait_recv()
        send_coef().wait_recv()

    def source_step(j):
        rows = part_rows(j)

        @pl.when(jnp.logical_and(s == 0, j // 2 != c))
        def _():
            send_source(j).wait_recv()
            src_b[rows, :] = turned(src_a[rows, :].astype(jnp.float32)).astype(jnp.bfloat16)

        @pl.when(s > 0)
        def _():
            send_prev(j).wait_recv()
            col, cols = j // 2, part_rows(lax.rem(j, 2))
            previous = prev_in[j].astype(jnp.float32)
            p_re, p_im = previous[:half], previous[half:]
            c_re, c_im = coupling_all[col, 0:1, cols], coupling_all[col, 1:2, cols]
            new_re = forcing_t[col, :half, cols] - (c_re * p_re - c_im * p_im)
            new_im = forcing_t[col, half:, cols] - (c_re * p_im + c_im * p_re)
            src_a[rows, :] = jnp.concatenate([new_re, new_im], axis=0).T.astype(jnp.bfloat16)
            src_b[rows, :] = jnp.concatenate([-new_im, new_re], axis=0).T.astype(jnp.bfloat16)

    def reach(k):
        return jnp.where(r == last(k), lax.rem(k, HALF), PARTS - 1)

    def forward_step(k):
        begun = jnp.logical_and(s == 0, r < last(k))

        def keep(total):
            own[k] = total
            pre_out[k] = total.astype(jnp.bfloat16)
            suf_out[k] = total.astype(jnp.bfloat16)

        @pl.when(begun)
        def _():
            keep(own[k] + product(k, half_rows(other)))

        for m in range(PARTS):
            @pl.when(jnp.logical_and(reach(k) == m, jnp.logical_not(begun)))
            def _(m=m):
                load(k).wait()
                keep(product(k, slice(0, (m + 1) * part)))

        @pl.when(jnp.logical_and(r == 0, last(k) > 0))
        def _():
            for h in range(SUBS):
                send_pre(k, h).start()

        @pl.when(jnp.logical_and(r > 0, r == last(k)))
        def _():
            for h in range(SUBS):
                send_suf(k, h).start()

    def relay(send, held, came, k):
        for h in range(SUBS):
            rows = slice(h * (chunk // SUBS), (h + 1) * (chunk // SUBS))
            send(k, h).wait_recv()
            held[k, rows, :] += came[k, rows, :]
            send(k, h).start()

    def relay_right(k):
        relay(send_pre, pre_out, pre_in, k)

    def relay_left(k):
        relay(send_suf, suf_out, suf_in, k)

    def back_step(k):
        rows = chunk_rows(k)
        left, right = r > 0, r < last(k)

        @pl.when(jnp.logical_and(left, jnp.logical_not(right)))
        def _():
            for h in range(SUBS):
                send_pre(k, h).wait_recv()

        @pl.when(jnp.logical_and(right, jnp.logical_not(left)))
        def _():
            for h in range(SUBS):
                send_suf(k, h).wait_recv()

        for with_left in (False, True):
            for with_right in (False, True):
                @pl.when(jnp.logical_and(left == with_left, right == with_right))
                def _(with_left=with_left, with_right=with_right):
                    total = own[k]
                    if with_left:
                        total += pre_in[k].astype(jnp.float32)
                    if with_right:
                        total += suf_in[k].astype(jnp.float32)
                    forward = total.T
                    d_re, d_im = dinv[0, 0:1, rows], dinv[0, 1:2, rows]
                    f_re, f_im = forward[:half], forward[half:]
                    s_re, s_im = d_re * f_re - d_im * f_im, d_re * f_im + d_im * f_re
                    lhs[0] = jnp.concatenate([s_re, s_im], axis=0).astype(jnp.bfloat16)
                    lhs[1] = jnp.concatenate([-s_im, s_re], axis=0).astype(jnp.bfloat16)

        for m in range(PARTS):
            @pl.when(reach(k) == m)
            def _(m=m):
                cols = slice(0, (m + 1) * part)
                total = jnp.dot(lhs[0], factor[0, rows, cols], preferred_element_type=jnp.float32)
                total += jnp.dot(lhs[1], factor[1, rows, cols], preferred_element_type=jnp.float32)
                for j in range(m + 1):
                    back[j] += total[:, j * part : (j + 1) * part]

    @pl.loop(0, count)
    def _(e):
        at = e // PER_WORD
        word = words[0]
        for i in range(1, len(words)):
            word = jnp.where(at == i, words[i], word)
        code = lax.rem(lax.shift_right_logical(word, 6 * lax.rem(e, PER_WORD)), 64)
        k = lax.rem(code, CHUNKS)
        step = code // CHUNKS
        for i, action in enumerate((forward_step, relay_right, relay_left, back_step, source_step)):
            @pl.when(step == i)
            def _(action=action):
                action(k)

    def order(first, i):
        return (2 * first + i) % PARTS if isinstance(first, int) else lax.rem(2 * first + i, PARTS)

    def sends_y(i):
        wanted = jnp.logical_or(paired, c == 1) if i < 2 else paired
        return wanted if i < 2 else jnp.logical_and(wanted, jnp.logical_not(ends))

    def takes_y(i):
        wanted = jnp.logical_or(paired, c == 0) if i < 2 else paired
        return wanted if i < 2 else jnp.logical_and(wanted, jnp.logical_not(ends))

    for i in range(PARTS):
        j = order(other, i)

        @pl.when(sends_y(i))
        def _(j=j):
            y_out[j] = back[j].astype(jnp.bfloat16)
            send_y(j).start()

    passes = jnp.logical_and(active, jnp.logical_not(ends))
    for i in range(PARTS):
        j = order(c, i)

        @pl.when(takes_y(i))
        def _(j=j):
            send_y(j).wait_recv()
            back[j] += y_in[j].astype(jnp.float32)

        @pl.when(passes)
        def _(j=j):
            prev_out[j] = back[j].astype(jnp.bfloat16)
            send_prev(j).start()

    for i in range(2):
        out[0, i * part : (i + 1) * part, :] = back[order(c, i)].T

    @pl.when(s == 0)
    def _():
        @pl.when(needed)
        def _():
            for i in range(2):
                send_source(2 * c + i).wait_send()

    @pl.when(s > 0)
    def _():
        send_rhs().wait_send()
        send_coef().wait_send()

    for k in range(CHUNKS):
        @pl.when(r < last(k))
        def _(k=k):
            for h in range(SUBS):
                send_pre(k, h).wait_send()

        @pl.when(jnp.logical_and(r > 0, r <= last(k)))
        def _(k=k):
            for h in range(SUBS):
                send_suf(k, h).wait_send()

    for i in range(PARTS):
        @pl.when(sends_y(i))
        def _(i=i):
            send_y(order(other, i)).wait_send()

        @pl.when(passes)
        def _(i=i):
            send_prev(i).wait_send()


def sweep(n_sec, n_row, n_col, forcing, inverse_factor, diag_inverse, coupling):
    share, width = forcing.shape[1:]
    block_rows, block_cols = inverse_factor.shape[2:]
    chunk, part = block_rows // CHUNKS, block_cols // PARTS
    vmem = pl.BlockSpec(memory_space=pltpu.VMEM)
    bf16, f32 = jnp.bfloat16, jnp.float32
    dma = pltpu.SemaphoreType.DMA
    return pl.pallas_call(
        functools.partial(sweep_kernel, n_sec, n_row, n_col),
        out_shape=jax.ShapeDtypeStruct(forcing.shape, f32),
        in_specs=[vmem, vmem, vmem, pl.BlockSpec(memory_space=pl.ANY)],
        out_specs=vmem,
        scratch_shapes=[
            pltpu.VMEM((2, block_rows, block_cols), bf16),
            pltpu.VMEM((block_cols, width), bf16),
            pltpu.VMEM((block_cols, width), bf16),
            pltpu.VMEM((CHUNKS, chunk, width), f32),
            pltpu.VMEM((CHUNKS, chunk, width), bf16),
            pltpu.VMEM((CHUNKS, chunk, width), bf16),
            pltpu.VMEM((CHUNKS, chunk, width), bf16),
            pltpu.VMEM((CHUNKS, chunk, width), bf16),
            pltpu.VMEM((2, width, chunk), bf16),
            pltpu.VMEM((PARTS, width, part), f32),
            pltpu.VMEM((PARTS, width, part), bf16),
            pltpu.VMEM((PARTS, width, part), bf16),
            pltpu.VMEM((PARTS, width, part), bf16),
            pltpu.VMEM((PARTS, width, part), bf16),
            pltpu.VMEM((n_col, width, share), f32),
            pltpu.VMEM((n_col, 2, share), f32),
            dma((CHUNKS,)),
            dma((2,)), dma((2,)),
            dma((CHUNKS * SUBS,)), dma((CHUNKS * SUBS,)),
            dma((CHUNKS * SUBS,)), dma((CHUNKS * SUBS,)),
            dma((PARTS,)), dma((PARTS,)),
            dma((PARTS,)), dma((PARTS,)),
            dma, dma, dma, dma,
        ],
        compiler_params=pltpu.CompilerParams(
            collective_id=0, has_side_effects=True, vmem_limit_bytes=56 * 2**20
        ),
    )(forcing, diag_inverse, coupling, inverse_factor)


def solution(mesh):
    placed = (
        P("sec", ("row", "col"), None),
        P("sec", None, "col", "row"),
        P("sec", None, "col"),
        P("sec", None, ("row", "col")),
    )
    n_sec, n_row, n_col = (mesh.shape[axis] for axis in ("sec", "row", "col"))

    def body(forcing, inverse_factor, diag_inverse, coupling):
        share, width = forcing.shape[1:]
        fits = inverse_factor.size * 2 <= 32 * 2**20
        block = inverse_factor.shape[2] == 4 * share and inverse_factor.shape[3] == 2 * share
        if share % 256 or width % 128 or not fits or n_sec < 3 or (n_row, n_col) != (4, 2) or not block:
            return local(forcing, inverse_factor, diag_inverse, coupling)
        return sweep(n_sec, n_row, n_col, forcing, inverse_factor, diag_inverse, coupling)

    return jax.shard_map(
        body, mesh=mesh, in_specs=placed, out_specs=P("sec", ("row", "col"), None), check_vma=False
    )
```

```python
import functools

import jax
import jax.numpy as jnp
from jax import lax
from jax.experimental import pallas as pl
from jax.experimental.pallas import tpu as pltpu
from jax.sharding import PartitionSpec as P


def shifted(value, axis, steps):
    count = lax.axis_size(axis)
    initial, last = (max(0, -steps), min(count, count - steps))
    return lax.ppermute(value, axis, [(source, source + steps) for source in range(initial, last)])


def complex_rows(coef_re, coef_im, values, half):
    v_re = values[:, :half]
    v_im = values[:, half:]
    out_re = coef_re[:, None] * v_re - coef_im[:, None] * v_im
    out_im = coef_re[:, None] * v_im + coef_im[:, None] * v_re
    return jnp.concatenate([out_re, out_im], axis=1)


def combine_stack(product):
    half = product.shape[2] // 2
    out_re = product[0, :, :half] - product[1, :, half:]
    out_im = product[0, :, half:] + product[1, :, :half]
    return jnp.concatenate([out_re, out_im], axis=1)


def solve_section(source, factor, dinv):
    width = source.shape[1]
    product = jnp.einsum(
        "kij,jb->kib",
        factor,
        lax.all_gather(source, "col", axis=0, tiled=True),
        preferred_element_type=jnp.float32,
    )
    forward = combine_stack(product)
    share = lax.psum_scatter(
        forward.astype(jnp.bfloat16), "row", scatter_dimension=0, tiled=True
    ).astype(jnp.float32)
    share_rows = share.shape[0]
    local_dinv = lax.dynamic_slice_in_dim(dinv, lax.axis_index("row") * share_rows, share_rows, 1)
    scaled = complex_rows(local_dinv[0], local_dinv[1], share, width // 2).astype(jnp.bfloat16)
    product = jnp.einsum(
        "kij,ib->kjb",
        factor,
        lax.all_gather(scaled, "row", axis=0, tiled=True),
        preferred_element_type=jnp.float32,
    )
    back = combine_stack(product)
    return lax.psum_scatter(
        back.astype(jnp.bfloat16), "col", scatter_dimension=0, tiled=True
    ).astype(jnp.float32)


def local(forcing, inverse_factor, diag_inverse, coupling):
    sections = lax.axis_size("sec")
    section_id = lax.axis_index("sec")
    local_rhs = forcing[0]
    factor = inverse_factor[0]
    dinv = diag_inverse[0]
    couple = coupling[0]
    rows_here = local_rhs.shape[0]
    half = local_rhs.shape[1] // 2
    block_count = 1
    block_width = half // block_count
    rhs_blocks = local_rhs.reshape(rows_here, 2, block_count, block_width)
    results = jnp.zeros((rows_here, 2, block_count, block_width), jnp.float32)
    outgoing = jnp.zeros((rows_here, 2 * block_width), jnp.float32)
    for step_index in range(block_count + sections - 1):
        if step_index > 0:
            incoming = shifted(outgoing.astype(jnp.bfloat16), "sec", 1).astype(outgoing.dtype)
        else:
            incoming = jnp.zeros((rows_here, 2 * block_width), jnp.float32)
        block_index = step_index - section_id
        active = jnp.logical_and(block_index >= 0, block_index < block_count)
        safe_index = jnp.clip(block_index, 0, block_count - 1)
        current = lax.dynamic_index_in_dim(rhs_blocks, safe_index, 2, keepdims=False)
        current = current.reshape(rows_here, 2 * block_width)
        source = (current - complex_rows(couple[0], couple[1], incoming, block_width)).astype(
            jnp.bfloat16
        )
        field = solve_section(source, factor, dinv)
        updated = lax.dynamic_update_index_in_dim(
            results, field.reshape(rows_here, 2, block_width), safe_index, 2
        )
        results = jnp.where(active, updated, results)
        outgoing = field
    return results.reshape(1, rows_here, 2 * half)


MESH = pl.DeviceIdType.MESH

CHUNKS = 8
SUBS = 2
HALF = CHUNKS // 2
PARTS = 4
EARLY = 4
PLANS = {
    (1, 0): (
        0o40, 0o41, 0o42, 0o43, 0o04, 0o05, 0o06, 0o07, 0o00, 0o01, 0o02, 0o03, 0o30, 0o31, 0o34,
        0o32, 0o35, 0o36, 0o37, 0o33,
    ),
    (1, 1): (
        0o40, 0o41, 0o42, 0o43, 0o04, 0o05, 0o00, 0o20, 0o01, 0o14, 0o21, 0o15, 0o06, 0o24, 0o16,
        0o07, 0o17, 0o02, 0o22, 0o25, 0o10, 0o26, 0o11, 0o03, 0o27, 0o12, 0o34, 0o23, 0o13, 0o35,
        0o30, 0o36, 0o31, 0o37, 0o32, 0o33,
    ),
    (1, 2): (
        0o40, 0o41, 0o42, 0o43, 0o00, 0o04, 0o01, 0o05, 0o24, 0o02, 0o25, 0o06, 0o26, 0o07, 0o27,
        0o03, 0o14, 0o15, 0o34, 0o16, 0o35, 0o17, 0o36, 0o37, 0o30, 0o31, 0o32, 0o33,
    ),
    (1, 3): (
        0o40, 0o41, 0o42, 0o43, 0o04, 0o05, 0o06, 0o07, 0o34, 0o35, 0o36, 0o37,
    ),
    (0, 0): (
        0o40, 0o00, 0o41, 0o01, 0o42, 0o02, 0o43, 0o04, 0o05, 0o06, 0o07, 0o03, 0o34, 0o35, 0o36,
        0o37, 0o30, 0o31, 0o32, 0o33,
    ),
    (0, 1): (
        0o40, 0o04, 0o41, 0o05, 0o42, 0o06, 0o43, 0o07, 0o34, 0o35, 0o36, 0o37,
    ),
}
PER_WORD = 3
ACTIONS = [("F", m) for m in range(PARTS + 1)] + [("R",), ("L",), ("S",)] + [("B", True, True), ("B", False, True)]
ACTIONS += [("B", left, False, m) for left in (True, False) for m in range(PARTS)]


def plan_words(col, row, plan):
    codes = []
    for step in plan:
        kind, k = "FRLBS"[step // CHUNKS], step % CHUNKS
        end = 2 * col + k // HALF
        if kind == "F":
            action = ("F", k % HALF if row == end else PARTS)
        elif kind == "B":
            action = ("B", row > 0, row < end)
            action += () if row < end else (k % HALF,)
        else:
            action = (kind,)
        codes.append(ACTIONS.index(action) * CHUNKS + k)
    words = []
    for i in range(0, len(codes), PER_WORD):
        words.append(sum(code * 256**j for j, code in enumerate(codes[i : i + PER_WORD])))
    return len(codes), words


def sweep_kernel(
    n_sec, n_row, n_col, forcing, dinv, coupling, factor_hbm, out,
    factor, src_a, src_b, own, pre_in, suf_in, pre_out, suf_out,
    back, y_out, y_in, prev_out, prev_in, forcing_t, coupling_all,
    load_sem, src_send, src_recv, pre_send, pre_recv, suf_send, suf_recv,
    y_send, y_recv, prev_send, prev_recv,
    rhs_send, rhs_recv, coef_send, coef_recv, go,
):
    chunk = own.shape[1]
    half = own.shape[2] // 2
    share = forcing_t.shape[2]
    part = back.shape[2]
    s, r, c = lax.axis_index("sec"), lax.axis_index("row"), lax.axis_index("col")
    other = 1 - c
    ends = s == n_sec - 1
    active = r <= 2 * c + 1
    paired = r < 2
    needed = jnp.logical_or(paired, c == 0)

    def last(k):
        return 2 * c + k // HALF

    def chunk_rows(k):
        return pl.ds(pl.multiple_of(k * chunk, chunk), chunk)

    def load(k):
        rows = chunk_rows(k)
        return pltpu.make_async_copy(
            factor_hbm.at[0, :, rows, :], factor.at[:, rows, :], load_sem.at[k]
        )

    def half_rows(col):
        return pl.ds(pl.multiple_of(col * share, share), share)

    def remote(src, dst, send_sem, recv_sem, device):
        return pltpu.make_async_remote_copy(
            src_ref=src, dst_ref=dst, send_sem=send_sem, recv_sem=recv_sem,
            device_id=device, device_id_type=MESH,
        )

    across = (s, r, other)
    after = (lax.rem(s + 1, n_sec), r, c)

    def part_rows(j):
        return pl.ds(pl.multiple_of(j * part, part), part)

    def send_source(j):
        rows = part_rows(j)
        at = lax.rem(j, 2)
        return remote(src_a.at[rows], src_a.at[rows], src_send.at[at], src_recv.at[at], across)

    def send_rhs():
        return remote(forcing_t.at[c], forcing_t.at[c], rhs_send, rhs_recv, across)

    def send_coef():
        return remote(coupling_all.at[c], coupling_all.at[c], coef_send, coef_recv, across)

    def send_pre(k, h):
        rows = pl.ds(h * (chunk // SUBS), chunk // SUBS)
        at = k * SUBS + h
        return remote(
            pre_out.at[k, rows], pre_in.at[k, rows], pre_send.at[at], pre_recv.at[at],
            (s, lax.rem(r + 1, n_row), c),
        )

    def send_suf(k, h):
        rows = pl.ds(h * (chunk // SUBS), chunk // SUBS)
        at = k * SUBS + h
        return remote(
            suf_out.at[k, rows], suf_in.at[k, rows], suf_send.at[at], suf_recv.at[at],
            (s, lax.rem(r + n_row - 1, n_row), c),
        )

    def send_y(j):
        return remote(y_out.at[j], y_in.at[j], y_send.at[j], y_recv.at[j], across)

    def send_prev(j):
        return remote(prev_out.at[j], prev_in.at[j], prev_send.at[j], prev_recv.at[j], after)

    count = jnp.int32(0)
    packed = {place: plan_words(*place, plan) for place, plan in PLANS.items()}
    words = [jnp.int32(0)] * max(len(held) for _, held in packed.values())
    for (col, row), (length, held) in packed.items():
        mine = jnp.logical_and(c == col, r == row)
        count = jnp.where(mine, length, count)
        for i, word in enumerate(held):
            words[i] = jnp.where(mine, word, words[i])

    for i in range(CHUNKS):
        k = (i + HALF) % CHUNKS

        @pl.when(r <= last(k))
        def _(k=k):
            load(k).start()

    barrier = pltpu.get_barrier_semaphore()
    for device in (
        (s, lax.rem(r + 1, n_row), c), (s, lax.rem(r + n_row - 1, n_row), c), across,
        after, (lax.rem(s + n_sec - 1, n_sec), r, c),
    ):
        pl.semaphore_signal(barrier, 1, device_id=device, device_id_type=MESH)

    def turned(value):
        return jnp.concatenate([-value[:, half:], value[:, :half]], axis=1)

    def product(k, cols):
        rows = chunk_rows(k)
        total = jnp.dot(factor[0, rows, cols], src_a[cols, :], preferred_element_type=jnp.float32)
        return total + jnp.dot(
            factor[1, rows, cols], src_b[cols, :], preferred_element_type=jnp.float32
        )

    def begin(first, stop):
        @pl.loop(first, stop)
        def _(i):
            k = lax.rem(i + HALF, CHUNKS)

            @pl.when(r < last(k))
            def _():
                load(k).wait()
                own[k] = product(k, half_rows(c))

    back[...] = jnp.zeros_like(back)

    @pl.when(s == 0)
    def _():
        src_a[half_rows(c), :] = forcing[0].astype(jnp.bfloat16)
        src_b[half_rows(c), :] = turned(forcing[0].astype(jnp.bfloat16).astype(jnp.float32)).astype(
            jnp.bfloat16
        )
        begin(0, EARLY)

    @pl.when(s > 0)
    def _():
        forcing_t[c] = forcing[0].T
        coupling_all[c] = coupling[0]

    pl.semaphore_wait(barrier, 5)

    @pl.when(s == 0)
    def _():
        @pl.when(needed)
        def _():
            for i in range(2):
                send_source(2 * c + i).start()

        begin(EARLY, CHUNKS)
        pl.semaphore_signal(go, 1, device_id=after, device_id_type=MESH)

    @pl.when(s == 1)
    def _():
        pl.semaphore_wait(go, 1)

    @pl.when(s > 0)
    def _():
        send_rhs().start()
        send_coef().start()
        send_rhs().wait_recv()
        send_coef().wait_recv()

    def source_step(j):
        rows = part_rows(j)

        @pl.when(jnp.logical_and(s == 0, j // 2 != c))
        def _():
            send_source(j).wait_recv()
            src_b[rows, :] = turned(src_a[rows, :].astype(jnp.float32)).astype(jnp.bfloat16)

        @pl.when(s > 0)
        def _():
            send_prev(j).wait_recv()
            col, cols = j // 2, part_rows(lax.rem(j, 2))
            previous = prev_in[j].astype(jnp.float32)
            p_re, p_im = previous[:half], previous[half:]
            c_re, c_im = coupling_all[col, 0:1, cols], coupling_all[col, 1:2, cols]
            new_re = forcing_t[col, :half, cols] - (c_re * p_re - c_im * p_im)
            new_im = forcing_t[col, half:, cols] - (c_re * p_im + c_im * p_re)
            src_a[rows, :] = jnp.concatenate([new_re, new_im], axis=0).T.astype(jnp.bfloat16)
            src_b[rows, :] = jnp.concatenate([-new_im, new_re], axis=0).T.astype(jnp.bfloat16)

    def keep(k, total):
        own[k] = total
        pre_out[k] = total.astype(jnp.bfloat16)
        suf_out[k] = total.astype(jnp.bfloat16)

    def forward_full(k):
        @pl.when(s == 0)
        def _():
            keep(k, own[k] + product(k, half_rows(other)))

        @pl.when(s > 0)
        def _():
            load(k).wait()
            keep(k, product(k, slice(0, PARTS * part)))

        @pl.when(r == 0)
        def _():
            for h in range(SUBS):
                send_pre(k, h).start()

    def forward_diagonal(m, k):
        load(k).wait()
        keep(k, product(k, slice(0, (m + 1) * part)))

        @pl.when(r > 0)
        def _():
            for h in range(SUBS):
                send_suf(k, h).start()

    def relay(send, held, came, k):
        for h in range(SUBS):
            rows = slice(h * (chunk // SUBS), (h + 1) * (chunk // SUBS))
            send(k, h).wait_recv()
            held[k, rows, :] += came[k, rows, :]
            send(k, h).start()

    def relay_right(k):
        relay(send_pre, pre_out, pre_in, k)

    def relay_left(k):
        relay(send_suf, suf_out, suf_in, k)

    def back_step(left, right, m, k):
        rows = chunk_rows(k)
        total = own[k]
        if left != right:
            for h in range(SUBS):
                (send_pre if left else send_suf)(k, h).wait_recv()
        if left:
            total += pre_in[k].astype(jnp.float32)
        if right:
            total += suf_in[k].astype(jnp.float32)
        forward = total.T
        d_re, d_im = dinv[0, 0:1, rows], dinv[0, 1:2, rows]
        f_re, f_im = forward[:half], forward[half:]
        s_re, s_im = d_re * f_re - d_im * f_im, d_re * f_im + d_im * f_re
        lhs_a = jnp.concatenate([s_re, s_im], axis=0).astype(jnp.bfloat16)
        lhs_b = jnp.concatenate([-s_im, s_re], axis=0).astype(jnp.bfloat16)
        cols = slice(0, (m + 1) * part)
        total = jnp.dot(lhs_a, factor[0, rows, cols], preferred_element_type=jnp.float32)
        total += jnp.dot(lhs_b, factor[1, rows, cols], preferred_element_type=jnp.float32)
        for j in range(m + 1):
            back[j] += total[:, j * part : (j + 1) * part]

    def act(action, k):
        kind = action[0]
        if kind == "F":
            if action[1] == PARTS:
                forward_full(k)
            else:
                forward_diagonal(action[1], k)
        elif kind == "B":
            back_step(action[1], action[2], action[3] if len(action) > 3 else PARTS - 1, k)
        else:
            {"R": relay_right, "L": relay_left, "S": source_step}[kind](k)

    def dispatch(step, first, stop, k):
        if stop - first == 1:
            act(ACTIONS[first], k)
            return
        middle = (first + stop) // 2

        @pl.when(step < middle)
        def _():
            dispatch(step, first, middle, k)

        @pl.when(step >= middle)
        def _():
            dispatch(step, middle, stop, k)

    @pl.loop(0, count)
    def _(e):
        at = e // PER_WORD
        word = words[0]
        for i in range(1, len(words)):
            word = jnp.where(at == i, words[i], word)
        code = lax.rem(lax.shift_right_logical(word, 8 * lax.rem(e, PER_WORD)), 256)
        dispatch(code // CHUNKS, 0, len(ACTIONS), lax.rem(code, CHUNKS))

    def order(first, i):
        return (2 * first + i) % PARTS if isinstance(first, int) else lax.rem(2 * first + i, PARTS)

    def sends_y(i):
        wanted = jnp.logical_or(paired, c == 1) if i < 2 else paired
        return wanted if i < 2 else jnp.logical_and(wanted, jnp.logical_not(ends))

    def takes_y(i):
        wanted = jnp.logical_or(paired, c == 0) if i < 2 else paired
        return wanted if i < 2 else jnp.logical_and(wanted, jnp.logical_not(ends))

    for i in range(PARTS):
        j = order(other, i)

        @pl.when(sends_y(i))
        def _(j=j):
            y_out[j] = back[j].astype(jnp.bfloat16)
            send_y(j).start()

    passes = jnp.logical_and(active, jnp.logical_not(ends))
    for i in range(PARTS):
        j = order(c, i)

        @pl.when(takes_y(i))
        def _(j=j):
            send_y(j).wait_recv()
            back[j] += y_in[j].astype(jnp.float32)

        @pl.when(passes)
        def _(j=j):
            prev_out[j] = back[j].astype(jnp.bfloat16)
            send_prev(j).start()

    for i in range(2):
        out[0, i * part : (i + 1) * part, :] = back[order(c, i)].T

    @pl.when(s == 0)
    def _():
        @pl.when(needed)
        def _():
            for i in range(2):
                send_source(2 * c + i).wait_send()

    @pl.when(s > 0)
    def _():
        send_rhs().wait_send()
        send_coef().wait_send()

    for k in range(CHUNKS):
        @pl.when(r < last(k))
        def _(k=k):
            for h in range(SUBS):
                send_pre(k, h).wait_send()

        @pl.when(jnp.logical_and(r > 0, r <= last(k)))
        def _(k=k):
            for h in range(SUBS):
                send_suf(k, h).wait_send()

    for i in range(PARTS):
        @pl.when(sends_y(i))
        def _(i=i):
            send_y(order(other, i)).wait_send()

        @pl.when(passes)
        def _(i=i):
            send_prev(i).wait_send()


def sweep(n_sec, n_row, n_col, forcing, inverse_factor, diag_inverse, coupling):
    share, width = forcing.shape[1:]
    block_rows, block_cols = inverse_factor.shape[2:]
    chunk, part = block_rows // CHUNKS, block_cols // PARTS
    vmem = pl.BlockSpec(memory_space=pltpu.VMEM)
    bf16, f32 = jnp.bfloat16, jnp.float32
    dma = pltpu.SemaphoreType.DMA
    return pl.pallas_call(
        functools.partial(sweep_kernel, n_sec, n_row, n_col),
        out_shape=jax.ShapeDtypeStruct(forcing.shape, f32),
        in_specs=[vmem, vmem, vmem, pl.BlockSpec(memory_space=pl.ANY)],
        out_specs=vmem,
        scratch_shapes=[
            pltpu.VMEM((2, block_rows, block_cols), bf16),
            pltpu.VMEM((block_cols, width), bf16),
            pltpu.VMEM((block_cols, width), bf16),
            pltpu.VMEM((CHUNKS, chunk, width), f32),
            pltpu.VMEM((CHUNKS, chunk, width), bf16),
            pltpu.VMEM((CHUNKS, chunk, width), bf16),
            pltpu.VMEM((CHUNKS, chunk, width), bf16),
            pltpu.VMEM((CHUNKS, chunk, width), bf16),
            pltpu.VMEM((PARTS, width, part), f32),
            pltpu.VMEM((PARTS, width, part), bf16),
            pltpu.VMEM((PARTS, width, part), bf16),
            pltpu.VMEM((PARTS, width, part), bf16),
            pltpu.VMEM((PARTS, width, part), bf16),
            pltpu.VMEM((n_col, width, share), f32),
            pltpu.VMEM((n_col, 2, share), f32),
            dma((CHUNKS,)),
            dma((2,)), dma((2,)),
            dma((CHUNKS * SUBS,)), dma((CHUNKS * SUBS,)),
            dma((CHUNKS * SUBS,)), dma((CHUNKS * SUBS,)),
            dma((PARTS,)), dma((PARTS,)),
            dma((PARTS,)), dma((PARTS,)),
            dma, dma, dma, dma,
            pltpu.SemaphoreType.REGULAR,
        ],
        compiler_params=pltpu.CompilerParams(
            collective_id=0, has_side_effects=True, vmem_limit_bytes=56 * 2**20
        ),
    )(forcing, diag_inverse, coupling, inverse_factor)


def solution(mesh):
    placed = (
        P("sec", ("row", "col"), None),
        P("sec", None, "col", "row"),
        P("sec", None, "col"),
        P("sec", None, ("row", "col")),
    )
    n_sec, n_row, n_col = (mesh.shape[axis] for axis in ("sec", "row", "col"))

    def body(forcing, inverse_factor, diag_inverse, coupling):
        share, width = forcing.shape[1:]
        fits = inverse_factor.size * 2 <= 32 * 2**20
        block = inverse_factor.shape[2] == 4 * share and inverse_factor.shape[3] == 2 * share
        if share % 256 or width % 128 or not fits or n_sec < 3 or (n_row, n_col) != (4, 2) or not block:
            return local(forcing, inverse_factor, diag_inverse, coupling)
        return sweep(n_sec, n_row, n_col, forcing, inverse_factor, diag_inverse, coupling)

    return jax.shard_map(
        body, mesh=mesh, in_specs=placed, out_specs=P("sec", ("row", "col"), None), check_vma=False
    )
```

```python
import functools

import jax
import jax.numpy as jnp
from jax import lax
from jax.experimental import pallas as pl
from jax.experimental.pallas import tpu as pltpu
from jax.sharding import PartitionSpec as P


def shifted(value, axis, steps):
    count = lax.axis_size(axis)
    initial, last = (max(0, -steps), min(count, count - steps))
    return lax.ppermute(value, axis, [(source, source + steps) for source in range(initial, last)])


def complex_rows(coef_re, coef_im, values, half):
    v_re = values[:, :half]
    v_im = values[:, half:]
    out_re = coef_re[:, None] * v_re - coef_im[:, None] * v_im
    out_im = coef_re[:, None] * v_im + coef_im[:, None] * v_re
    return jnp.concatenate([out_re, out_im], axis=1)


def combine_stack(product):
    half = product.shape[2] // 2
    out_re = product[0, :, :half] - product[1, :, half:]
    out_im = product[0, :, half:] + product[1, :, :half]
    return jnp.concatenate([out_re, out_im], axis=1)


def solve_section(source, factor, dinv):
    width = source.shape[1]
    product = jnp.einsum(
        "kij,jb->kib",
        factor,
        lax.all_gather(source, "col", axis=0, tiled=True),
        preferred_element_type=jnp.float32,
    )
    forward = combine_stack(product)
    share = lax.psum_scatter(
        forward.astype(jnp.bfloat16), "row", scatter_dimension=0, tiled=True
    ).astype(jnp.float32)
    share_rows = share.shape[0]
    local_dinv = lax.dynamic_slice_in_dim(dinv, lax.axis_index("row") * share_rows, share_rows, 1)
    scaled = complex_rows(local_dinv[0], local_dinv[1], share, width // 2).astype(jnp.bfloat16)
    product = jnp.einsum(
        "kij,ib->kjb",
        factor,
        lax.all_gather(scaled, "row", axis=0, tiled=True),
        preferred_element_type=jnp.float32,
    )
    back = combine_stack(product)
    return lax.psum_scatter(
        back.astype(jnp.bfloat16), "col", scatter_dimension=0, tiled=True
    ).astype(jnp.float32)


def local(forcing, inverse_factor, diag_inverse, coupling):
    sections = lax.axis_size("sec")
    section_id = lax.axis_index("sec")
    local_rhs = forcing[0]
    factor = inverse_factor[0]
    dinv = diag_inverse[0]
    couple = coupling[0]
    rows_here = local_rhs.shape[0]
    half = local_rhs.shape[1] // 2
    block_count = 1
    block_width = half // block_count
    rhs_blocks = local_rhs.reshape(rows_here, 2, block_count, block_width)
    results = jnp.zeros((rows_here, 2, block_count, block_width), jnp.float32)
    outgoing = jnp.zeros((rows_here, 2 * block_width), jnp.float32)
    for step_index in range(block_count + sections - 1):
        if step_index > 0:
            incoming = shifted(outgoing.astype(jnp.bfloat16), "sec", 1).astype(outgoing.dtype)
        else:
            incoming = jnp.zeros((rows_here, 2 * block_width), jnp.float32)
        block_index = step_index - section_id
        active = jnp.logical_and(block_index >= 0, block_index < block_count)
        safe_index = jnp.clip(block_index, 0, block_count - 1)
        current = lax.dynamic_index_in_dim(rhs_blocks, safe_index, 2, keepdims=False)
        current = current.reshape(rows_here, 2 * block_width)
        source = (current - complex_rows(couple[0], couple[1], incoming, block_width)).astype(
            jnp.bfloat16
        )
        field = solve_section(source, factor, dinv)
        updated = lax.dynamic_update_index_in_dim(
            results, field.reshape(rows_here, 2, block_width), safe_index, 2
        )
        results = jnp.where(active, updated, results)
        outgoing = field
    return results.reshape(1, rows_here, 2 * half)


MESH = pl.DeviceIdType.MESH

CHUNKS = 8
SUBS = 2
HALF = CHUNKS // 2
PARTS = 4
EARLY = 2
BEGUN = 6
PLANS = {
    (1, 0, 0): (
        0o40, 0o41, 0o42, 0o43, 0o04, 0o05, 0o06, 0o07, 0o00, 0o01, 0o02, 0o03, 0o30, 0o31, 0o34,
        0o32, 0o35, 0o36, 0o37, 0o33,
    ),
    (1, 1, 0): (
        0o40, 0o41, 0o42, 0o43, 0o04, 0o05, 0o00, 0o20, 0o01, 0o14, 0o21, 0o15, 0o06, 0o24, 0o16,
        0o07, 0o17, 0o02, 0o22, 0o25, 0o10, 0o26, 0o11, 0o03, 0o27, 0o12, 0o34, 0o23, 0o13, 0o35,
        0o30, 0o36, 0o31, 0o37, 0o32, 0o33,
    ),
    (1, 2, 0): (
        0o40, 0o41, 0o42, 0o43, 0o00, 0o04, 0o01, 0o05, 0o24, 0o02, 0o25, 0o06, 0o26, 0o07, 0o27,
        0o03, 0o14, 0o15, 0o34, 0o16, 0o35, 0o17, 0o36, 0o37, 0o30, 0o31, 0o32, 0o33,
    ),
    (1, 3, 0): (
        0o40, 0o41, 0o42, 0o43, 0o04, 0o05, 0o06, 0o07, 0o34, 0o35, 0o36, 0o37,
    ),
    (0, 0, 0): (
        0o40, 0o00, 0o41, 0o01, 0o42, 0o02, 0o43, 0o04, 0o05, 0o06, 0o07, 0o03, 0o34, 0o35, 0o36,
        0o37, 0o30, 0o31, 0o32, 0o33,
    ),
    (0, 0, 1): (
        0o40, 0o41, 0o54, 0o55, 0o42, 0o56, 0o57, 0o43, 0o64, 0o65, 0o66, 0o67, 0o34, 0o35, 0o36,
        0o37,
    ),
    (0, 1, 0): (
        0o40, 0o04, 0o41, 0o05, 0o42, 0o06, 0o43, 0o07, 0o34, 0o35, 0o36, 0o37,
    ),
}
PER_WORD = 3
ACTIONS = [("F", m) for m in range(PARTS + 1)] + [("R",), ("L",), ("S",), ("G",), ("H",)] + [("B", True, True), ("B", False, True)]
ACTIONS += [("B", left, False, m) for left in (True, False) for m in range(PARTS)]


def plan_words(col, row, plan):
    codes = []
    for step in plan:
        kind, k = "FRLBSGH"[step // CHUNKS], step % CHUNKS
        end = 2 * col + k // HALF
        if kind == "F":
            action = ("F", k % HALF if row == end else PARTS)
        elif kind == "B":
            action = ("B", row > 0, row < end)
            action += () if row < end else (k % HALF,)
        else:
            action = (kind,)
        codes.append(ACTIONS.index(action) * CHUNKS + k)
    words = []
    for i in range(0, len(codes), PER_WORD):
        words.append(sum(code * 256**j for j, code in enumerate(codes[i : i + PER_WORD])))
    return len(codes), words


def sweep_kernel(
    n_sec, n_row, n_col, forcing, dinv, coupling, factor_hbm, out,
    factor, src_a, src_b, own, pre_in, suf_in, pre_out, suf_out,
    back, y_out, y_in, prev_out, prev_in, forcing_t, coupling_all,
    load_sem, src_send, src_recv, pre_send, pre_recv, suf_send, suf_recv,
    y_send, y_recv, prev_send, prev_recv,
    rhs_send, rhs_recv, coef_send, coef_recv, go,
    corner_0, corner_1, corner_2, corner_3, corner_scale, help_out, help_in,
    corner_send, corner_recv, scale_send, scale_recv, lent_send, lent_recv, help_send, help_recv,
):
    corners = (corner_0, corner_1, corner_2, corner_3)
    chunk = own.shape[1]
    half = own.shape[2] // 2
    share = forcing_t.shape[2]
    part = back.shape[2]
    s, r, c = lax.axis_index("sec"), lax.axis_index("row"), lax.axis_index("col")
    other = 1 - c
    ends = s == n_sec - 1
    active = r <= 2 * c + 1
    paired = r < 2
    corner = jnp.logical_and(r == 0, c == 0)
    helped = jnp.logical_and(corner, lax.rem(s, 2) == 1)
    helper = jnp.logical_and(corner, lax.rem(s, 2) == 0)
    needed = jnp.logical_or(paired, c == 0)

    def last(k):
        return 2 * c + k // HALF

    def chunk_rows(k):
        return pl.ds(pl.multiple_of(k * chunk, chunk), chunk)

    def load(k):
        rows = chunk_rows(k)
        return pltpu.make_async_copy(
            factor_hbm.at[0, :, rows, :], factor.at[:, rows, :], load_sem.at[k]
        )

    def half_rows(col):
        return pl.ds(pl.multiple_of(col * share, share), share)

    def remote(src, dst, send_sem, recv_sem, device):
        return pltpu.make_async_remote_copy(
            src_ref=src, dst_ref=dst, send_sem=send_sem, recv_sem=recv_sem,
            device_id=device, device_id_type=MESH,
        )

    across = (s, r, other)
    after = (lax.rem(s + 1, n_sec), r, c)

    def part_rows(j):
        return pl.ds(pl.multiple_of(j * part, part), part)

    def send_source(j):
        rows = part_rows(j)
        at = lax.rem(j, 2)
        return remote(src_a.at[rows], src_a.at[rows], src_send.at[at], src_recv.at[at], across)

    before = (lax.rem(s + n_sec - 1, n_sec), r, c)

    def send_corner(m):
        rows, cols = slice(m * chunk, (m + 1) * chunk), slice(0, (m + 1) * part)
        return remote(
            factor_hbm.at[0, :, rows, cols], corners[m], corner_send.at[m], corner_recv.at[m], before
        )

    def send_scale():
        scales = dinv.at[0, :, slice(0, HALF * chunk)]
        return remote(scales, corner_scale, scale_send, scale_recv, before)

    def send_lent(j):
        rows = part_rows(j)
        return [
            remote(held.at[rows], held.at[rows], lent_send.at[i, j], lent_recv.at[i, j], before)
            for i, held in enumerate((src_a, src_b))
        ]

    def send_help(j):
        return remote(help_out.at[j], help_in.at[j], help_send.at[j], help_recv.at[j], after)

    def send_rhs():
        return remote(forcing_t.at[c], forcing_t.at[c], rhs_send, rhs_recv, across)

    def send_coef():
        return remote(coupling_all.at[c], coupling_all.at[c], coef_send, coef_recv, across)

    def send_pre(k, h):
        rows = pl.ds(h * (chunk // SUBS), chunk // SUBS)
        at = k * SUBS + h
        return remote(
            pre_out.at[k, rows], pre_in.at[k, rows], pre_send.at[at], pre_recv.at[at],
            (s, lax.rem(r + 1, n_row), c),
        )

    def send_suf(k, h):
        rows = pl.ds(h * (chunk // SUBS), chunk // SUBS)
        at = k * SUBS + h
        return remote(
            suf_out.at[k, rows], suf_in.at[k, rows], suf_send.at[at], suf_recv.at[at],
            (s, lax.rem(r + n_row - 1, n_row), c),
        )

    def send_y(j):
        return remote(y_out.at[j], y_in.at[j], y_send.at[j], y_recv.at[j], across)

    def send_prev(j):
        return remote(prev_out.at[j], prev_in.at[j], prev_send.at[j], prev_recv.at[j], after)

    count = jnp.int32(0)
    packed = {place: plan_words(*place[:2], plan) for place, plan in PLANS.items()}
    words = [jnp.int32(0)] * max(len(held) for _, held in packed.values())
    for (col, row, odd), (length, held) in packed.items():
        mine = jnp.logical_and(jnp.logical_and(c == col, r == row), odd * (1 - lax.rem(s, 2)) == 0)
        count = jnp.where(mine, length, count)
        for i, word in enumerate(held):
            words[i] = jnp.where(mine, word, words[i])

    for i in range(CHUNKS):
        k = (i + HALF) % CHUNKS

        @pl.when(jnp.logical_and(r <= last(k), jnp.logical_not(helped)) if k < HALF else r <= last(k))
        def _(k=k):
            load(k).start()

    barrier = pltpu.get_barrier_semaphore()
    for device in (
        (s, lax.rem(r + 1, n_row), c), (s, lax.rem(r + n_row - 1, n_row), c), across,
        after, before,
    ):
        pl.semaphore_signal(barrier, 1, device_id=device, device_id_type=MESH)

    def turned(value):
        return jnp.concatenate([-value[:, half:], value[:, :half]], axis=1)

    def product(k, cols):
        rows = chunk_rows(k)
        total = jnp.dot(factor[0, rows, cols], src_a[cols, :], preferred_element_type=jnp.float32)
        return total + jnp.dot(
            factor[1, rows, cols], src_b[cols, :], preferred_element_type=jnp.float32
        )

    def begin(first, stop):
        @pl.loop(first, stop)
        def _(i):
            k = lax.rem(i + HALF, CHUNKS)

            @pl.when(r < last(k))
            def _():
                load(k).wait()
                own[k] = product(k, half_rows(c))

    back[...] = jnp.zeros_like(back)

    @pl.when(s == 0)
    def _():
        src_a[half_rows(c), :] = forcing[0].astype(jnp.bfloat16)
        src_b[half_rows(c), :] = turned(forcing[0].astype(jnp.bfloat16).astype(jnp.float32)).astype(
            jnp.bfloat16
        )
        begin(0, EARLY)

    @pl.when(s > 0)
    def _():
        forcing_t[c] = forcing[0].T
        coupling_all[c] = coupling[0]

    pl.semaphore_wait(barrier, 5)

    @pl.when(s == 0)
    def _():
        @pl.when(needed)
        def _():
            for i in range(2):
                send_source(2 * c + i).start()

        begin(EARLY, BEGUN)
        pl.semaphore_signal(go, 1, device_id=after, device_id_type=MESH)

    @pl.when(helped)
    def _():
        send_scale().start()
        for m in range(PARTS):
            send_corner(m).start()

    @pl.when(s == 1)
    def _():
        pl.semaphore_wait(go, 1)

    @pl.when(s > 0)
    def _():
        send_rhs().start()
        send_coef().start()
        send_rhs().wait_recv()
        send_coef().wait_recv()

    def source_step(j):
        rows = part_rows(j)

        @pl.when(jnp.logical_and(s == 0, j // 2 != c))
        def _():
            send_source(j).wait_recv()
            src_b[rows, :] = turned(src_a[rows, :].astype(jnp.float32)).astype(jnp.bfloat16)

        @pl.when(s > 0)
        def _():
            send_prev(j).wait_recv()
            col, cols = j // 2, part_rows(lax.rem(j, 2))
            previous = prev_in[j].astype(jnp.float32)
            p_re, p_im = previous[:half], previous[half:]
            c_re, c_im = coupling_all[col, 0:1, cols], coupling_all[col, 1:2, cols]
            new_re = forcing_t[col, :half, cols] - (c_re * p_re - c_im * p_im)
            new_im = forcing_t[col, half:, cols] - (c_re * p_im + c_im * p_re)
            src_a[rows, :] = jnp.concatenate([new_re, new_im], axis=0).T.astype(jnp.bfloat16)
            src_b[rows, :] = jnp.concatenate([-new_im, new_re], axis=0).T.astype(jnp.bfloat16)

            @pl.when(helped)
            def _():
                for copy in send_lent(j):
                    copy.start()

    def keep(k, total):
        own[k] = total
        pre_out[k] = total.astype(jnp.bfloat16)
        suf_out[k] = total.astype(jnp.bfloat16)

    def forward_full(k):
        begun = jnp.logical_and(s == 0, lax.rem(k + HALF, CHUNKS) < BEGUN)

        @pl.when(begun)
        def _():
            keep(k, own[k] + product(k, half_rows(other)))

        @pl.when(jnp.logical_not(begun))
        def _():
            load(k).wait()
            keep(k, product(k, slice(0, PARTS * part)))

        @pl.when(r == 0)
        def _():
            for h in range(SUBS):
                send_pre(k, h).start()

    def forward_first(k):
        load(k).wait()
        own[k] = product(k, slice(0, 2 * part))

    def forward_second(k):
        keep(k, own[k] + product(k, slice(2 * part, 4 * part)))
        for h in range(SUBS):
            send_pre(k, h).start()

    def forward_diagonal(m, k):
        load(k).wait()
        keep(k, product(k, slice(0, (m + 1) * part)))

        @pl.when(r > 0)
        def _():
            for h in range(SUBS):
                send_suf(k, h).start()

    def relay(send, held, came, k):
        for h in range(SUBS):
            rows = slice(h * (chunk // SUBS), (h + 1) * (chunk // SUBS))
            send(k, h).wait_recv()
            held[k, rows, :] += came[k, rows, :]
            send(k, h).start()

    def relay_right(k):
        relay(send_pre, pre_out, pre_in, k)

    def relay_left(k):
        relay(send_suf, suf_out, suf_in, k)

    def gather(m, total, scale, block_re, block_im):
        forward = total.T
        d_re, d_im = scale[0:1], scale[1:2]
        f_re, f_im = forward[:half], forward[half:]
        s_re, s_im = d_re * f_re - d_im * f_im, d_re * f_im + d_im * f_re
        lhs_a = jnp.concatenate([s_re, s_im], axis=0).astype(jnp.bfloat16)
        lhs_b = jnp.concatenate([-s_im, s_re], axis=0).astype(jnp.bfloat16)
        total = jnp.dot(lhs_a, block_re, preferred_element_type=jnp.float32)
        total += jnp.dot(lhs_b, block_im, preferred_element_type=jnp.float32)
        for j in range(m + 1):
            back[j] += total[:, j * part : (j + 1) * part]

    def back_step(left, right, m, k):
        rows = chunk_rows(k)
        total = own[k]
        if left != right:
            for h in range(SUBS):
                (send_pre if left else send_suf)(k, h).wait_recv()
        if left:
            total += pre_in[k].astype(jnp.float32)
        if right:
            total += suf_in[k].astype(jnp.float32)
        cols = slice(0, (m + 1) * part)
        gather(m, total, dinv[0, :, rows], factor[0, rows, cols], factor[1, rows, cols])

    def act(action, k):
        kind = action[0]
        if kind == "F":
            if action[1] == PARTS:
                forward_full(k)
            else:
                forward_diagonal(action[1], k)
        elif kind == "B":
            back_step(action[1], action[2], action[3] if len(action) > 3 else PARTS - 1, k)
        else:
            {
                "R": relay_right, "L": relay_left, "S": source_step,
                "G": forward_first, "H": forward_second,
            }[kind](k)

    def dispatch(step, first, stop, k):
        if stop - first == 1:
            act(ACTIONS[first], k)
            return
        middle = (first + stop) // 2

        @pl.when(step < middle)
        def _():
            dispatch(step, first, middle, k)

        @pl.when(step >= middle)
        def _():
            dispatch(step, middle, stop, k)

    @pl.loop(0, count)
    def _(e):
        at = e // PER_WORD
        word = words[0]
        for i in range(1, len(words)):
            word = jnp.where(at == i, words[i], word)
        code = lax.rem(lax.shift_right_logical(word, 8 * lax.rem(e, PER_WORD)), 256)
        dispatch(code // CHUNKS, 0, len(ACTIONS), lax.rem(code, CHUNKS))

    @pl.when(helped)
    def _():
        for j in range(PARTS):
            send_help(j).wait_recv()
            back[j] += help_in[j].astype(jnp.float32)

    @pl.when(jnp.logical_and(s == 0, needed))
    def _():
        for i in range(2):
            send_source(2 * c + i).wait_send()

    def order(first, i):
        return (2 * first + i) % PARTS if isinstance(first, int) else lax.rem(2 * first + i, PARTS)

    def sends_y(i):
        wanted = jnp.logical_or(paired, c == 1) if i < 2 else paired
        return wanted if i < 2 else jnp.logical_and(wanted, jnp.logical_not(ends))

    def takes_y(i):
        wanted = jnp.logical_or(paired, c == 0) if i < 2 else paired
        return wanted if i < 2 else jnp.logical_and(wanted, jnp.logical_not(ends))

    for i in range(PARTS):
        j = order(other, i)

        @pl.when(sends_y(i))
        def _(j=j):
            y_out[j] = back[j].astype(jnp.bfloat16)
            send_y(j).start()

    passes = jnp.logical_and(active, jnp.logical_not(ends))
    for i in range(PARTS):
        j = order(c, i)

        @pl.when(takes_y(i))
        def _(j=j):
            send_y(j).wait_recv()
            back[j] += y_in[j].astype(jnp.float32)

        @pl.when(passes)
        def _(j=j):
            prev_out[j] = back[j].astype(jnp.bfloat16)
            send_prev(j).start()

    for i in range(2):
        out[0, i * part : (i + 1) * part, :] = back[order(c, i)].T

    @pl.when(helper)
    def _():
        back[...] = jnp.zeros_like(back)
        send_scale().wait_recv()
        for m in range(PARTS):
            send_corner(m).wait_recv()
            for copy in send_lent(m):
                copy.wait_recv()
            rows, cols = slice(m * chunk, (m + 1) * chunk), slice(0, (m + 1) * part)
            total = jnp.dot(corners[m][0], src_a[cols, :], preferred_element_type=jnp.float32)
            total += jnp.dot(corners[m][1], src_b[cols, :], preferred_element_type=jnp.float32)
            gather(m, total, corner_scale[:, rows], corners[m][0], corners[m][1])
        for j in range(PARTS):
            help_out[j] = back[j].astype(jnp.bfloat16)
            send_help(j).start()
        for j in range(PARTS):
            send_help(j).wait_send()

    @pl.when(helped)
    def _():
        send_scale().wait_send()
        for m in range(PARTS):
            send_corner(m).wait_send()
            for copy in send_lent(m):
                copy.wait_send()

    @pl.when(s > 0)
    def _():
        send_rhs().wait_send()
        send_coef().wait_send()

    for k in range(CHUNKS):
        @pl.when(r < last(k))
        def _(k=k):
            for h in range(SUBS):
                send_pre(k, h).wait_send()

        @pl.when(jnp.logical_and(r > 0, r <= last(k)))
        def _(k=k):
            for h in range(SUBS):
                send_suf(k, h).wait_send()

    for i in range(PARTS):
        @pl.when(sends_y(i))
        def _(i=i):
            send_y(order(other, i)).wait_send()

        @pl.when(passes)
        def _(i=i):
            send_prev(i).wait_send()


def sweep(n_sec, n_row, n_col, forcing, inverse_factor, diag_inverse, coupling):
    share, width = forcing.shape[1:]
    block_rows, block_cols = inverse_factor.shape[2:]
    chunk, part = block_rows // CHUNKS, block_cols // PARTS
    vmem = pl.BlockSpec(memory_space=pltpu.VMEM)
    bf16, f32 = jnp.bfloat16, jnp.float32
    dma = pltpu.SemaphoreType.DMA
    return pl.pallas_call(
        functools.partial(sweep_kernel, n_sec, n_row, n_col),
        out_shape=jax.ShapeDtypeStruct(forcing.shape, f32),
        in_specs=[vmem, vmem, vmem, pl.BlockSpec(memory_space=pl.ANY)],
        out_specs=vmem,
        scratch_shapes=[
            pltpu.VMEM((2, block_rows, block_cols), bf16),
            pltpu.VMEM((block_cols, width), bf16),
            pltpu.VMEM((block_cols, width), bf16),
            pltpu.VMEM((CHUNKS, chunk, width), f32),
            pltpu.VMEM((CHUNKS, chunk, width), bf16),
            pltpu.VMEM((CHUNKS, chunk, width), bf16),
            pltpu.VMEM((CHUNKS, chunk, width), bf16),
            pltpu.VMEM((CHUNKS, chunk, width), bf16),
            pltpu.VMEM((PARTS, width, part), f32),
            pltpu.VMEM((PARTS, width, part), bf16),
            pltpu.VMEM((PARTS, width, part), bf16),
            pltpu.VMEM((PARTS, width, part), bf16),
            pltpu.VMEM((PARTS, width, part), bf16),
            pltpu.VMEM((n_col, width, share), f32),
            pltpu.VMEM((n_col, 2, share), f32),
            dma((CHUNKS,)),
            dma((2,)), dma((2,)),
            dma((CHUNKS * SUBS,)), dma((CHUNKS * SUBS,)),
            dma((CHUNKS * SUBS,)), dma((CHUNKS * SUBS,)),
            dma((PARTS,)), dma((PARTS,)),
            dma((PARTS,)), dma((PARTS,)),
            dma, dma, dma, dma,
            pltpu.SemaphoreType.REGULAR,
            *[pltpu.VMEM((2, chunk, (m + 1) * part), bf16) for m in range(PARTS)],
            pltpu.VMEM((2, HALF * chunk), f32),
            pltpu.VMEM((PARTS, width, part), bf16),
            pltpu.VMEM((PARTS, width, part), bf16),
            dma((PARTS,)), dma((PARTS,)), dma, dma,
            dma((2, PARTS)), dma((2, PARTS)), dma((PARTS,)), dma((PARTS,)),
        ],
        compiler_params=pltpu.CompilerParams(
            collective_id=0, has_side_effects=True, vmem_limit_bytes=60 * 2**20
        ),
    )(forcing, diag_inverse, coupling, inverse_factor)


def solution(mesh):
    placed = (
        P("sec", ("row", "col"), None),
        P("sec", None, "col", "row"),
        P("sec", None, "col"),
        P("sec", None, ("row", "col")),
    )
    n_sec, n_row, n_col = (mesh.shape[axis] for axis in ("sec", "row", "col"))

    def body(forcing, inverse_factor, diag_inverse, coupling):
        share, width = forcing.shape[1:]
        fits = inverse_factor.size * 2 <= 32 * 2**20
        block = inverse_factor.shape[2] == 4 * share and inverse_factor.shape[3] == 2 * share
        if share % 256 or width % 128 or not fits or n_sec != 4 or (n_row, n_col) != (4, 2) or not block:
            return local(forcing, inverse_factor, diag_inverse, coupling)
        return sweep(n_sec, n_row, n_col, forcing, inverse_factor, diag_inverse, coupling)

    return jax.shard_map(
        body, mesh=mesh, in_specs=placed, out_specs=P("sec", ("row", "col"), None), check_vma=False
    )
```

```python
import functools

import jax
import jax.numpy as jnp
from jax import lax
from jax.experimental import pallas as pl
from jax.experimental.pallas import tpu as pltpu
from jax.sharding import PartitionSpec as P


def shifted(value, axis, steps):
    count = lax.axis_size(axis)
    initial, last = (max(0, -steps), min(count, count - steps))
    return lax.ppermute(value, axis, [(source, source + steps) for source in range(initial, last)])


def complex_rows(coef_re, coef_im, values, half):
    v_re = values[:, :half]
    v_im = values[:, half:]
    out_re = coef_re[:, None] * v_re - coef_im[:, None] * v_im
    out_im = coef_re[:, None] * v_im + coef_im[:, None] * v_re
    return jnp.concatenate([out_re, out_im], axis=1)


def combine_stack(product):
    half = product.shape[2] // 2
    out_re = product[0, :, :half] - product[1, :, half:]
    out_im = product[0, :, half:] + product[1, :, :half]
    return jnp.concatenate([out_re, out_im], axis=1)


def solve_section(source, factor, dinv):
    width = source.shape[1]
    product = jnp.einsum(
        "kij,jb->kib",
        factor,
        lax.all_gather(source, "col", axis=0, tiled=True),
        preferred_element_type=jnp.float32,
    )
    forward = combine_stack(product)
    share = lax.psum_scatter(
        forward.astype(jnp.bfloat16), "row", scatter_dimension=0, tiled=True
    ).astype(jnp.float32)
    share_rows = share.shape[0]
    local_dinv = lax.dynamic_slice_in_dim(dinv, lax.axis_index("row") * share_rows, share_rows, 1)
    scaled = complex_rows(local_dinv[0], local_dinv[1], share, width // 2).astype(jnp.bfloat16)
    product = jnp.einsum(
        "kij,ib->kjb",
        factor,
        lax.all_gather(scaled, "row", axis=0, tiled=True),
        preferred_element_type=jnp.float32,
    )
    back = combine_stack(product)
    return lax.psum_scatter(
        back.astype(jnp.bfloat16), "col", scatter_dimension=0, tiled=True
    ).astype(jnp.float32)


def local(forcing, inverse_factor, diag_inverse, coupling):
    sections = lax.axis_size("sec")
    section_id = lax.axis_index("sec")
    local_rhs = forcing[0]
    factor = inverse_factor[0]
    dinv = diag_inverse[0]
    couple = coupling[0]
    rows_here = local_rhs.shape[0]
    half = local_rhs.shape[1] // 2
    block_count = 1
    block_width = half // block_count
    rhs_blocks = local_rhs.reshape(rows_here, 2, block_count, block_width)
    results = jnp.zeros((rows_here, 2, block_count, block_width), jnp.float32)
    outgoing = jnp.zeros((rows_here, 2 * block_width), jnp.float32)
    for step_index in range(block_count + sections - 1):
        if step_index > 0:
            incoming = shifted(outgoing.astype(jnp.bfloat16), "sec", 1).astype(outgoing.dtype)
        else:
            incoming = jnp.zeros((rows_here, 2 * block_width), jnp.float32)
        block_index = step_index - section_id
        active = jnp.logical_and(block_index >= 0, block_index < block_count)
        safe_index = jnp.clip(block_index, 0, block_count - 1)
        current = lax.dynamic_index_in_dim(rhs_blocks, safe_index, 2, keepdims=False)
        current = current.reshape(rows_here, 2 * block_width)
        source = (current - complex_rows(couple[0], couple[1], incoming, block_width)).astype(
            jnp.bfloat16
        )
        field = solve_section(source, factor, dinv)
        updated = lax.dynamic_update_index_in_dim(
            results, field.reshape(rows_here, 2, block_width), safe_index, 2
        )
        results = jnp.where(active, updated, results)
        outgoing = field
    return results.reshape(1, rows_here, 2 * half)


MESH = pl.DeviceIdType.MESH

CHUNKS = 8
SUBS = 2
HALF = CHUNKS // 2
PARTS = 4
EARLY = 2
BEGUN = 6
LENT = 6
PLANS = {
    (1, 0, 0): (
        0o40, 0o41, 0o42, 0o43, 0o04, 0o05, 0o06, 0o07, 0o00, 0o01, 0o02, 0o03, 0o30, 0o31, 0o34,
        0o32, 0o35, 0o36, 0o37, 0o33,
    ),
    (1, 1, 0): (
        0o40, 0o41, 0o42, 0o43, 0o04, 0o05, 0o00, 0o20, 0o01, 0o14, 0o21, 0o15, 0o06, 0o24, 0o16,
        0o07, 0o17, 0o02, 0o22, 0o25, 0o10, 0o26, 0o11, 0o03, 0o27, 0o12, 0o34, 0o23, 0o13, 0o35,
        0o30, 0o36, 0o31, 0o37, 0o32, 0o33,
    ),
    (1, 2, 0): (
        0o40, 0o41, 0o42, 0o43, 0o00, 0o04, 0o01, 0o05, 0o24, 0o02, 0o25, 0o06, 0o26, 0o07, 0o27,
        0o03, 0o14, 0o15, 0o34, 0o16, 0o35, 0o17, 0o36, 0o37, 0o30, 0o31, 0o32, 0o33,
    ),
    (1, 3, 0): (
        0o40, 0o41, 0o42, 0o43, 0o04, 0o05, 0o06, 0o07, 0o34, 0o35, 0o36, 0o37,
    ),
    (1, 0, 2): (
        0o40, 0o41, 0o42, 0o43, 0o04, 0o05, 0o76, 0o77, 0o00, 0o01, 0o02, 0o03, 0o30, 0o31, 0o34,
        0o32, 0o35, 0o33, 0o36, 0o37,
    ),
    (1, 1, 2): (
        0o40, 0o41, 0o42, 0o43, 0o00, 0o01, 0o04, 0o20, 0o05, 0o14, 0o21, 0o15, 0o76, 0o02, 0o24,
        0o16, 0o77, 0o22, 0o17, 0o03, 0o25, 0o10, 0o34, 0o23, 0o11, 0o35, 0o26, 0o12, 0o30, 0o27,
        0o13, 0o31, 0o36, 0o32, 0o37, 0o33,
    ),
    (1, 2, 2): (
        0o40, 0o41, 0o42, 0o43, 0o00, 0o04, 0o01, 0o05, 0o24, 0o76, 0o02, 0o25, 0o77, 0o03, 0o26,
        0o27, 0o14, 0o34, 0o15, 0o35, 0o16, 0o36, 0o17, 0o37, 0o30, 0o31, 0o32, 0o33,
    ),
    (0, 0, 0): (
        0o40, 0o00, 0o41, 0o01, 0o42, 0o02, 0o43, 0o04, 0o05, 0o06, 0o07, 0o03, 0o34, 0o35, 0o36,
        0o37, 0o30, 0o31, 0o32, 0o33,
    ),
    (0, 0, 1): (
        0o40, 0o41, 0o54, 0o55, 0o42, 0o56, 0o57, 0o43, 0o64, 0o65, 0o66, 0o67, 0o34, 0o35, 0o36,
        0o37,
    ),
    (0, 1, 0): (
        0o40, 0o04, 0o41, 0o05, 0o42, 0o06, 0o43, 0o07, 0o34, 0o35, 0o36, 0o37,
    ),
}
PER_WORD = 3
ACTIONS = [("F", m) for m in range(PARTS + 1)] + [("R",), ("L",), ("S",), ("G",), ("H",), ("W",)] + [("B", True, True), ("B", False, True)]
ACTIONS += [("B", left, False, m) for left in (True, False) for m in range(PARTS)]


def plan_words(col, row, plan):
    codes = []
    for step in plan:
        kind, k = "FRLBSGHW"[step // CHUNKS], step % CHUNKS
        end = 2 * col + k // HALF
        if kind == "F":
            action = ("F", k % HALF if row == end else PARTS)
        elif kind == "B":
            action = ("B", row > 0, row < end)
            action += () if row < end else (k % HALF,)
        else:
            action = (kind,)
        codes.append(ACTIONS.index(action) * CHUNKS + k)
    words = []
    for i in range(0, len(codes), PER_WORD):
        words.append(sum(code * 256**j for j, code in enumerate(codes[i : i + PER_WORD])))
    return len(codes), words


def sweep_kernel(
    n_sec, n_row, n_col, forcing, dinv, coupling, factor_hbm, out,
    factor, src_a, src_b, own, pre_in, suf_in, pre_out, suf_out,
    back, y_out, y_in, prev_out, prev_in, forcing_t, coupling_all,
    load_sem, src_send, src_recv, pre_send, pre_recv, suf_send, suf_recv,
    y_send, y_recv, prev_send, prev_recv,
    rhs_send, rhs_recv, coef_send, coef_recv, go,
    corner_0, corner_1, corner_2, corner_3, corner_scale, help_out, help_in,
    corner_send, corner_recv, scale_send, scale_recv, lent_send, lent_recv, help_send, help_recv, lend_send, lend_recv,
):
    corners = (corner_0, corner_1, corner_2, corner_3)
    chunk = own.shape[1]
    half = own.shape[2] // 2
    share = forcing_t.shape[2]
    part = back.shape[2]
    s, r, c = lax.axis_index("sec"), lax.axis_index("row"), lax.axis_index("col")
    other = 1 - c
    ends = s == n_sec - 1
    active = r <= 2 * c + 1
    paired = r < 2
    corner = jnp.logical_and(r == 0, c == 0)
    helped = jnp.logical_and(corner, lax.rem(s, 2) == 1)
    helper = jnp.logical_and(corner, lax.rem(s, 2) == 0)
    inner = jnp.logical_and(c == 1, r < n_row - 1)
    lent = jnp.logical_and(inner, s > 0)
    lends = jnp.logical_and(inner, s != 1)
    needed = jnp.logical_or(paired, c == 0)

    def last(k):
        return 2 * c + k // HALF

    def chunk_rows(k):
        return pl.ds(pl.multiple_of(k * chunk, chunk), chunk)

    def load(k):
        rows = chunk_rows(k)
        return pltpu.make_async_copy(
            factor_hbm.at[0, :, rows, :], factor.at[:, rows, :], load_sem.at[k]
        )

    def half_rows(col):
        return pl.ds(pl.multiple_of(col * share, share), share)

    def remote(src, dst, send_sem, recv_sem, device):
        return pltpu.make_async_remote_copy(
            src_ref=src, dst_ref=dst, send_sem=send_sem, recv_sem=recv_sem,
            device_id=device, device_id_type=MESH,
        )

    across = (s, r, other)
    after = (lax.rem(s + 1, n_sec), r, c)

    def part_rows(j):
        return pl.ds(pl.multiple_of(j * part, part), part)

    def send_source(j):
        rows = part_rows(j)
        at = lax.rem(j, 2)
        return remote(src_a.at[rows], src_a.at[rows], src_send.at[at], src_recv.at[at], across)

    before = (lax.rem(s + n_sec - 1, n_sec), r, c)

    partner = (s + 1 - 2 * lax.rem(s, 2), r, c)

    def send_block(i):
        k, m, first, stop = ((LENT, 3, 0, 4), (LENT + 1, 2, 0, 3), (LENT + 1, 0, 3, 4))[i]
        rows, cols = slice(k * chunk, (k + 1) * chunk), slice(first * part, stop * part)
        return remote(
            factor_hbm.at[0, :, rows, cols], corners[m], corner_send.at[m], corner_recv.at[m], partner
        )

    def send_lend(k):
        at = k - LENT
        return remote(own.at[k], own.at[k], lend_send.at[at], lend_recv.at[at], partner)

    def send_corner(m):
        rows, cols = slice(m * chunk, (m + 1) * chunk), slice(0, (m + 1) * part)
        return remote(
            factor_hbm.at[0, :, rows, cols], corners[m], corner_send.at[m], corner_recv.at[m], before
        )

    def send_scale():
        scales = dinv.at[0, :, slice(0, HALF * chunk)]
        return remote(scales, corner_scale, scale_send, scale_recv, before)

    def send_lent(j):
        rows = part_rows(j)
        return [
            remote(held.at[rows], held.at[rows], lent_send.at[i, j], lent_recv.at[i, j], partner)
            for i, held in enumerate((src_a, src_b))
        ]

    def send_help(j):
        return remote(help_out.at[j], help_in.at[j], help_send.at[j], help_recv.at[j], after)

    def send_rhs():
        return remote(forcing_t.at[c], forcing_t.at[c], rhs_send, rhs_recv, across)

    def send_coef():
        return remote(coupling_all.at[c], coupling_all.at[c], coef_send, coef_recv, across)

    def send_pre(k, h):
        rows = pl.ds(h * (chunk // SUBS), chunk // SUBS)
        at = k * SUBS + h
        return remote(
            pre_out.at[k, rows], pre_in.at[k, rows], pre_send.at[at], pre_recv.at[at],
            (s, lax.rem(r + 1, n_row), c),
        )

    def send_suf(k, h):
        rows = pl.ds(h * (chunk // SUBS), chunk // SUBS)
        at = k * SUBS + h
        return remote(
            suf_out.at[k, rows], suf_in.at[k, rows], suf_send.at[at], suf_recv.at[at],
            (s, lax.rem(r + n_row - 1, n_row), c),
        )

    def send_y(j):
        return remote(y_out.at[j], y_in.at[j], y_send.at[j], y_recv.at[j], across)

    def send_prev(j):
        return remote(prev_out.at[j], prev_in.at[j], prev_send.at[j], prev_recv.at[j], after)

    count = jnp.int32(0)
    packed = {place: plan_words(*place[:2], plan) for place, plan in PLANS.items()}
    words = [jnp.int32(0)] * max(len(held) for _, held in packed.values())
    for (col, row, where), (length, held) in packed.items():
        mine = jnp.logical_and(c == col, r == row)
        if where:
            mine = jnp.logical_and(mine, lax.rem(s, 2) == 1 if where == 1 else s > 0)
        count = jnp.where(mine, length, count)
        for i, word in enumerate(held):
            words[i] = jnp.where(mine, word, words[i])

    for i in range(CHUNKS):
        k = (i + HALF) % CHUNKS

        @pl.when(jnp.logical_and(r <= last(k), jnp.logical_not(helped)) if k < HALF else r <= last(k))
        def _(k=k):
            load(k).start()

    barrier = pltpu.get_barrier_semaphore()
    for device in (
        (s, lax.rem(r + 1, n_row), c), (s, lax.rem(r + n_row - 1, n_row), c), across,
        after, before,
    ):
        pl.semaphore_signal(barrier, 1, device_id=device, device_id_type=MESH)

    def turned(value):
        return jnp.concatenate([-value[:, half:], value[:, :half]], axis=1)

    def product(k, cols):
        rows = chunk_rows(k)
        total = jnp.dot(factor[0, rows, cols], src_a[cols, :], preferred_element_type=jnp.float32)
        return total + jnp.dot(
            factor[1, rows, cols], src_b[cols, :], preferred_element_type=jnp.float32
        )

    def begin(first, stop):
        @pl.loop(first, stop)
        def _(i):
            k = lax.rem(i + HALF, CHUNKS)

            @pl.when(r < last(k))
            def _():
                load(k).wait()
                own[k] = product(k, half_rows(c))

    back[...] = jnp.zeros_like(back)

    @pl.when(s == 0)
    def _():
        src_a[half_rows(c), :] = forcing[0].astype(jnp.bfloat16)
        src_b[half_rows(c), :] = turned(forcing[0].astype(jnp.bfloat16).astype(jnp.float32)).astype(
            jnp.bfloat16
        )
        begin(0, EARLY)

    @pl.when(s > 0)
    def _():
        forcing_t[c] = forcing[0].T
        coupling_all[c] = coupling[0]

    pl.semaphore_wait(barrier, 5)

    @pl.when(s == 0)
    def _():
        @pl.when(needed)
        def _():
            for i in range(2):
                send_source(2 * c + i).start()

        begin(EARLY, BEGUN)
        pl.semaphore_signal(go, 1, device_id=after, device_id_type=MESH)

    @pl.when(helped)
    def _():
        send_scale().start()
        for m in range(PARTS):
            send_corner(m).start()

    @pl.when(lent)
    def _():
        for i in range(3):
            send_block(i).start()

    @pl.when(s == 1)
    def _():
        pl.semaphore_wait(go, 1)

    @pl.when(s > 0)
    def _():
        send_rhs().start()
        send_coef().start()
        send_rhs().wait_recv()
        send_coef().wait_recv()

    def source_step(j):
        rows = part_rows(j)

        @pl.when(jnp.logical_and(s == 0, j // 2 != c))
        def _():
            send_source(j).wait_recv()
            src_b[rows, :] = turned(src_a[rows, :].astype(jnp.float32)).astype(jnp.bfloat16)

        @pl.when(s > 0)
        def _():
            send_prev(j).wait_recv()
            col, cols = j // 2, part_rows(lax.rem(j, 2))
            previous = prev_in[j].astype(jnp.float32)
            p_re, p_im = previous[:half], previous[half:]
            c_re, c_im = coupling_all[col, 0:1, cols], coupling_all[col, 1:2, cols]
            new_re = forcing_t[col, :half, cols] - (c_re * p_re - c_im * p_im)
            new_im = forcing_t[col, half:, cols] - (c_re * p_im + c_im * p_re)
            src_a[rows, :] = jnp.concatenate([new_re, new_im], axis=0).T.astype(jnp.bfloat16)
            src_b[rows, :] = jnp.concatenate([-new_im, new_re], axis=0).T.astype(jnp.bfloat16)

            @pl.when(jnp.logical_or(helped, lent))
            def _():
                for copy in send_lent(j):
                    copy.start()

    def keep(k, total):
        own[k] = total
        pre_out[k] = total.astype(jnp.bfloat16)
        suf_out[k] = total.astype(jnp.bfloat16)

    def forward_full(k):
        begun = jnp.logical_and(s == 0, lax.rem(k + HALF, CHUNKS) < BEGUN)

        @pl.when(begun)
        def _():
            keep(k, own[k] + product(k, half_rows(other)))

        @pl.when(jnp.logical_not(begun))
        def _():
            load(k).wait()
            keep(k, product(k, slice(0, PARTS * part)))

        @pl.when(r == 0)
        def _():
            for h in range(SUBS):
                send_pre(k, h).start()

    def forward_first(k):
        load(k).wait()
        own[k] = product(k, slice(0, 2 * part))

    def forward_second(k):
        keep(k, own[k] + product(k, slice(2 * part, 4 * part)))
        for h in range(SUBS):
            send_pre(k, h).start()

    def forward_lent(k):
        load(k).wait()
        send_lend(k).wait_recv()
        pre_out[k] = own[k].astype(jnp.bfloat16)
        suf_out[k] = own[k].astype(jnp.bfloat16)

        @pl.when(r == 0)
        def _():
            for h in range(SUBS):
                send_pre(k, h).start()

    def forward_diagonal(m, k):
        load(k).wait()
        keep(k, product(k, slice(0, (m + 1) * part)))

        @pl.when(r > 0)
        def _():
            for h in range(SUBS):
                send_suf(k, h).start()

    def relay(send, held, came, k):
        for h in range(SUBS):
            rows = slice(h * (chunk // SUBS), (h + 1) * (chunk // SUBS))
            send(k, h).wait_recv()
            held[k, rows, :] += came[k, rows, :]
            send(k, h).start()

    def relay_right(k):
        relay(send_pre, pre_out, pre_in, k)

    def relay_left(k):
        relay(send_suf, suf_out, suf_in, k)

    def gather(m, total, scale, block_re, block_im):
        forward = total.T
        d_re, d_im = scale[0:1], scale[1:2]
        f_re, f_im = forward[:half], forward[half:]
        s_re, s_im = d_re * f_re - d_im * f_im, d_re * f_im + d_im * f_re
        lhs_a = jnp.concatenate([s_re, s_im], axis=0).astype(jnp.bfloat16)
        lhs_b = jnp.concatenate([-s_im, s_re], axis=0).astype(jnp.bfloat16)
        total = jnp.dot(lhs_a, block_re, preferred_element_type=jnp.float32)
        total += jnp.dot(lhs_b, block_im, preferred_element_type=jnp.float32)
        for j in range(m + 1):
            back[j] += total[:, j * part : (j + 1) * part]

    def back_step(left, right, m, k):
        rows = chunk_rows(k)
        total = own[k]
        if left != right:
            for h in range(SUBS):
                (send_pre if left else send_suf)(k, h).wait_recv()
        if left:
            total += pre_in[k].astype(jnp.float32)
        if right:
            total += suf_in[k].astype(jnp.float32)
        cols = slice(0, (m + 1) * part)
        gather(m, total, dinv[0, :, rows], factor[0, rows, cols], factor[1, rows, cols])

    def act(action, k):
        kind = action[0]
        if kind == "F":
            if action[1] == PARTS:
                forward_full(k)
            else:
                forward_diagonal(action[1], k)
        elif kind == "B":
            back_step(action[1], action[2], action[3] if len(action) > 3 else PARTS - 1, k)
        else:
            {
                "R": relay_right, "L": relay_left, "S": source_step,
                "G": forward_first, "H": forward_second, "W": forward_lent,
            }[kind](k)

    def dispatch(step, first, stop, k):
        if stop - first == 1:
            act(ACTIONS[first], k)
            return
        middle = (first + stop) // 2

        @pl.when(step < middle)
        def _():
            dispatch(step, first, middle, k)

        @pl.when(step >= middle)
        def _():
            dispatch(step, middle, stop, k)

    def lend():
        for j in range(PARTS):
            for copy in send_lent(j):
                copy.wait_recv()
        send_block(0).wait_recv()
        total = jnp.dot(corners[3][0], src_a[...], preferred_element_type=jnp.float32)
        total += jnp.dot(corners[3][1], src_b[...], preferred_element_type=jnp.float32)
        own[LENT] = total
        send_lend(LENT).start()
        send_block(1).wait_recv()
        send_block(2).wait_recv()
        total = jnp.zeros((chunk, 2 * half), jnp.float32)
        for m, cols in ((2, slice(0, 3 * part)), (0, slice(3 * part, 4 * part))):
            total += jnp.dot(corners[m][0], src_a[cols, :], preferred_element_type=jnp.float32)
            total += jnp.dot(corners[m][1], src_b[cols, :], preferred_element_type=jnp.float32)
        own[LENT + 1] = total
        send_lend(LENT + 1).start()
        for k in (LENT, LENT + 1):
            send_lend(k).wait_send()

    @pl.when(jnp.logical_and(lends, ends))
    def _():
        lend()

    @pl.loop(0, count)
    def _(e):
        at = e // PER_WORD
        word = words[0]
        for i in range(1, len(words)):
            word = jnp.where(at == i, words[i], word)
        code = lax.rem(lax.shift_right_logical(word, 8 * lax.rem(e, PER_WORD)), 256)
        dispatch(code // CHUNKS, 0, len(ACTIONS), lax.rem(code, CHUNKS))

    @pl.when(helped)
    def _():
        for j in range(PARTS):
            send_help(j).wait_recv()
            back[j] += help_in[j].astype(jnp.float32)

    @pl.when(jnp.logical_and(s == 0, needed))
    def _():
        for i in range(2):
            send_source(2 * c + i).wait_send()

    @pl.when(lent)
    def _():
        for j in range(PARTS):
            for copy in send_lent(j):
                copy.wait_send()

    def order(first, i):
        return (2 * first + i) % PARTS if isinstance(first, int) else lax.rem(2 * first + i, PARTS)

    def sends_y(i):
        wanted = jnp.logical_or(paired, c == 1) if i < 2 else paired
        return wanted if i < 2 else jnp.logical_and(wanted, jnp.logical_not(ends))

    def takes_y(i):
        wanted = jnp.logical_or(paired, c == 0) if i < 2 else paired
        return wanted if i < 2 else jnp.logical_and(wanted, jnp.logical_not(ends))

    for i in range(PARTS):
        j = order(other, i)

        @pl.when(sends_y(i))
        def _(j=j):
            y_out[j] = back[j].astype(jnp.bfloat16)
            send_y(j).start()

    passes = jnp.logical_and(active, jnp.logical_not(ends))
    for i in range(PARTS):
        j = order(c, i)

        @pl.when(takes_y(i))
        def _(j=j):
            send_y(j).wait_recv()
            back[j] += y_in[j].astype(jnp.float32)

        @pl.when(passes)
        def _(j=j):
            prev_out[j] = back[j].astype(jnp.bfloat16)
            send_prev(j).start()

    for i in range(2):
        out[0, i * part : (i + 1) * part, :] = back[order(c, i)].T

    @pl.when(jnp.logical_and(lends, jnp.logical_not(ends)))
    def _():
        lend()

    @pl.when(helper)
    def _():
        back[...] = jnp.zeros_like(back)
        send_scale().wait_recv()
        for m in range(PARTS):
            send_corner(m).wait_recv()
            for copy in send_lent(m):
                copy.wait_recv()
            rows, cols = slice(m * chunk, (m + 1) * chunk), slice(0, (m + 1) * part)
            total = jnp.dot(corners[m][0], src_a[cols, :], preferred_element_type=jnp.float32)
            total += jnp.dot(corners[m][1], src_b[cols, :], preferred_element_type=jnp.float32)
            gather(m, total, corner_scale[:, rows], corners[m][0], corners[m][1])
        for j in range(PARTS):
            help_out[j] = back[j].astype(jnp.bfloat16)
            send_help(j).start()
        for j in range(PARTS):
            send_help(j).wait_send()

    @pl.when(lent)
    def _():
        for i in range(3):
            send_block(i).wait_send()

    @pl.when(helped)
    def _():
        send_scale().wait_send()
        for m in range(PARTS):
            send_corner(m).wait_send()
            for copy in send_lent(m):
                copy.wait_send()

    @pl.when(s > 0)
    def _():
        send_rhs().wait_send()
        send_coef().wait_send()

    for k in range(CHUNKS):
        @pl.when(r < last(k))
        def _(k=k):
            for h in range(SUBS):
                send_pre(k, h).wait_send()

        @pl.when(jnp.logical_and(r > 0, r <= last(k)))
        def _(k=k):
            for h in range(SUBS):
                send_suf(k, h).wait_send()

    for i in range(PARTS):
        @pl.when(sends_y(i))
        def _(i=i):
            send_y(order(other, i)).wait_send()

        @pl.when(passes)
        def _(i=i):
            send_prev(i).wait_send()


def sweep(n_sec, n_row, n_col, forcing, inverse_factor, diag_inverse, coupling):
    share, width = forcing.shape[1:]
    block_rows, block_cols = inverse_factor.shape[2:]
    chunk, part = block_rows // CHUNKS, block_cols // PARTS
    vmem = pl.BlockSpec(memory_space=pltpu.VMEM)
    bf16, f32 = jnp.bfloat16, jnp.float32
    dma = pltpu.SemaphoreType.DMA
    return pl.pallas_call(
        functools.partial(sweep_kernel, n_sec, n_row, n_col),
        out_shape=jax.ShapeDtypeStruct(forcing.shape, f32),
        in_specs=[vmem, vmem, vmem, pl.BlockSpec(memory_space=pl.ANY)],
        out_specs=vmem,
        scratch_shapes=[
            pltpu.VMEM((2, block_rows, block_cols), bf16),
            pltpu.VMEM((block_cols, width), bf16),
            pltpu.VMEM((block_cols, width), bf16),
            pltpu.VMEM((CHUNKS, chunk, width), f32),
            pltpu.VMEM((CHUNKS, chunk, width), bf16),
            pltpu.VMEM((CHUNKS, chunk, width), bf16),
            pltpu.VMEM((CHUNKS, chunk, width), bf16),
            pltpu.VMEM((CHUNKS, chunk, width), bf16),
            pltpu.VMEM((PARTS, width, part), f32),
            pltpu.VMEM((PARTS, width, part), bf16),
            pltpu.VMEM((PARTS, width, part), bf16),
            pltpu.VMEM((PARTS, width, part), bf16),
            pltpu.VMEM((PARTS, width, part), bf16),
            pltpu.VMEM((n_col, width, share), f32),
            pltpu.VMEM((n_col, 2, share), f32),
            dma((CHUNKS,)),
            dma((2,)), dma((2,)),
            dma((CHUNKS * SUBS,)), dma((CHUNKS * SUBS,)),
            dma((CHUNKS * SUBS,)), dma((CHUNKS * SUBS,)),
            dma((PARTS,)), dma((PARTS,)),
            dma((PARTS,)), dma((PARTS,)),
            dma, dma, dma, dma,
            pltpu.SemaphoreType.REGULAR,
            *[pltpu.VMEM((2, chunk, (m + 1) * part), bf16) for m in range(PARTS)],
            pltpu.VMEM((2, HALF * chunk), f32),
            pltpu.VMEM((PARTS, width, part), bf16),
            pltpu.VMEM((PARTS, width, part), bf16),
            dma((PARTS,)), dma((PARTS,)), dma, dma,
            dma((2, PARTS)), dma((2, PARTS)), dma((PARTS,)), dma((PARTS,)), dma((2,)), dma((2,)),
        ],
        compiler_params=pltpu.CompilerParams(
            collective_id=0, has_side_effects=True, vmem_limit_bytes=60 * 2**20
        ),
    )(forcing, diag_inverse, coupling, inverse_factor)


def solution(mesh):
    placed = (
        P("sec", ("row", "col"), None),
        P("sec", None, "col", "row"),
        P("sec", None, "col"),
        P("sec", None, ("row", "col")),
    )
    n_sec, n_row, n_col = (mesh.shape[axis] for axis in ("sec", "row", "col"))

    def body(forcing, inverse_factor, diag_inverse, coupling):
        share, width = forcing.shape[1:]
        fits = inverse_factor.size * 2 <= 32 * 2**20
        block = inverse_factor.shape[2] == 4 * share and inverse_factor.shape[3] == 2 * share
        if share % 256 or width % 128 or not fits or n_sec != 4 or (n_row, n_col) != (4, 2) or not block:
            return local(forcing, inverse_factor, diag_inverse, coupling)
        return sweep(n_sec, n_row, n_col, forcing, inverse_factor, diag_inverse, coupling)

    return jax.shard_map(
        body, mesh=mesh, in_specs=placed, out_specs=P("sec", ("row", "col"), None), check_vma=False
    )
```

```python
import functools

import jax
import jax.numpy as jnp
from jax import lax
from jax.experimental import pallas as pl
from jax.experimental.pallas import tpu as pltpu
from jax.sharding import PartitionSpec as P


def shifted(value, axis, steps):
    count = lax.axis_size(axis)
    initial, last = (max(0, -steps), min(count, count - steps))
    return lax.ppermute(value, axis, [(source, source + steps) for source in range(initial, last)])


def complex_rows(coef_re, coef_im, values, half):
    v_re = values[:, :half]
    v_im = values[:, half:]
    out_re = coef_re[:, None] * v_re - coef_im[:, None] * v_im
    out_im = coef_re[:, None] * v_im + coef_im[:, None] * v_re
    return jnp.concatenate([out_re, out_im], axis=1)


def combine_stack(product):
    half = product.shape[2] // 2
    out_re = product[0, :, :half] - product[1, :, half:]
    out_im = product[0, :, half:] + product[1, :, :half]
    return jnp.concatenate([out_re, out_im], axis=1)


def solve_section(source, factor, dinv):
    width = source.shape[1]
    product = jnp.einsum(
        "kij,jb->kib",
        factor,
        lax.all_gather(source, "col", axis=0, tiled=True),
        preferred_element_type=jnp.float32,
    )
    forward = combine_stack(product)
    share = lax.psum_scatter(
        forward.astype(jnp.bfloat16), "row", scatter_dimension=0, tiled=True
    ).astype(jnp.float32)
    share_rows = share.shape[0]
    local_dinv = lax.dynamic_slice_in_dim(dinv, lax.axis_index("row") * share_rows, share_rows, 1)
    scaled = complex_rows(local_dinv[0], local_dinv[1], share, width // 2).astype(jnp.bfloat16)
    product = jnp.einsum(
        "kij,ib->kjb",
        factor,
        lax.all_gather(scaled, "row", axis=0, tiled=True),
        preferred_element_type=jnp.float32,
    )
    back = combine_stack(product)
    return lax.psum_scatter(
        back.astype(jnp.bfloat16), "col", scatter_dimension=0, tiled=True
    ).astype(jnp.float32)


def local(forcing, inverse_factor, diag_inverse, coupling):
    sections = lax.axis_size("sec")
    section_id = lax.axis_index("sec")
    local_rhs = forcing[0]
    factor = inverse_factor[0]
    dinv = diag_inverse[0]
    couple = coupling[0]
    rows_here = local_rhs.shape[0]
    half = local_rhs.shape[1] // 2
    block_count = 1
    block_width = half // block_count
    rhs_blocks = local_rhs.reshape(rows_here, 2, block_count, block_width)
    results = jnp.zeros((rows_here, 2, block_count, block_width), jnp.float32)
    outgoing = jnp.zeros((rows_here, 2 * block_width), jnp.float32)
    for step_index in range(block_count + sections - 1):
        if step_index > 0:
            incoming = shifted(outgoing.astype(jnp.bfloat16), "sec", 1).astype(outgoing.dtype)
        else:
            incoming = jnp.zeros((rows_here, 2 * block_width), jnp.float32)
        block_index = step_index - section_id
        active = jnp.logical_and(block_index >= 0, block_index < block_count)
        safe_index = jnp.clip(block_index, 0, block_count - 1)
        current = lax.dynamic_index_in_dim(rhs_blocks, safe_index, 2, keepdims=False)
        current = current.reshape(rows_here, 2 * block_width)
        source = (current - complex_rows(couple[0], couple[1], incoming, block_width)).astype(
            jnp.bfloat16
        )
        field = solve_section(source, factor, dinv)
        updated = lax.dynamic_update_index_in_dim(
            results, field.reshape(rows_here, 2, block_width), safe_index, 2
        )
        results = jnp.where(active, updated, results)
        outgoing = field
    return results.reshape(1, rows_here, 2 * half)


MESH = pl.DeviceIdType.MESH

CHUNKS = 8
SUBS = 2
HALF = CHUNKS // 2
PARTS = 4
EARLY = 2
BEGUN = 6
LENT = 6
PLANS = {
    (1, 0, 0): (
        0o40, 0o41, 0o42, 0o43, 0o04, 0o05, 0o06, 0o07, 0o00, 0o01, 0o02, 0o03, 0o30, 0o31, 0o34,
        0o32, 0o35, 0o36, 0o37, 0o33,
    ),
    (1, 1, 0): (
        0o40, 0o41, 0o42, 0o43, 0o04, 0o05, 0o00, 0o20, 0o01, 0o14, 0o21, 0o15, 0o06, 0o24, 0o16,
        0o07, 0o17, 0o02, 0o22, 0o25, 0o10, 0o26, 0o11, 0o03, 0o27, 0o12, 0o34, 0o23, 0o13, 0o35,
        0o30, 0o36, 0o31, 0o37, 0o32, 0o33,
    ),
    (1, 2, 0): (
        0o40, 0o41, 0o42, 0o43, 0o00, 0o04, 0o01, 0o05, 0o24, 0o02, 0o25, 0o06, 0o26, 0o07, 0o27,
        0o03, 0o14, 0o15, 0o34, 0o16, 0o35, 0o17, 0o36, 0o37, 0o30, 0o31, 0o32, 0o33,
    ),
    (1, 3, 0): (
        0o40, 0o41, 0o42, 0o43, 0o04, 0o05, 0o06, 0o07, 0o34, 0o35, 0o36, 0o37,
    ),
    (1, 0, 2): (
        0o40, 0o41, 0o42, 0o43, 0o04, 0o05, 0o00, 0o76, 0o77, 0o01, 0o02, 0o03, 0o30, 0o34, 0o31,
        0o35, 0o32, 0o36, 0o33, 0o37,
    ),
    (1, 1, 2): (
        0o40, 0o41, 0o42, 0o43, 0o04, 0o05, 0o00, 0o20, 0o01, 0o14, 0o76, 0o77, 0o21, 0o15, 0o02,
        0o24, 0o10, 0o16, 0o22, 0o03, 0o25, 0o17, 0o23, 0o11, 0o34, 0o26, 0o30, 0o12, 0o27, 0o35,
        0o13, 0o31, 0o36, 0o32, 0o37, 0o33,
    ),
    (1, 2, 2): (
        0o40, 0o41, 0o42, 0o43, 0o00, 0o04, 0o01, 0o05, 0o24, 0o76, 0o02, 0o25, 0o77, 0o03, 0o26,
        0o27, 0o14, 0o34, 0o15, 0o35, 0o16, 0o36, 0o17, 0o37, 0o30, 0o31, 0o32, 0o33,
    ),
    (0, 0, 0): (
        0o40, 0o00, 0o41, 0o01, 0o42, 0o02, 0o43, 0o04, 0o05, 0o06, 0o07, 0o03, 0o34, 0o35, 0o36,
        0o37, 0o30, 0o31, 0o32, 0o33,
    ),
    (0, 0, 1): (
        0o40, 0o41, 0o54, 0o55, 0o42, 0o56, 0o57, 0o43, 0o64, 0o65, 0o66, 0o67, 0o34, 0o35, 0o36,
        0o37,
    ),
    (0, 1, 0): (
        0o40, 0o04, 0o41, 0o05, 0o42, 0o06, 0o43, 0o07, 0o34, 0o35, 0o36, 0o37,
    ),
}
PER_WORD = 3
ACTIONS = [("F", m) for m in range(PARTS + 1)] + [("R",), ("L",), ("S",), ("G",), ("H",), ("W",)] + [("B", True, True), ("B", False, True)]
ACTIONS += [("B", left, False, m) for left in (True, False) for m in range(PARTS)]


def plan_words(col, row, plan):
    codes = []
    for step in plan:
        kind, k = "FRLBSGHW"[step // CHUNKS], step % CHUNKS
        end = 2 * col + k // HALF
        if kind == "F":
            action = ("F", k % HALF if row == end else PARTS)
        elif kind == "B":
            action = ("B", row > 0, row < end)
            action += () if row < end else (k % HALF,)
        else:
            action = (kind,)
        codes.append(ACTIONS.index(action) * CHUNKS + k)
    words = []
    for i in range(0, len(codes), PER_WORD):
        words.append(sum(code * 256**j for j, code in enumerate(codes[i : i + PER_WORD])))
    return len(codes), words


def sweep_kernel(
    n_sec, n_row, n_col, forcing, dinv, coupling, factor_hbm, out,
    factor, src_a, src_b, own, pre_in, suf_in, pre_out, suf_out,
    back, y_out, y_in, prev_out, prev_in, forcing_t, coupling_all,
    load_sem, src_send, src_recv, pre_send, pre_recv, suf_send, suf_recv,
    y_send, y_recv, prev_send, prev_recv,
    rhs_send, rhs_recv, coef_send, coef_recv, go,
    corner_0, corner_1, corner_2, corner_3, corner_scale, help_out, help_in,
    corner_send, corner_recv, scale_send, scale_recv, lent_send, lent_recv, help_send, help_recv, lend_send, lend_recv,
    direct_in, direct_send, direct_recv,
):
    corners = (corner_0, corner_1, corner_2, corner_3)
    chunk = own.shape[1]
    half = own.shape[2] // 2
    share = forcing_t.shape[2]
    part = back.shape[2]
    s, r, c = lax.axis_index("sec"), lax.axis_index("row"), lax.axis_index("col")
    other = 1 - c
    ends = s == n_sec - 1
    active = r <= 2 * c + 1
    paired = r < 2
    corner = jnp.logical_and(r == 0, c == 0)
    helped = jnp.logical_and(corner, lax.rem(s, 2) == 1)
    helper = jnp.logical_and(corner, lax.rem(s, 2) == 0)
    inner = jnp.logical_and(c == 1, r < n_row - 1)
    lent = jnp.logical_and(inner, s > 0)
    lends = jnp.logical_and(inner, s != 1)
    needed = jnp.logical_or(paired, c == 0)

    def last(k):
        return 2 * c + k // HALF

    def chunk_rows(k):
        return pl.ds(pl.multiple_of(k * chunk, chunk), chunk)

    def load(k):
        rows = chunk_rows(k)
        return pltpu.make_async_copy(
            factor_hbm.at[0, :, rows, :], factor.at[:, rows, :], load_sem.at[k]
        )

    def half_rows(col):
        return pl.ds(pl.multiple_of(col * share, share), share)

    def remote(src, dst, send_sem, recv_sem, device):
        return pltpu.make_async_remote_copy(
            src_ref=src, dst_ref=dst, send_sem=send_sem, recv_sem=recv_sem,
            device_id=device, device_id_type=MESH,
        )

    across = (s, r, other)
    after = (lax.rem(s + 1, n_sec), r, c)

    def part_rows(j):
        return pl.ds(pl.multiple_of(j * part, part), part)

    def send_source(j):
        rows = part_rows(j)
        at = lax.rem(j, 2)
        return remote(src_a.at[rows], src_a.at[rows], src_send.at[at], src_recv.at[at], across)

    before = (lax.rem(s + n_sec - 1, n_sec), r, c)

    partner = (s + 1 - 2 * lax.rem(s, 2), r, c)

    def send_block(i):
        k, m, first, stop = ((LENT, 3, 0, 4), (LENT + 1, 2, 0, 3), (LENT + 1, 0, 3, 4))[i]
        rows, cols = slice(k * chunk, (k + 1) * chunk), slice(first * part, stop * part)
        return remote(
            factor_hbm.at[0, :, rows, cols], corners[m], corner_send.at[m], corner_recv.at[m], partner
        )

    def send_lend(k):
        at = k - LENT
        return remote(own.at[k], own.at[k], lend_send.at[at], lend_recv.at[at], partner)

    def send_corner(m):
        rows, cols = slice(m * chunk, (m + 1) * chunk), slice(0, (m + 1) * part)
        return remote(
            factor_hbm.at[0, :, rows, cols], corners[m], corner_send.at[m], corner_recv.at[m], before
        )

    def send_scale():
        scales = dinv.at[0, :, slice(0, HALF * chunk)]
        return remote(scales, corner_scale, scale_send, scale_recv, before)

    def send_lent(j):
        rows = part_rows(j)
        return [
            remote(held.at[rows], held.at[rows], lent_send.at[i, j], lent_recv.at[i, j], partner)
            for i, held in enumerate((src_a, src_b))
        ]

    def send_help(j):
        return remote(help_out.at[j], help_in.at[j], help_send.at[j], help_recv.at[j], after)

    def send_rhs():
        return remote(forcing_t.at[c], forcing_t.at[c], rhs_send, rhs_recv, across)

    def send_coef():
        return remote(coupling_all.at[c], coupling_all.at[c], coef_send, coef_recv, across)

    def send_pre(k, h):
        rows = pl.ds(h * (chunk // SUBS), chunk // SUBS)
        at = k * SUBS + h
        return remote(
            pre_out.at[k, rows], pre_in.at[k, rows], pre_send.at[at], pre_recv.at[at],
            (s, lax.rem(r + 1, n_row), c),
        )

    def send_suf(k, h):
        rows = pl.ds(h * (chunk // SUBS), chunk // SUBS)
        at = k * SUBS + h
        return remote(
            suf_out.at[k, rows], suf_in.at[k, rows], suf_send.at[at], suf_recv.at[at],
            (s, lax.rem(r + n_row - 1, n_row), c),
        )

    def send_y(j):
        return remote(y_out.at[j], y_in.at[j], y_send.at[j], y_recv.at[j], across)

    beyond = (lax.rem(s + 1, n_sec), r, other)
    even = lax.rem(s, 2) == 0
    direct = jnp.logical_and(jnp.logical_and(paired, even), c == 1)
    split = jnp.logical_and(jnp.logical_and(paired, even), c == 0)
    summed = jnp.logical_and(jnp.logical_and(paired, jnp.logical_not(even)), c == 0)

    def send_direct(j):
        return remote(
            y_out.at[j], direct_in.at[j], direct_send.at[j], direct_recv.at[j], beyond
        )

    def send_prev(j):
        return remote(prev_out.at[j], prev_in.at[j], prev_send.at[j], prev_recv.at[j], after)

    count = jnp.int32(0)
    packed = {place: plan_words(*place[:2], plan) for place, plan in PLANS.items()}
    words = [jnp.int32(0)] * max(len(held) for _, held in packed.values())
    for (col, row, where), (length, held) in packed.items():
        mine = jnp.logical_and(c == col, r == row)
        if where:
            mine = jnp.logical_and(mine, lax.rem(s, 2) == 1 if where == 1 else s > 0)
        count = jnp.where(mine, length, count)
        for i, word in enumerate(held):
            words[i] = jnp.where(mine, word, words[i])

    for i in range(CHUNKS):
        k = (i + HALF) % CHUNKS

        @pl.when(jnp.logical_and(r <= last(k), jnp.logical_not(helped)) if k < HALF else r <= last(k))
        def _(k=k):
            load(k).start()

    barrier = pltpu.get_barrier_semaphore()
    for device in (
        (s, lax.rem(r + 1, n_row), c), (s, lax.rem(r + n_row - 1, n_row), c), across,
        after, before, beyond, (lax.rem(s + n_sec - 1, n_sec), r, other),
    ):
        pl.semaphore_signal(barrier, 1, device_id=device, device_id_type=MESH)

    def turned(value):
        return jnp.concatenate([-value[:, half:], value[:, :half]], axis=1)

    def product(k, cols):
        rows = chunk_rows(k)
        total = jnp.dot(factor[0, rows, cols], src_a[cols, :], preferred_element_type=jnp.float32)
        return total + jnp.dot(
            factor[1, rows, cols], src_b[cols, :], preferred_element_type=jnp.float32
        )

    def begin(first, stop):
        @pl.loop(first, stop)
        def _(i):
            k = lax.rem(i + HALF, CHUNKS)

            @pl.when(r < last(k))
            def _():
                load(k).wait()
                own[k] = product(k, half_rows(c))

    back[...] = jnp.zeros_like(back)

    @pl.when(s == 0)
    def _():
        src_a[half_rows(c), :] = forcing[0].astype(jnp.bfloat16)
        src_b[half_rows(c), :] = turned(forcing[0].astype(jnp.bfloat16).astype(jnp.float32)).astype(
            jnp.bfloat16
        )
        begin(0, EARLY)

    @pl.when(s > 0)
    def _():
        forcing_t[c] = forcing[0].T
        coupling_all[c] = coupling[0]

    pl.semaphore_wait(barrier, 7)

    @pl.when(s == 0)
    def _():
        @pl.when(needed)
        def _():
            for i in range(2):
                send_source(2 * c + i).start()

        begin(EARLY, BEGUN)
        pl.semaphore_signal(go, 1, device_id=after, device_id_type=MESH)

    @pl.when(helped)
    def _():
        send_scale().start()
        for m in range(PARTS):
            send_corner(m).start()

    @pl.when(lent)
    def _():
        for i in range(3):
            send_block(i).start()

    @pl.when(s == 1)
    def _():
        pl.semaphore_wait(go, 1)

    @pl.when(s > 0)
    def _():
        send_rhs().start()
        send_coef().start()
        send_rhs().wait_recv()
        send_coef().wait_recv()

    def enter(j, previous):
        rows = part_rows(j)
        col, cols = j // 2, part_rows(lax.rem(j, 2))
        p_re, p_im = previous[:half], previous[half:]
        c_re, c_im = coupling_all[col, 0:1, cols], coupling_all[col, 1:2, cols]
        new_re = forcing_t[col, :half, cols] - (c_re * p_re - c_im * p_im)
        new_im = forcing_t[col, half:, cols] - (c_re * p_im + c_im * p_re)
        src_a[rows, :] = jnp.concatenate([new_re, new_im], axis=0).T.astype(jnp.bfloat16)
        src_b[rows, :] = jnp.concatenate([-new_im, new_re], axis=0).T.astype(jnp.bfloat16)

    def source_step(j):
        rows = part_rows(j)

        @pl.when(jnp.logical_and(s == 0, j // 2 != c))
        def _():
            send_source(j).wait_recv()
            src_b[rows, :] = turned(src_a[rows, :].astype(jnp.float32)).astype(jnp.bfloat16)

        @pl.when(s > 0)
        def _():
            send_prev(j).wait_recv()

            @pl.when(summed)
            def _():
                send_direct(j).wait_recv()
                enter(j, prev_in[j].astype(jnp.float32) + direct_in[j].astype(jnp.float32))

            @pl.when(jnp.logical_not(summed))
            def _():
                enter(j, prev_in[j].astype(jnp.float32))

            @pl.when(jnp.logical_or(helped, lent))
            def _():
                for copy in send_lent(j):
                    copy.start()

    def keep(k, total):
        own[k] = total
        pre_out[k] = total.astype(jnp.bfloat16)
        suf_out[k] = total.astype(jnp.bfloat16)

    def forward_full(k):
        begun = jnp.logical_and(s == 0, lax.rem(k + HALF, CHUNKS) < BEGUN)

        @pl.when(begun)
        def _():
            keep(k, own[k] + product(k, half_rows(other)))

        @pl.when(jnp.logical_not(begun))
        def _():
            load(k).wait()
            keep(k, product(k, slice(0, PARTS * part)))

        @pl.when(r == 0)
        def _():
            for h in range(SUBS):
                send_pre(k, h).start()

    def forward_first(k):
        load(k).wait()
        own[k] = product(k, slice(0, 2 * part))

    def forward_second(k):
        keep(k, own[k] + product(k, slice(2 * part, 4 * part)))
        for h in range(SUBS):
            send_pre(k, h).start()

    def forward_lent(k):
        load(k).wait()
        send_lend(k).wait_recv()
        pre_out[k] = own[k].astype(jnp.bfloat16)
        suf_out[k] = own[k].astype(jnp.bfloat16)

        @pl.when(r == 0)
        def _():
            for h in range(SUBS):
                send_pre(k, h).start()

    def forward_diagonal(m, k):
        load(k).wait()
        keep(k, product(k, slice(0, (m + 1) * part)))

        @pl.when(r > 0)
        def _():
            for h in range(SUBS):
                send_suf(k, h).start()

    def relay(send, held, came, k):
        for h in range(SUBS):
            rows = slice(h * (chunk // SUBS), (h + 1) * (chunk // SUBS))
            send(k, h).wait_recv()
            held[k, rows, :] += came[k, rows, :]
            send(k, h).start()

    def relay_right(k):
        relay(send_pre, pre_out, pre_in, k)

    def relay_left(k):
        relay(send_suf, suf_out, suf_in, k)

    def gather(m, total, scale, block_re, block_im):
        forward = total.T
        d_re, d_im = scale[0:1], scale[1:2]
        f_re, f_im = forward[:half], forward[half:]
        s_re, s_im = d_re * f_re - d_im * f_im, d_re * f_im + d_im * f_re
        lhs_a = jnp.concatenate([s_re, s_im], axis=0).astype(jnp.bfloat16)
        lhs_b = jnp.concatenate([-s_im, s_re], axis=0).astype(jnp.bfloat16)
        total = jnp.dot(lhs_a, block_re, preferred_element_type=jnp.float32)
        total += jnp.dot(lhs_b, block_im, preferred_element_type=jnp.float32)
        for j in range(m + 1):
            back[j] += total[:, j * part : (j + 1) * part]

    def back_step(left, right, m, k):
        rows = chunk_rows(k)
        total = own[k]
        if left != right:
            for h in range(SUBS):
                (send_pre if left else send_suf)(k, h).wait_recv()
        if left:
            total += pre_in[k].astype(jnp.float32)
        if right:
            total += suf_in[k].astype(jnp.float32)
        cols = slice(0, (m + 1) * part)
        gather(m, total, dinv[0, :, rows], factor[0, rows, cols], factor[1, rows, cols])

    def act(action, k):
        kind = action[0]
        if kind == "F":
            if action[1] == PARTS:
                forward_full(k)
            else:
                forward_diagonal(action[1], k)
        elif kind == "B":
            back_step(action[1], action[2], action[3] if len(action) > 3 else PARTS - 1, k)
        else:
            {
                "R": relay_right, "L": relay_left, "S": source_step,
                "G": forward_first, "H": forward_second, "W": forward_lent,
            }[kind](k)

    def dispatch(step, first, stop, k):
        if stop - first == 1:
            act(ACTIONS[first], k)
            return
        middle = (first + stop) // 2

        @pl.when(step < middle)
        def _():
            dispatch(step, first, middle, k)

        @pl.when(step >= middle)
        def _():
            dispatch(step, middle, stop, k)

    def lend():
        for j in range(PARTS):
            for copy in send_lent(j):
                copy.wait_recv()
        send_block(0).wait_recv()
        total = jnp.dot(corners[3][0], src_a[...], preferred_element_type=jnp.float32)
        total += jnp.dot(corners[3][1], src_b[...], preferred_element_type=jnp.float32)
        own[LENT] = total
        send_lend(LENT).start()
        send_block(1).wait_recv()
        send_block(2).wait_recv()
        total = jnp.zeros((chunk, 2 * half), jnp.float32)
        for m, cols in ((2, slice(0, 3 * part)), (0, slice(3 * part, 4 * part))):
            total += jnp.dot(corners[m][0], src_a[cols, :], preferred_element_type=jnp.float32)
            total += jnp.dot(corners[m][1], src_b[cols, :], preferred_element_type=jnp.float32)
        own[LENT + 1] = total
        send_lend(LENT + 1).start()
        for k in (LENT, LENT + 1):
            send_lend(k).wait_send()

    @pl.when(jnp.logical_and(lends, ends))
    def _():
        lend()

    @pl.loop(0, count)
    def _(e):
        at = e // PER_WORD
        word = words[0]
        for i in range(1, len(words)):
            word = jnp.where(at == i, words[i], word)
        code = lax.rem(lax.shift_right_logical(word, 8 * lax.rem(e, PER_WORD)), 256)
        dispatch(code // CHUNKS, 0, len(ACTIONS), lax.rem(code, CHUNKS))

    @pl.when(helped)
    def _():
        for j in range(PARTS):
            send_help(j).wait_recv()
            back[j] += help_in[j].astype(jnp.float32)

    @pl.when(jnp.logical_and(s == 0, needed))
    def _():
        for i in range(2):
            send_source(2 * c + i).wait_send()

    @pl.when(lent)
    def _():
        for j in range(PARTS):
            for copy in send_lent(j):
                copy.wait_send()

    def order(first, i):
        return (2 * first + i) % PARTS if isinstance(first, int) else lax.rem(2 * first + i, PARTS)

    def sends_y(i):
        wanted = jnp.logical_or(paired, c == 1) if i < 2 else paired
        return wanted if i < 2 else jnp.logical_and(wanted, jnp.logical_not(ends))

    def takes_y(i):
        wanted = jnp.logical_or(paired, c == 0) if i < 2 else jnp.logical_and(paired, jnp.logical_not(split))
        return wanted if i < 2 else jnp.logical_and(wanted, jnp.logical_not(ends))

    for i in range(PARTS):
        j = order(other, i)

        @pl.when(sends_y(i))
        def _(j=j):
            y_out[j] = back[j].astype(jnp.bfloat16)

            @pl.when(direct)
            def _():
                send_direct(j).start()

            @pl.when(jnp.logical_not(direct))
            def _():
                send_y(j).start()

    @pl.when(direct)
    def _():
        for i in range(2):
            send_y(order(other, i)).start()

    @pl.when(split)
    def _():
        for j in range(PARTS):
            prev_out[j] = back[j].astype(jnp.bfloat16)
            send_prev(j).start()

    passes = jnp.logical_and(active, jnp.logical_not(ends))
    for i in range(PARTS):
        j = order(c, i)

        @pl.when(takes_y(i))
        def _(j=j):
            send_y(j).wait_recv()
            back[j] += y_in[j].astype(jnp.float32)

        @pl.when(jnp.logical_and(passes, jnp.logical_not(split)))
        def _(j=j):
            prev_out[j] = back[j].astype(jnp.bfloat16)
            send_prev(j).start()

    for i in range(2):
        out[0, i * part : (i + 1) * part, :] = back[order(c, i)].T

    @pl.when(jnp.logical_and(lends, jnp.logical_not(ends)))
    def _():
        lend()

    @pl.when(helper)
    def _():
        back[...] = jnp.zeros_like(back)
        send_scale().wait_recv()
        for m in range(PARTS):
            send_corner(m).wait_recv()
            for copy in send_lent(m):
                copy.wait_recv()
            rows, cols = slice(m * chunk, (m + 1) * chunk), slice(0, (m + 1) * part)
            total = jnp.dot(corners[m][0], src_a[cols, :], preferred_element_type=jnp.float32)
            total += jnp.dot(corners[m][1], src_b[cols, :], preferred_element_type=jnp.float32)
            gather(m, total, corner_scale[:, rows], corners[m][0], corners[m][1])
        for j in range(PARTS):
            help_out[j] = back[j].astype(jnp.bfloat16)
            send_help(j).start()
        for j in range(PARTS):
            send_help(j).wait_send()

    @pl.when(lent)
    def _():
        for i in range(3):
            send_block(i).wait_send()

    @pl.when(helped)
    def _():
        send_scale().wait_send()
        for m in range(PARTS):
            send_corner(m).wait_send()
            for copy in send_lent(m):
                copy.wait_send()

    @pl.when(s > 0)
    def _():
        send_rhs().wait_send()
        send_coef().wait_send()

    for k in range(CHUNKS):
        @pl.when(r < last(k))
        def _(k=k):
            for h in range(SUBS):
                send_pre(k, h).wait_send()

        @pl.when(jnp.logical_and(r > 0, r <= last(k)))
        def _(k=k):
            for h in range(SUBS):
                send_suf(k, h).wait_send()

    for i in range(PARTS):
        @pl.when(direct)
        def _(i=i):
            send_direct(i).wait_send()

        @pl.when(jnp.logical_and(sends_y(i), jnp.logical_or(i < 2, jnp.logical_not(direct))))
        def _(i=i):
            send_y(order(other, i)).wait_send()

        @pl.when(passes)
        def _(i=i):
            send_prev(i).wait_send()


def sweep(n_sec, n_row, n_col, forcing, inverse_factor, diag_inverse, coupling):
    share, width = forcing.shape[1:]
    block_rows, block_cols = inverse_factor.shape[2:]
    chunk, part = block_rows // CHUNKS, block_cols // PARTS
    vmem = pl.BlockSpec(memory_space=pltpu.VMEM)
    bf16, f32 = jnp.bfloat16, jnp.float32
    dma = pltpu.SemaphoreType.DMA
    return pl.pallas_call(
        functools.partial(sweep_kernel, n_sec, n_row, n_col),
        out_shape=jax.ShapeDtypeStruct(forcing.shape, f32),
        in_specs=[vmem, vmem, vmem, pl.BlockSpec(memory_space=pl.ANY)],
        out_specs=vmem,
        scratch_shapes=[
            pltpu.VMEM((2, block_rows, block_cols), bf16),
            pltpu.VMEM((block_cols, width), bf16),
            pltpu.VMEM((block_cols, width), bf16),
            pltpu.VMEM((CHUNKS, chunk, width), f32),
            pltpu.VMEM((CHUNKS, chunk, width), bf16),
            pltpu.VMEM((CHUNKS, chunk, width), bf16),
            pltpu.VMEM((CHUNKS, chunk, width), bf16),
            pltpu.VMEM((CHUNKS, chunk, width), bf16),
            pltpu.VMEM((PARTS, width, part), f32),
            pltpu.VMEM((PARTS, width, part), bf16),
            pltpu.VMEM((PARTS, width, part), bf16),
            pltpu.VMEM((PARTS, width, part), bf16),
            pltpu.VMEM((PARTS, width, part), bf16),
            pltpu.VMEM((n_col, width, share), f32),
            pltpu.VMEM((n_col, 2, share), f32),
            dma((CHUNKS,)),
            dma((2,)), dma((2,)),
            dma((CHUNKS * SUBS,)), dma((CHUNKS * SUBS,)),
            dma((CHUNKS * SUBS,)), dma((CHUNKS * SUBS,)),
            dma((PARTS,)), dma((PARTS,)),
            dma((PARTS,)), dma((PARTS,)),
            dma, dma, dma, dma,
            pltpu.SemaphoreType.REGULAR,
            *[pltpu.VMEM((2, chunk, (m + 1) * part), bf16) for m in range(PARTS)],
            pltpu.VMEM((2, HALF * chunk), f32),
            pltpu.VMEM((PARTS, width, part), bf16),
            pltpu.VMEM((PARTS, width, part), bf16),
            dma((PARTS,)), dma((PARTS,)), dma, dma,
            dma((2, PARTS)), dma((2, PARTS)), dma((PARTS,)), dma((PARTS,)), dma((2,)), dma((2,)),
            pltpu.VMEM((PARTS, width, part), bf16), dma((PARTS,)), dma((PARTS,)),
        ],
        compiler_params=pltpu.CompilerParams(
            collective_id=0, has_side_effects=True, vmem_limit_bytes=60 * 2**20
        ),
    )(forcing, diag_inverse, coupling, inverse_factor)


def solution(mesh):
    placed = (
        P("sec", ("row", "col"), None),
        P("sec", None, "col", "row"),
        P("sec", None, "col"),
        P("sec", None, ("row", "col")),
    )
    n_sec, n_row, n_col = (mesh.shape[axis] for axis in ("sec", "row", "col"))

    def body(forcing, inverse_factor, diag_inverse, coupling):
        share, width = forcing.shape[1:]
        fits = inverse_factor.size * 2 <= 32 * 2**20
        block = inverse_factor.shape[2] == 4 * share and inverse_factor.shape[3] == 2 * share
        if share % 256 or width % 128 or not fits or n_sec != 4 or (n_row, n_col) != (4, 2) or not block:
            return local(forcing, inverse_factor, diag_inverse, coupling)
        return sweep(n_sec, n_row, n_col, forcing, inverse_factor, diag_inverse, coupling)

    return jax.shard_map(
        body, mesh=mesh, in_specs=placed, out_specs=P("sec", ("row", "col"), None), check_vma=False
    )
```

```python
import functools

import jax
import jax.numpy as jnp
from jax import lax
from jax.experimental import pallas as pl
from jax.experimental.pallas import tpu as pltpu
from jax.sharding import PartitionSpec as P


def shifted(value, axis, steps):
    count = lax.axis_size(axis)
    initial, last = (max(0, -steps), min(count, count - steps))
    return lax.ppermute(value, axis, [(source, source + steps) for source in range(initial, last)])


def complex_rows(coef_re, coef_im, values, half):
    v_re = values[:, :half]
    v_im = values[:, half:]
    out_re = coef_re[:, None] * v_re - coef_im[:, None] * v_im
    out_im = coef_re[:, None] * v_im + coef_im[:, None] * v_re
    return jnp.concatenate([out_re, out_im], axis=1)


def combine_stack(product):
    half = product.shape[2] // 2
    out_re = product[0, :, :half] - product[1, :, half:]
    out_im = product[0, :, half:] + product[1, :, :half]
    return jnp.concatenate([out_re, out_im], axis=1)


def solve_section(source, factor, dinv):
    width = source.shape[1]
    product = jnp.einsum(
        "kij,jb->kib",
        factor,
        lax.all_gather(source, "col", axis=0, tiled=True),
        preferred_element_type=jnp.float32,
    )
    forward = combine_stack(product)
    share = lax.psum_scatter(
        forward.astype(jnp.bfloat16), "row", scatter_dimension=0, tiled=True
    ).astype(jnp.float32)
    share_rows = share.shape[0]
    local_dinv = lax.dynamic_slice_in_dim(dinv, lax.axis_index("row") * share_rows, share_rows, 1)
    scaled = complex_rows(local_dinv[0], local_dinv[1], share, width // 2).astype(jnp.bfloat16)
    product = jnp.einsum(
        "kij,ib->kjb",
        factor,
        lax.all_gather(scaled, "row", axis=0, tiled=True),
        preferred_element_type=jnp.float32,
    )
    back = combine_stack(product)
    return lax.psum_scatter(
        back.astype(jnp.bfloat16), "col", scatter_dimension=0, tiled=True
    ).astype(jnp.float32)


def local(forcing, inverse_factor, diag_inverse, coupling):
    sections = lax.axis_size("sec")
    section_id = lax.axis_index("sec")
    local_rhs = forcing[0]
    factor = inverse_factor[0]
    dinv = diag_inverse[0]
    couple = coupling[0]
    rows_here = local_rhs.shape[0]
    half = local_rhs.shape[1] // 2
    block_count = 1
    block_width = half // block_count
    rhs_blocks = local_rhs.reshape(rows_here, 2, block_count, block_width)
    results = jnp.zeros((rows_here, 2, block_count, block_width), jnp.float32)
    outgoing = jnp.zeros((rows_here, 2 * block_width), jnp.float32)
    for step_index in range(block_count + sections - 1):
        if step_index > 0:
            incoming = shifted(outgoing.astype(jnp.bfloat16), "sec", 1).astype(outgoing.dtype)
        else:
            incoming = jnp.zeros((rows_here, 2 * block_width), jnp.float32)
        block_index = step_index - section_id
        active = jnp.logical_and(block_index >= 0, block_index < block_count)
        safe_index = jnp.clip(block_index, 0, block_count - 1)
        current = lax.dynamic_index_in_dim(rhs_blocks, safe_index, 2, keepdims=False)
        current = current.reshape(rows_here, 2 * block_width)
        source = (current - complex_rows(couple[0], couple[1], incoming, block_width)).astype(
            jnp.bfloat16
        )
        field = solve_section(source, factor, dinv)
        updated = lax.dynamic_update_index_in_dim(
            results, field.reshape(rows_here, 2, block_width), safe_index, 2
        )
        results = jnp.where(active, updated, results)
        outgoing = field
    return results.reshape(1, rows_here, 2 * half)


MESH = pl.DeviceIdType.MESH

CHUNKS = 8
SUBS = 2
HALF = CHUNKS // 2
PARTS = 4
EARLY = 2
BEGUN = 6
LENT = 6
PLANS = {
    (1, 0, 0): (
        0o40, 0o41, 0o42, 0o43, 0o04, 0o05, 0o06, 0o07, 0o00, 0o01, 0o02, 0o03, 0o30, 0o31, 0o34,
        0o32, 0o35, 0o36, 0o37, 0o33,
    ),
    (1, 1, 0): (
        0o40, 0o41, 0o42, 0o43, 0o04, 0o05, 0o00, 0o20, 0o01, 0o14, 0o21, 0o15, 0o06, 0o24, 0o16,
        0o07, 0o17, 0o02, 0o22, 0o25, 0o10, 0o26, 0o11, 0o03, 0o27, 0o12, 0o34, 0o23, 0o13, 0o35,
        0o30, 0o36, 0o31, 0o37, 0o32, 0o33,
    ),
    (1, 2, 0): (
        0o40, 0o41, 0o42, 0o43, 0o00, 0o04, 0o01, 0o05, 0o24, 0o02, 0o25, 0o06, 0o26, 0o07, 0o27,
        0o03, 0o14, 0o15, 0o34, 0o16, 0o35, 0o17, 0o36, 0o37, 0o30, 0o31, 0o32, 0o33,
    ),
    (1, 3, 0): (
        0o40, 0o41, 0o42, 0o43, 0o04, 0o05, 0o06, 0o07, 0o34, 0o35, 0o36, 0o37,
    ),
    (1, 0, 2): (
        0o40, 0o41, 0o42, 0o43, 0o04, 0o05, 0o00, 0o76, 0o77, 0o01, 0o02, 0o03, 0o30, 0o34, 0o31,
        0o35, 0o32, 0o36, 0o33, 0o37,
    ),
    (1, 1, 2): (
        0o40, 0o41, 0o42, 0o43, 0o04, 0o05, 0o00, 0o20, 0o01, 0o14, 0o76, 0o77, 0o21, 0o15, 0o02,
        0o24, 0o10, 0o16, 0o22, 0o03, 0o25, 0o17, 0o23, 0o11, 0o34, 0o26, 0o30, 0o12, 0o27, 0o35,
        0o13, 0o31, 0o36, 0o32, 0o37, 0o33,
    ),
    (1, 2, 2): (
        0o40, 0o41, 0o42, 0o43, 0o00, 0o04, 0o01, 0o05, 0o24, 0o76, 0o02, 0o25, 0o77, 0o03, 0o26,
        0o27, 0o14, 0o34, 0o15, 0o35, 0o16, 0o36, 0o17, 0o37, 0o30, 0o31, 0o32, 0o33,
    ),
    (0, 0, 0): (
        0o40, 0o00, 0o41, 0o01, 0o42, 0o02, 0o43, 0o04, 0o05, 0o06, 0o07, 0o03, 0o34, 0o35, 0o36,
        0o37, 0o30, 0o31, 0o32, 0o33,
    ),
    (0, 0, 1): (
        0o40, 0o41, 0o54, 0o55, 0o42, 0o56, 0o57, 0o43, 0o64, 0o65, 0o66, 0o67, 0o34, 0o35, 0o36,
        0o37,
    ),
    (0, 1, 0): (
        0o40, 0o04, 0o41, 0o05, 0o42, 0o06, 0o43, 0o07, 0o34, 0o35, 0o36, 0o37,
    ),
}
PER_WORD = 3
ACTIONS = [("F", m) for m in range(PARTS + 1)] + [("R",), ("L",), ("S",), ("G",), ("H",), ("W",)] + [("B", True, True), ("B", False, True)]
ACTIONS += [("B", left, False, m) for left in (True, False) for m in range(PARTS)]


def plan_words(col, row, plan):
    codes = []
    for step in plan:
        kind, k = "FRLBSGHW"[step // CHUNKS], step % CHUNKS
        end = 2 * col + k // HALF
        if kind == "F":
            action = ("F", k % HALF if row == end else PARTS)
        elif kind == "B":
            action = ("B", row > 0, row < end)
            action += () if row < end else (k % HALF,)
        else:
            action = (kind,)
        codes.append(ACTIONS.index(action) * CHUNKS + k)
    words = []
    for i in range(0, len(codes), PER_WORD):
        words.append(sum(code * 256**j for j, code in enumerate(codes[i : i + PER_WORD])))
    return len(codes), words


def sweep_kernel(
    n_sec, n_row, n_col, forcing, dinv, coupling, factor_hbm, out,
    factor, src_a, src_b, own, pre_in, suf_in, pre_out, suf_out,
    back, y_out, y_in, prev_out, prev_in, forcing_t, coupling_all,
    load_sem, src_send, src_recv, pre_send, pre_recv, suf_send, suf_recv,
    y_send, y_recv, prev_send, prev_recv,
    rhs_send, rhs_recv, coef_send, coef_recv, go,
    corner_0, corner_1, corner_2, corner_3, corner_scale, help_out, help_in,
    corner_send, corner_recv, scale_send, scale_recv, lent_send, lent_recv, help_send, help_recv, lend_send, lend_recv,
    direct_in, direct_send, direct_recv,
):
    corners = (corner_0, corner_1, corner_2, corner_3)
    chunk = own.shape[1]
    half = own.shape[2] // 2
    share = forcing_t.shape[2]
    part = back.shape[2]
    s, r, c = lax.axis_index("sec"), lax.axis_index("row"), lax.axis_index("col")
    other = 1 - c
    ends = s == n_sec - 1
    active = r <= 2 * c + 1
    paired = r < 2
    corner = jnp.logical_and(r == 0, c == 0)
    helped = jnp.logical_and(corner, lax.rem(s, 2) == 1)
    helper = jnp.logical_and(corner, lax.rem(s, 2) == 0)
    inner = jnp.logical_and(c == 1, r < n_row - 1)
    lent = jnp.logical_and(inner, s > 0)
    lends = jnp.logical_and(inner, s != 1)
    needed = jnp.logical_or(paired, c == 0)

    def last(k):
        return 2 * c + k // HALF

    def chunk_rows(k):
        return pl.ds(pl.multiple_of(k * chunk, chunk), chunk)

    def load(k):
        rows = chunk_rows(k)
        return pltpu.make_async_copy(
            factor_hbm.at[0, :, rows, :], factor.at[:, rows, :], load_sem.at[k]
        )

    def half_rows(col):
        return pl.ds(pl.multiple_of(col * share, share), share)

    def remote(src, dst, send_sem, recv_sem, device):
        return pltpu.make_async_remote_copy(
            src_ref=src, dst_ref=dst, send_sem=send_sem, recv_sem=recv_sem,
            device_id=device, device_id_type=MESH,
        )

    across = (s, r, other)
    after = (lax.rem(s + 1, n_sec), r, c)

    def part_rows(j):
        return pl.ds(pl.multiple_of(j * part, part), part)

    def send_source(j):
        rows = part_rows(j)
        at = lax.rem(j, 2)
        return remote(src_a.at[rows], src_a.at[rows], src_send.at[at], src_recv.at[at], across)

    before = (lax.rem(s + n_sec - 1, n_sec), r, c)

    partner = (s + 1 - 2 * lax.rem(s, 2), r, c)

    def send_block(i):
        k, m, first, stop = ((LENT, 3, 0, 4), (LENT + 1, 2, 0, 3), (LENT + 1, 0, 3, 4))[i]
        rows, cols = slice(k * chunk, (k + 1) * chunk), slice(first * part, stop * part)
        return remote(
            factor_hbm.at[0, :, rows, cols], corners[m], corner_send.at[m], corner_recv.at[m], partner
        )

    def send_lend(k):
        at = k - LENT
        return remote(own.at[k], own.at[k], lend_send.at[at], lend_recv.at[at], partner)

    def send_corner(m):
        rows, cols = slice(m * chunk, (m + 1) * chunk), slice(0, (m + 1) * part)
        return remote(
            factor_hbm.at[0, :, rows, cols], corners[m], corner_send.at[m], corner_recv.at[m], before
        )

    def send_scale():
        scales = dinv.at[0, :, slice(0, HALF * chunk)]
        return remote(scales, corner_scale, scale_send, scale_recv, before)

    def send_lent(j):
        rows = part_rows(j)
        return [
            remote(held.at[rows], held.at[rows], lent_send.at[i, j], lent_recv.at[i, j], partner)
            for i, held in enumerate((src_a, src_b))
        ]

    def send_help(j):
        return remote(help_out.at[j], help_in.at[j], help_send.at[j], help_recv.at[j], after)

    def send_rhs():
        return remote(forcing_t.at[c], forcing_t.at[c], rhs_send, rhs_recv, across)

    def send_coef():
        return remote(coupling_all.at[c], coupling_all.at[c], coef_send, coef_recv, across)

    def send_pre(k, h):
        rows = pl.ds(h * (chunk // SUBS), chunk // SUBS)
        at = k * SUBS + h
        return remote(
            pre_out.at[k, rows], pre_in.at[k, rows], pre_send.at[at], pre_recv.at[at],
            (s, lax.rem(r + 1, n_row), c),
        )

    def send_suf(k, h):
        rows = pl.ds(h * (chunk // SUBS), chunk // SUBS)
        at = k * SUBS + h
        return remote(
            suf_out.at[k, rows], suf_in.at[k, rows], suf_send.at[at], suf_recv.at[at],
            (s, lax.rem(r + n_row - 1, n_row), c),
        )

    def send_y(j):
        return remote(y_out.at[j], y_in.at[j], y_send.at[j], y_recv.at[j], across)

    beyond = (lax.rem(s + 1, n_sec), r, other)
    even = lax.rem(s, 2) == 0
    direct = jnp.logical_and(jnp.logical_and(paired, even), c == 1)
    split = jnp.logical_and(jnp.logical_and(paired, even), c == 0)
    summed = jnp.logical_and(jnp.logical_and(paired, jnp.logical_not(even)), c == 0)

    def send_direct(j):
        return remote(
            y_out.at[j], direct_in.at[j], direct_send.at[j], direct_recv.at[j], beyond
        )

    def send_prev(j):
        return remote(prev_out.at[j], prev_in.at[j], prev_send.at[j], prev_recv.at[j], after)

    count = jnp.int32(0)
    packed = {place: plan_words(*place[:2], plan) for place, plan in PLANS.items()}
    words = [jnp.int32(0)] * max(len(held) for _, held in packed.values())
    for (col, row, where), (length, held) in packed.items():
        mine = jnp.logical_and(c == col, r == row)
        if where:
            mine = jnp.logical_and(mine, lax.rem(s, 2) == 1 if where == 1 else s > 0)
        count = jnp.where(mine, length, count)
        for i, word in enumerate(held):
            words[i] = jnp.where(mine, word, words[i])

    for i in range(CHUNKS):
        k = (i + HALF) % CHUNKS

        @pl.when(jnp.logical_and(r <= last(k), jnp.logical_not(helped)) if k < HALF else r <= last(k))
        def _(k=k):
            load(k).start()

    barrier = pltpu.get_barrier_semaphore()
    for device in (
        (s, lax.rem(r + 1, n_row), c), (s, lax.rem(r + n_row - 1, n_row), c), across,
        after, before, beyond, (lax.rem(s + n_sec - 1, n_sec), r, other),
    ):
        pl.semaphore_signal(barrier, 1, device_id=device, device_id_type=MESH)

    def turned(value):
        return jnp.concatenate([-value[:, half:], value[:, :half]], axis=1)

    def product(k, cols):
        rows = chunk_rows(k)
        total = jnp.dot(factor[0, rows, cols], src_a[cols, :], preferred_element_type=jnp.float32)
        return total + jnp.dot(
            factor[1, rows, cols], src_b[cols, :], preferred_element_type=jnp.float32
        )

    def begin(first, stop):
        @pl.loop(first, stop)
        def _(i):
            k = lax.rem(i + HALF, CHUNKS)

            @pl.when(r < last(k))
            def _():
                load(k).wait()
                own[k] = product(k, half_rows(c))

    back[...] = jnp.zeros_like(back)

    @pl.when(s == 0)
    def _():
        src_a[half_rows(c), :] = forcing[0].astype(jnp.bfloat16)
        src_b[half_rows(c), :] = turned(forcing[0].astype(jnp.bfloat16).astype(jnp.float32)).astype(
            jnp.bfloat16
        )
        begin(0, EARLY)

    @pl.when(s > 0)
    def _():
        forcing_t[c] = forcing[0].T
        coupling_all[c] = coupling[0]

    pl.semaphore_wait(barrier, 7)

    @pl.when(s == 0)
    def _():
        @pl.when(needed)
        def _():
            for i in range(2):
                send_source(2 * c + i).start()

        begin(EARLY, BEGUN)
        pl.semaphore_signal(go, 1, device_id=after, device_id_type=MESH)

    @pl.when(s == 1)
    def _():
        pl.semaphore_wait(go, 1)

    @pl.when(helped)
    def _():
        send_scale().start()
        for m in range(PARTS):
            send_corner(m).start()

    @pl.when(lent)
    def _():
        for i in range(3):
            send_block(i).start()

    @pl.when(s > 0)
    def _():
        send_rhs().start()
        send_coef().start()
        send_rhs().wait_recv()
        send_coef().wait_recv()

    def enter(j, previous):
        rows = part_rows(j)
        col, cols = j // 2, part_rows(lax.rem(j, 2))
        p_re, p_im = previous[:half], previous[half:]
        c_re, c_im = coupling_all[col, 0:1, cols], coupling_all[col, 1:2, cols]
        new_re = forcing_t[col, :half, cols] - (c_re * p_re - c_im * p_im)
        new_im = forcing_t[col, half:, cols] - (c_re * p_im + c_im * p_re)
        src_a[rows, :] = jnp.concatenate([new_re, new_im], axis=0).T.astype(jnp.bfloat16)
        src_b[rows, :] = jnp.concatenate([-new_im, new_re], axis=0).T.astype(jnp.bfloat16)

    def source_step(j):
        rows = part_rows(j)

        @pl.when(jnp.logical_and(s == 0, j // 2 != c))
        def _():
            send_source(j).wait_recv()
            src_b[rows, :] = turned(src_a[rows, :].astype(jnp.float32)).astype(jnp.bfloat16)

        @pl.when(s > 0)
        def _():
            send_prev(j).wait_recv()

            @pl.when(summed)
            def _():
                send_direct(j).wait_recv()
                enter(j, prev_in[j].astype(jnp.float32) + direct_in[j].astype(jnp.float32))

            @pl.when(jnp.logical_not(summed))
            def _():
                enter(j, prev_in[j].astype(jnp.float32))

            @pl.when(jnp.logical_or(helped, lent))
            def _():
                for copy in send_lent(j):
                    copy.start()

    def keep(k, total):
        own[k] = total
        pre_out[k] = total.astype(jnp.bfloat16)
        suf_out[k] = total.astype(jnp.bfloat16)

    def forward_full(k):
        begun = jnp.logical_and(s == 0, lax.rem(k + HALF, CHUNKS) < BEGUN)

        @pl.when(begun)
        def _():
            keep(k, own[k] + product(k, half_rows(other)))

        @pl.when(jnp.logical_not(begun))
        def _():
            load(k).wait()
            keep(k, product(k, slice(0, PARTS * part)))

        @pl.when(r == 0)
        def _():
            for h in range(SUBS):
                send_pre(k, h).start()

    def forward_first(k):
        load(k).wait()
        own[k] = product(k, slice(0, 2 * part))

    def forward_second(k):
        keep(k, own[k] + product(k, slice(2 * part, 4 * part)))
        for h in range(SUBS):
            send_pre(k, h).start()

    def forward_lent(k):
        load(k).wait()
        send_lend(k).wait_recv()
        pre_out[k] = own[k].astype(jnp.bfloat16)
        suf_out[k] = own[k].astype(jnp.bfloat16)

        @pl.when(r == 0)
        def _():
            for h in range(SUBS):
                send_pre(k, h).start()

    def forward_diagonal(m, k):
        load(k).wait()
        keep(k, product(k, slice(0, (m + 1) * part)))

        @pl.when(r > 0)
        def _():
            for h in range(SUBS):
                send_suf(k, h).start()

    def relay(send, held, came, k):
        for h in range(SUBS):
            rows = slice(h * (chunk // SUBS), (h + 1) * (chunk // SUBS))
            send(k, h).wait_recv()
            held[k, rows, :] += came[k, rows, :]
            send(k, h).start()

    def relay_right(k):
        relay(send_pre, pre_out, pre_in, k)

    def relay_left(k):
        relay(send_suf, suf_out, suf_in, k)

    def gather(m, total, scale, block_re, block_im):
        forward = total.T
        d_re, d_im = scale[0:1], scale[1:2]
        f_re, f_im = forward[:half], forward[half:]
        s_re, s_im = d_re * f_re - d_im * f_im, d_re * f_im + d_im * f_re
        lhs_a = jnp.concatenate([s_re, s_im], axis=0).astype(jnp.bfloat16)
        lhs_b = jnp.concatenate([-s_im, s_re], axis=0).astype(jnp.bfloat16)
        total = jnp.dot(lhs_a, block_re, preferred_element_type=jnp.float32)
        total += jnp.dot(lhs_b, block_im, preferred_element_type=jnp.float32)
        for j in range(m + 1):
            back[j] += total[:, j * part : (j + 1) * part]

    def back_step(left, right, m, k):
        rows = chunk_rows(k)
        total = own[k]
        if left != right:
            for h in range(SUBS):
                (send_pre if left else send_suf)(k, h).wait_recv()
        if left:
            total += pre_in[k].astype(jnp.float32)
        if right:
            total += suf_in[k].astype(jnp.float32)
        cols = slice(0, (m + 1) * part)
        gather(m, total, dinv[0, :, rows], factor[0, rows, cols], factor[1, rows, cols])

    def act(action, k):
        kind = action[0]
        if kind == "F":
            if action[1] == PARTS:
                forward_full(k)
            else:
                forward_diagonal(action[1], k)
        elif kind == "B":
            back_step(action[1], action[2], action[3] if len(action) > 3 else PARTS - 1, k)
        else:
            {
                "R": relay_right, "L": relay_left, "S": source_step,
                "G": forward_first, "H": forward_second, "W": forward_lent,
            }[kind](k)

    def dispatch(step, first, stop, k):
        if stop - first == 1:
            act(ACTIONS[first], k)
            return
        middle = (first + stop) // 2

        @pl.when(step < middle)
        def _():
            dispatch(step, first, middle, k)

        @pl.when(step >= middle)
        def _():
            dispatch(step, middle, stop, k)

    def lend():
        for j in range(PARTS):
            for copy in send_lent(j):
                copy.wait_recv()
        send_block(0).wait_recv()
        total = jnp.dot(corners[3][0], src_a[...], preferred_element_type=jnp.float32)
        total += jnp.dot(corners[3][1], src_b[...], preferred_element_type=jnp.float32)
        own[LENT] = total
        send_lend(LENT).start()
        send_block(1).wait_recv()
        send_block(2).wait_recv()
        total = jnp.zeros((chunk, 2 * half), jnp.float32)
        for m, cols in ((2, slice(0, 3 * part)), (0, slice(3 * part, 4 * part))):
            total += jnp.dot(corners[m][0], src_a[cols, :], preferred_element_type=jnp.float32)
            total += jnp.dot(corners[m][1], src_b[cols, :], preferred_element_type=jnp.float32)
        own[LENT + 1] = total
        send_lend(LENT + 1).start()
        for k in (LENT, LENT + 1):
            send_lend(k).wait_send()

    @pl.when(jnp.logical_and(lends, ends))
    def _():
        lend()

    @pl.loop(0, count)
    def _(e):
        at = e // PER_WORD
        word = words[0]
        for i in range(1, len(words)):
            word = jnp.where(at == i, words[i], word)
        code = lax.rem(lax.shift_right_logical(word, 8 * lax.rem(e, PER_WORD)), 256)
        dispatch(code // CHUNKS, 0, len(ACTIONS), lax.rem(code, CHUNKS))

    @pl.when(helped)
    def _():
        for j in range(PARTS):
            send_help(j).wait_recv()
            back[j] += help_in[j].astype(jnp.float32)

    @pl.when(jnp.logical_and(s == 0, needed))
    def _():
        for i in range(2):
            send_source(2 * c + i).wait_send()

    @pl.when(lent)
    def _():
        for j in range(PARTS):
            for copy in send_lent(j):
                copy.wait_send()

    def order(first, i):
        return (2 * first + i) % PARTS if isinstance(first, int) else lax.rem(2 * first + i, PARTS)

    def sends_y(i):
        wanted = jnp.logical_or(paired, c == 1) if i < 2 else paired
        return wanted if i < 2 else jnp.logical_and(wanted, jnp.logical_not(ends))

    def takes_y(i):
        wanted = jnp.logical_or(paired, c == 0) if i < 2 else jnp.logical_and(paired, jnp.logical_not(split))
        return wanted if i < 2 else jnp.logical_and(wanted, jnp.logical_not(ends))

    behind = jnp.logical_or(direct, jnp.logical_and(jnp.logical_not(paired), c == 1))
    late = jnp.logical_and(jnp.logical_and(paired, c == 1), jnp.logical_not(jnp.logical_or(even, ends)))

    for i in range(PARTS):
        j = order(other, i)

        @pl.when(sends_y(i))
        def _(j=j):
            y_out[j] = back[j].astype(jnp.bfloat16)

        held = behind if i < 2 else jnp.logical_or(direct, late)

        @pl.when(jnp.logical_and(sends_y(i), jnp.logical_not(held)))
        def _(j=j):
            send_y(j).start()

    @pl.when(split)
    def _():
        for j in range(PARTS):
            prev_out[j] = back[j].astype(jnp.bfloat16)
            send_prev(j).start()

    passes = jnp.logical_and(active, jnp.logical_not(ends))
    for i in range(PARTS):
        j = order(c, i)

        @pl.when(takes_y(i))
        def _(j=j):
            send_y(j).wait_recv()
            back[j] += y_in[j].astype(jnp.float32)

        @pl.when(jnp.logical_and(passes, jnp.logical_not(split)))
        def _(j=j):
            prev_out[j] = back[j].astype(jnp.bfloat16)
            send_prev(j).start()

        @pl.when(direct)
        def _(i=i):
            send_direct(i).start()

        if i < 2:
            @pl.when(late)
            def _(i=i):
                send_y(2 + i).start()

    @pl.when(behind)
    def _():
        for i in range(2):
            send_y(i).start()

    for i in range(2):
        out[0, i * part : (i + 1) * part, :] = back[order(c, i)].T

    @pl.when(jnp.logical_and(lends, jnp.logical_not(ends)))
    def _():
        lend()

    @pl.when(helper)
    def _():
        back[...] = jnp.zeros_like(back)
        send_scale().wait_recv()
        for m in range(PARTS):
            send_corner(m).wait_recv()
            for copy in send_lent(m):
                copy.wait_recv()
            rows, cols = slice(m * chunk, (m + 1) * chunk), slice(0, (m + 1) * part)
            total = jnp.dot(corners[m][0], src_a[cols, :], preferred_element_type=jnp.float32)
            total += jnp.dot(corners[m][1], src_b[cols, :], preferred_element_type=jnp.float32)
            gather(m, total, corner_scale[:, rows], corners[m][0], corners[m][1])
        for j in range(PARTS):
            help_out[j] = back[j].astype(jnp.bfloat16)
            send_help(j).start()
        for j in range(PARTS):
            send_help(j).wait_send()

    @pl.when(lent)
    def _():
        for i in range(3):
            send_block(i).wait_send()

    @pl.when(helped)
    def _():
        send_scale().wait_send()
        for m in range(PARTS):
            send_corner(m).wait_send()
            for copy in send_lent(m):
                copy.wait_send()

    @pl.when(s > 0)
    def _():
        send_rhs().wait_send()
        send_coef().wait_send()

    for k in range(CHUNKS):
        @pl.when(r < last(k))
        def _(k=k):
            for h in range(SUBS):
                send_pre(k, h).wait_send()

        @pl.when(jnp.logical_and(r > 0, r <= last(k)))
        def _(k=k):
            for h in range(SUBS):
                send_suf(k, h).wait_send()

    for i in range(PARTS):
        @pl.when(direct)
        def _(i=i):
            send_direct(i).wait_send()

        @pl.when(jnp.logical_and(sends_y(i), jnp.logical_or(i < 2, jnp.logical_not(direct))))
        def _(i=i):
            send_y(order(other, i)).wait_send()

        @pl.when(passes)
        def _(i=i):
            send_prev(i).wait_send()


def sweep(n_sec, n_row, n_col, forcing, inverse_factor, diag_inverse, coupling):
    share, width = forcing.shape[1:]
    block_rows, block_cols = inverse_factor.shape[2:]
    chunk, part = block_rows // CHUNKS, block_cols // PARTS
    vmem = pl.BlockSpec(memory_space=pltpu.VMEM)
    bf16, f32 = jnp.bfloat16, jnp.float32
    dma = pltpu.SemaphoreType.DMA
    return pl.pallas_call(
        functools.partial(sweep_kernel, n_sec, n_row, n_col),
        out_shape=jax.ShapeDtypeStruct(forcing.shape, f32),
        in_specs=[vmem, vmem, vmem, pl.BlockSpec(memory_space=pl.ANY)],
        out_specs=vmem,
        scratch_shapes=[
            pltpu.VMEM((2, block_rows, block_cols), bf16),
            pltpu.VMEM((block_cols, width), bf16),
            pltpu.VMEM((block_cols, width), bf16),
            pltpu.VMEM((CHUNKS, chunk, width), f32),
            pltpu.VMEM((CHUNKS, chunk, width), bf16),
            pltpu.VMEM((CHUNKS, chunk, width), bf16),
            pltpu.VMEM((CHUNKS, chunk, width), bf16),
            pltpu.VMEM((CHUNKS, chunk, width), bf16),
            pltpu.VMEM((PARTS, width, part), f32),
            pltpu.VMEM((PARTS, width, part), bf16),
            pltpu.VMEM((PARTS, width, part), bf16),
            pltpu.VMEM((PARTS, width, part), bf16),
            pltpu.VMEM((PARTS, width, part), bf16),
            pltpu.VMEM((n_col, width, share), f32),
            pltpu.VMEM((n_col, 2, share), f32),
            dma((CHUNKS,)),
            dma((2,)), dma((2,)),
            dma((CHUNKS * SUBS,)), dma((CHUNKS * SUBS,)),
            dma((CHUNKS * SUBS,)), dma((CHUNKS * SUBS,)),
            dma((PARTS,)), dma((PARTS,)),
            dma((PARTS,)), dma((PARTS,)),
            dma, dma, dma, dma,
            pltpu.SemaphoreType.REGULAR,
            *[pltpu.VMEM((2, chunk, (m + 1) * part), bf16) for m in range(PARTS)],
            pltpu.VMEM((2, HALF * chunk), f32),
            pltpu.VMEM((PARTS, width, part), bf16),
            pltpu.VMEM((PARTS, width, part), bf16),
            dma((PARTS,)), dma((PARTS,)), dma, dma,
            dma((2, PARTS)), dma((2, PARTS)), dma((PARTS,)), dma((PARTS,)), dma((2,)), dma((2,)),
            pltpu.VMEM((PARTS, width, part), bf16), dma((PARTS,)), dma((PARTS,)),
        ],
        compiler_params=pltpu.CompilerParams(
            collective_id=0, has_side_effects=True, vmem_limit_bytes=60 * 2**20
        ),
    )(forcing, diag_inverse, coupling, inverse_factor)


def solution(mesh):
    placed = (
        P("sec", ("row", "col"), None),
        P("sec", None, "col", "row"),
        P("sec", None, "col"),
        P("sec", None, ("row", "col")),
    )
    n_sec, n_row, n_col = (mesh.shape[axis] for axis in ("sec", "row", "col"))

    def body(forcing, inverse_factor, diag_inverse, coupling):
        share, width = forcing.shape[1:]
        fits = inverse_factor.size * 2 <= 32 * 2**20
        block = inverse_factor.shape[2] == 4 * share and inverse_factor.shape[3] == 2 * share
        if share % 256 or width % 128 or not fits or n_sec != 4 or (n_row, n_col) != (4, 2) or not block:
            return local(forcing, inverse_factor, diag_inverse, coupling)
        return sweep(n_sec, n_row, n_col, forcing, inverse_factor, diag_inverse, coupling)

    return jax.shard_map(
        body, mesh=mesh, in_specs=placed, out_specs=P("sec", ("row", "col"), None), check_vma=False
    )
```

```python
import functools

import jax
import jax.numpy as jnp
from jax import lax
from jax.experimental import pallas as pl
from jax.experimental.pallas import tpu as pltpu
from jax.sharding import PartitionSpec as P


def shifted(value, axis, steps):
    count = lax.axis_size(axis)
    initial, last = (max(0, -steps), min(count, count - steps))
    return lax.ppermute(value, axis, [(source, source + steps) for source in range(initial, last)])


def complex_rows(coef_re, coef_im, values, half):
    v_re = values[:, :half]
    v_im = values[:, half:]
    out_re = coef_re[:, None] * v_re - coef_im[:, None] * v_im
    out_im = coef_re[:, None] * v_im + coef_im[:, None] * v_re
    return jnp.concatenate([out_re, out_im], axis=1)


def combine_stack(product):
    half = product.shape[2] // 2
    out_re = product[0, :, :half] - product[1, :, half:]
    out_im = product[0, :, half:] + product[1, :, :half]
    return jnp.concatenate([out_re, out_im], axis=1)


def solve_section(source, factor, dinv):
    width = source.shape[1]
    product = jnp.einsum(
        "kij,jb->kib",
        factor,
        lax.all_gather(source, "col", axis=0, tiled=True),
        preferred_element_type=jnp.float32,
    )
    forward = combine_stack(product)
    share = lax.psum_scatter(
        forward.astype(jnp.bfloat16), "row", scatter_dimension=0, tiled=True
    ).astype(jnp.float32)
    share_rows = share.shape[0]
    local_dinv = lax.dynamic_slice_in_dim(dinv, lax.axis_index("row") * share_rows, share_rows, 1)
    scaled = complex_rows(local_dinv[0], local_dinv[1], share, width // 2).astype(jnp.bfloat16)
    product = jnp.einsum(
        "kij,ib->kjb",
        factor,
        lax.all_gather(scaled, "row", axis=0, tiled=True),
        preferred_element_type=jnp.float32,
    )
    back = combine_stack(product)
    return lax.psum_scatter(
        back.astype(jnp.bfloat16), "col", scatter_dimension=0, tiled=True
    ).astype(jnp.float32)


def local(forcing, inverse_factor, diag_inverse, coupling):
    sections = lax.axis_size("sec")
    section_id = lax.axis_index("sec")
    local_rhs = forcing[0]
    factor = inverse_factor[0]
    dinv = diag_inverse[0]
    couple = coupling[0]
    rows_here = local_rhs.shape[0]
    half = local_rhs.shape[1] // 2
    block_count = 1
    block_width = half // block_count
    rhs_blocks = local_rhs.reshape(rows_here, 2, block_count, block_width)
    results = jnp.zeros((rows_here, 2, block_count, block_width), jnp.float32)
    outgoing = jnp.zeros((rows_here, 2 * block_width), jnp.float32)
    for step_index in range(block_count + sections - 1):
        if step_index > 0:
            incoming = shifted(outgoing.astype(jnp.bfloat16), "sec", 1).astype(outgoing.dtype)
        else:
            incoming = jnp.zeros((rows_here, 2 * block_width), jnp.float32)
        block_index = step_index - section_id
        active = jnp.logical_and(block_index >= 0, block_index < block_count)
        safe_index = jnp.clip(block_index, 0, block_count - 1)
        current = lax.dynamic_index_in_dim(rhs_blocks, safe_index, 2, keepdims=False)
        current = current.reshape(rows_here, 2 * block_width)
        source = (current - complex_rows(couple[0], couple[1], incoming, block_width)).astype(
            jnp.bfloat16
        )
        field = solve_section(source, factor, dinv)
        updated = lax.dynamic_update_index_in_dim(
            results, field.reshape(rows_here, 2, block_width), safe_index, 2
        )
        results = jnp.where(active, updated, results)
        outgoing = field
    return results.reshape(1, rows_here, 2 * half)


MESH = pl.DeviceIdType.MESH

CHUNKS = 8
SUBS = 2
HALF = CHUNKS // 2
PARTS = 4
EARLY = 2
BEGUN = 6
LENT = 6
PLANS = {
    (1, 0, 0): (
        0o40, 0o41, 0o42, 0o43, 0o04, 0o05, 0o06, 0o07, 0o00, 0o01, 0o02, 0o03, 0o30, 0o31, 0o34,
        0o32, 0o35, 0o36, 0o37, 0o33,
    ),
    (1, 1, 0): (
        0o40, 0o41, 0o42, 0o43, 0o04, 0o05, 0o00, 0o20, 0o01, 0o14, 0o21, 0o15, 0o06, 0o24, 0o16,
        0o07, 0o17, 0o02, 0o22, 0o25, 0o10, 0o26, 0o11, 0o03, 0o27, 0o12, 0o34, 0o23, 0o13, 0o35,
        0o30, 0o36, 0o31, 0o37, 0o32, 0o33,
    ),
    (1, 2, 0): (
        0o40, 0o41, 0o42, 0o43, 0o00, 0o04, 0o01, 0o05, 0o24, 0o02, 0o25, 0o06, 0o26, 0o07, 0o27,
        0o03, 0o14, 0o15, 0o34, 0o16, 0o35, 0o17, 0o36, 0o37, 0o30, 0o31, 0o32, 0o33,
    ),
    (1, 3, 0): (
        0o40, 0o41, 0o42, 0o43, 0o04, 0o05, 0o06, 0o07, 0o34, 0o35, 0o36, 0o37,
    ),
    (1, 0, 2): (
        0o40, 0o41, 0o42, 0o43, 0o04, 0o05, 0o00, 0o76, 0o77, 0o01, 0o02, 0o03, 0o30, 0o34, 0o31,
        0o35, 0o32, 0o36, 0o33, 0o37,
    ),
    (1, 1, 2): (
        0o40, 0o41, 0o42, 0o43, 0o04, 0o05, 0o00, 0o20, 0o01, 0o14, 0o76, 0o77, 0o21, 0o15, 0o02,
        0o24, 0o10, 0o16, 0o22, 0o03, 0o25, 0o17, 0o23, 0o11, 0o34, 0o26, 0o30, 0o12, 0o27, 0o35,
        0o13, 0o31, 0o36, 0o32, 0o37, 0o33,
    ),
    (1, 2, 2): (
        0o40, 0o41, 0o42, 0o43, 0o00, 0o04, 0o01, 0o05, 0o24, 0o76, 0o02, 0o25, 0o77, 0o03, 0o26,
        0o27, 0o14, 0o34, 0o15, 0o35, 0o16, 0o36, 0o17, 0o37, 0o30, 0o31, 0o32, 0o33,
    ),
    (0, 0, 0): (
        0o40, 0o00, 0o41, 0o01, 0o42, 0o02, 0o43, 0o04, 0o05, 0o06, 0o07, 0o03, 0o34, 0o35, 0o36,
        0o37, 0o30, 0o31, 0o32, 0o33,
    ),
    (0, 0, 1): (
        0o40, 0o41, 0o54, 0o55, 0o42, 0o56, 0o57, 0o43, 0o64, 0o65, 0o66, 0o67, 0o34, 0o35, 0o36,
        0o37,
    ),
    (0, 1, 0): (
        0o40, 0o04, 0o41, 0o05, 0o42, 0o06, 0o43, 0o07, 0o34, 0o35, 0o36, 0o37,
    ),
}
PER_WORD = 3
ACTIONS = [("F", m) for m in range(PARTS + 1)] + [("R",), ("L",), ("S",), ("G",), ("H",), ("W",)] + [("B", True, True), ("B", False, True)]
ACTIONS += [("B", left, False, m) for left in (True, False) for m in range(PARTS)]


def plan_words(col, row, plan):
    codes = []
    for step in plan:
        kind, k = "FRLBSGHW"[step // CHUNKS], step % CHUNKS
        end = 2 * col + k // HALF
        if kind == "F":
            action = ("F", k % HALF if row == end else PARTS)
        elif kind == "B":
            action = ("B", row > 0, row < end)
            action += () if row < end else (k % HALF,)
        else:
            action = (kind,)
        codes.append(ACTIONS.index(action) * CHUNKS + k)
    words = []
    for i in range(0, len(codes), PER_WORD):
        words.append(sum(code * 256**j for j, code in enumerate(codes[i : i + PER_WORD])))
    return len(codes), words


def sweep_kernel(
    n_sec, n_row, n_col, forcing, dinv, coupling, factor_hbm, out,
    factor, src_a, src_b, own, pre_in, suf_in, pre_out, suf_out,
    back, y_out, y_in, prev_out, prev_in, forcing_t, coupling_all,
    load_sem, src_send, src_recv, pre_send, pre_recv, suf_send, suf_recv,
    y_send, y_recv, prev_send, prev_recv,
    rhs_send, rhs_recv, coef_send, coef_recv, go,
    corner_0, corner_1, corner_2, corner_3, corner_scale, help_out, help_in,
    corner_send, corner_recv, scale_send, scale_recv, lent_send, lent_recv, help_send, help_recv, lend_send, lend_recv,
):
    corners = (corner_0, corner_1, corner_2, corner_3)
    chunk = own.shape[1]
    half = own.shape[2] // 2
    share = forcing_t.shape[2]
    part = back.shape[2]
    s, r, c = lax.axis_index("sec"), lax.axis_index("row"), lax.axis_index("col")
    other = 1 - c
    ends = s == n_sec - 1
    active = r <= 2 * c + 1
    paired = r < 2
    corner = jnp.logical_and(r == 0, c == 0)
    helped = jnp.logical_and(corner, lax.rem(s, 2) == 1)
    helper = jnp.logical_and(corner, lax.rem(s, 2) == 0)
    inner = jnp.logical_and(c == 1, r < n_row - 1)
    lent = jnp.logical_and(inner, s > 0)
    lends = jnp.logical_and(inner, s != 1)
    needed = jnp.logical_or(paired, c == 0)

    def last(k):
        return 2 * c + k // HALF

    def chunk_rows(k):
        return pl.ds(pl.multiple_of(k * chunk, chunk), chunk)

    def load(k):
        rows = chunk_rows(k)
        return pltpu.make_async_copy(
            factor_hbm.at[0, :, rows, :], factor.at[:, rows, :], load_sem.at[k]
        )

    def half_rows(col):
        return pl.ds(pl.multiple_of(col * share, share), share)

    def remote(src, dst, send_sem, recv_sem, device):
        return pltpu.make_async_remote_copy(
            src_ref=src, dst_ref=dst, send_sem=send_sem, recv_sem=recv_sem,
            device_id=device, device_id_type=MESH,
        )

    across = (s, r, other)
    after = (lax.rem(s + 1, n_sec), r, c)

    def part_rows(j):
        return pl.ds(pl.multiple_of(j * part, part), part)

    def send_source(j):
        rows = part_rows(j)
        at = lax.rem(j, 2)
        return remote(src_a.at[rows], src_a.at[rows], src_send.at[at], src_recv.at[at], across)

    before = (lax.rem(s + n_sec - 1, n_sec), r, c)

    partner = (s + 1 - 2 * lax.rem(s, 2), r, c)

    def send_block(i):
        k, m, first, stop = ((LENT, 3, 0, 4), (LENT + 1, 2, 0, 3), (LENT + 1, 0, 3, 4))[i]
        rows, cols = slice(k * chunk, (k + 1) * chunk), slice(first * part, stop * part)
        return remote(
            factor_hbm.at[0, :, rows, cols], corners[m], corner_send.at[m], corner_recv.at[m], partner
        )

    def send_lend(k):
        at = k - LENT
        return remote(own.at[k], own.at[k], lend_send.at[at], lend_recv.at[at], partner)

    def send_corner(m):
        rows, cols = slice(m * chunk, (m + 1) * chunk), slice(0, (m + 1) * part)
        return remote(
            factor_hbm.at[0, :, rows, cols], corners[m], corner_send.at[m], corner_recv.at[m], before
        )

    def send_scale():
        scales = dinv.at[0, :, slice(0, HALF * chunk)]
        return remote(scales, corner_scale, scale_send, scale_recv, before)

    def send_lent(j):
        rows = part_rows(j)
        return [
            remote(held.at[rows], held.at[rows], lent_send.at[i, j], lent_recv.at[i, j], partner)
            for i, held in enumerate((src_a, src_b))
        ]

    def send_help(j):
        return remote(help_out.at[j], help_in.at[j], help_send.at[j], help_recv.at[j], after)

    def send_rhs():
        return remote(forcing_t.at[c], forcing_t.at[c], rhs_send, rhs_recv, across)

    def send_coef():
        return remote(coupling_all.at[c], coupling_all.at[c], coef_send, coef_recv, across)

    def send_pre(k, h):
        rows = pl.ds(h * (chunk // SUBS), chunk // SUBS)
        at = k * SUBS + h
        return remote(
            pre_out.at[k, rows], pre_in.at[k, rows], pre_send.at[at], pre_recv.at[at],
            (s, lax.rem(r + 1, n_row), c),
        )

    def send_suf(k, h):
        rows = pl.ds(h * (chunk // SUBS), chunk // SUBS)
        at = k * SUBS + h
        return remote(
            suf_out.at[k, rows], suf_in.at[k, rows], suf_send.at[at], suf_recv.at[at],
            (s, lax.rem(r + n_row - 1, n_row), c),
        )

    def send_y(j):
        return remote(y_out.at[j], y_in.at[j], y_send.at[j], y_recv.at[j], across)

    def send_prev(j):
        return remote(prev_out.at[j], prev_in.at[j], prev_send.at[j], prev_recv.at[j], after)

    count = jnp.int32(0)
    packed = {place: plan_words(*place[:2], plan) for place, plan in PLANS.items()}
    words = [jnp.int32(0)] * max(len(held) for _, held in packed.values())
    for (col, row, where), (length, held) in packed.items():
        mine = jnp.logical_and(c == col, r == row)
        if where:
            mine = jnp.logical_and(mine, lax.rem(s, 2) == 1 if where == 1 else s > 0)
        count = jnp.where(mine, length, count)
        for i, word in enumerate(held):
            words[i] = jnp.where(mine, word, words[i])

    for i in range(CHUNKS):
        k = (i + HALF) % CHUNKS

        @pl.when(jnp.logical_and(r <= last(k), jnp.logical_not(helped)) if k < HALF else r <= last(k))
        def _(k=k):
            load(k).start()

    barrier = pltpu.get_barrier_semaphore()
    for device in (
        (s, lax.rem(r + 1, n_row), c), (s, lax.rem(r + n_row - 1, n_row), c), across,
        after, before,
    ):
        pl.semaphore_signal(barrier, 1, device_id=device, device_id_type=MESH)

    def turned(value):
        return jnp.concatenate([-value[:, half:], value[:, :half]], axis=1)

    def product(k, cols):
        rows = chunk_rows(k)
        total = jnp.dot(factor[0, rows, cols], src_a[cols, :], preferred_element_type=jnp.float32)
        return total + jnp.dot(
            factor[1, rows, cols], src_b[cols, :], preferred_element_type=jnp.float32
        )

    def begin(first, stop):
        @pl.loop(first, stop)
        def _(i):
            k = lax.rem(i + HALF, CHUNKS)

            @pl.when(r < last(k))
            def _():
                load(k).wait()
                own[k] = product(k, half_rows(c))

    back[...] = jnp.zeros_like(back)

    @pl.when(s == 0)
    def _():
        src_a[half_rows(c), :] = forcing[0].astype(jnp.bfloat16)
        src_b[half_rows(c), :] = turned(forcing[0].astype(jnp.bfloat16).astype(jnp.float32)).astype(
            jnp.bfloat16
        )
        begin(0, EARLY)

    @pl.when(s > 0)
    def _():
        forcing_t[c] = forcing[0].T
        coupling_all[c] = coupling[0]

    pl.semaphore_wait(barrier, 5)

    @pl.when(s == 0)
    def _():
        @pl.when(needed)
        def _():
            for i in range(2):
                send_source(2 * c + i).start()

        begin(EARLY, BEGUN)
        pl.semaphore_signal(go, 1, device_id=after, device_id_type=MESH)

    @pl.when(s == 1)
    def _():
        pl.semaphore_wait(go, 1)

    @pl.when(helped)
    def _():
        send_scale().start()
        for m in range(PARTS):
            send_corner(m).start()

    @pl.when(lent)
    def _():
        for i in range(3):
            send_block(i).start()

    @pl.when(s > 0)
    def _():
        send_rhs().start()
        send_coef().start()
        send_rhs().wait_recv()
        send_coef().wait_recv()

    def source_step(j):
        rows = part_rows(j)

        @pl.when(jnp.logical_and(s == 0, j // 2 != c))
        def _():
            send_source(j).wait_recv()
            src_b[rows, :] = turned(src_a[rows, :].astype(jnp.float32)).astype(jnp.bfloat16)

        @pl.when(s > 0)
        def _():
            send_prev(j).wait_recv()
            col, cols = j // 2, part_rows(lax.rem(j, 2))
            previous = prev_in[j].astype(jnp.float32)
            p_re, p_im = previous[:half], previous[half:]
            c_re, c_im = coupling_all[col, 0:1, cols], coupling_all[col, 1:2, cols]
            new_re = forcing_t[col, :half, cols] - (c_re * p_re - c_im * p_im)
            new_im = forcing_t[col, half:, cols] - (c_re * p_im + c_im * p_re)
            src_a[rows, :] = jnp.concatenate([new_re, new_im], axis=0).T.astype(jnp.bfloat16)
            src_b[rows, :] = jnp.concatenate([-new_im, new_re], axis=0).T.astype(jnp.bfloat16)

            @pl.when(jnp.logical_or(helped, lent))
            def _():
                for copy in send_lent(j):
                    copy.start()

    def keep(k, total):
        own[k] = total
        pre_out[k] = total.astype(jnp.bfloat16)
        suf_out[k] = total.astype(jnp.bfloat16)

    def forward_full(k):
        begun = jnp.logical_and(s == 0, lax.rem(k + HALF, CHUNKS) < BEGUN)

        @pl.when(begun)
        def _():
            keep(k, own[k] + product(k, half_rows(other)))

        @pl.when(jnp.logical_not(begun))
        def _():
            load(k).wait()
            keep(k, product(k, slice(0, PARTS * part)))

        @pl.when(r == 0)
        def _():
            for h in range(SUBS):
                send_pre(k, h).start()

    def forward_first(k):
        load(k).wait()
        own[k] = product(k, slice(0, 2 * part))

    def forward_second(k):
        keep(k, own[k] + product(k, slice(2 * part, 4 * part)))
        for h in range(SUBS):
            send_pre(k, h).start()

    def forward_lent(k):
        load(k).wait()
        send_lend(k).wait_recv()
        pre_out[k] = own[k].astype(jnp.bfloat16)
        suf_out[k] = own[k].astype(jnp.bfloat16)

        @pl.when(r == 0)
        def _():
            for h in range(SUBS):
                send_pre(k, h).start()

    def forward_diagonal(m, k):
        load(k).wait()
        keep(k, product(k, slice(0, (m + 1) * part)))

        @pl.when(r > 0)
        def _():
            for h in range(SUBS):
                send_suf(k, h).start()

    def relay(send, held, came, k):
        for h in range(SUBS):
            rows = slice(h * (chunk // SUBS), (h + 1) * (chunk // SUBS))
            send(k, h).wait_recv()
            held[k, rows, :] += came[k, rows, :]
            send(k, h).start()

    def relay_right(k):
        relay(send_pre, pre_out, pre_in, k)

    def relay_left(k):
        relay(send_suf, suf_out, suf_in, k)

    def gather(m, total, scale, block_re, block_im):
        forward = total.T
        d_re, d_im = scale[0:1], scale[1:2]
        f_re, f_im = forward[:half], forward[half:]
        s_re, s_im = d_re * f_re - d_im * f_im, d_re * f_im + d_im * f_re
        lhs_a = jnp.concatenate([s_re, s_im], axis=0).astype(jnp.bfloat16)
        lhs_b = jnp.concatenate([-s_im, s_re], axis=0).astype(jnp.bfloat16)
        total = jnp.dot(lhs_a, block_re, preferred_element_type=jnp.float32)
        total += jnp.dot(lhs_b, block_im, preferred_element_type=jnp.float32)
        for j in range(m + 1):
            back[j] += total[:, j * part : (j + 1) * part]

    def back_step(left, right, m, k):
        rows = chunk_rows(k)
        total = own[k]
        if left != right:
            for h in range(SUBS):
                (send_pre if left else send_suf)(k, h).wait_recv()
        if left:
            total += pre_in[k].astype(jnp.float32)
        if right:
            total += suf_in[k].astype(jnp.float32)
        cols = slice(0, (m + 1) * part)
        gather(m, total, dinv[0, :, rows], factor[0, rows, cols], factor[1, rows, cols])

    def act(action, k):
        kind = action[0]
        if kind == "F":
            if action[1] == PARTS:
                forward_full(k)
            else:
                forward_diagonal(action[1], k)
        elif kind == "B":
            back_step(action[1], action[2], action[3] if len(action) > 3 else PARTS - 1, k)
        else:
            {
                "R": relay_right, "L": relay_left, "S": source_step,
                "G": forward_first, "H": forward_second, "W": forward_lent,
            }[kind](k)

    def dispatch(step, first, stop, k):
        if stop - first == 1:
            act(ACTIONS[first], k)
            return
        middle = (first + stop) // 2

        @pl.when(step < middle)
        def _():
            dispatch(step, first, middle, k)

        @pl.when(step >= middle)
        def _():
            dispatch(step, middle, stop, k)

    def lend():
        for j in range(PARTS):
            for copy in send_lent(j):
                copy.wait_recv()
        send_block(0).wait_recv()
        total = jnp.dot(corners[3][0], src_a[...], preferred_element_type=jnp.float32)
        total += jnp.dot(corners[3][1], src_b[...], preferred_element_type=jnp.float32)
        own[LENT] = total
        send_lend(LENT).start()
        send_block(1).wait_recv()
        send_block(2).wait_recv()
        total = jnp.zeros((chunk, 2 * half), jnp.float32)
        for m, cols in ((2, slice(0, 3 * part)), (0, slice(3 * part, 4 * part))):
            total += jnp.dot(corners[m][0], src_a[cols, :], preferred_element_type=jnp.float32)
            total += jnp.dot(corners[m][1], src_b[cols, :], preferred_element_type=jnp.float32)
        own[LENT + 1] = total
        send_lend(LENT + 1).start()
        for k in (LENT, LENT + 1):
            send_lend(k).wait_send()

    @pl.when(jnp.logical_and(lends, ends))
    def _():
        lend()

    @pl.loop(0, count)
    def _(e):
        at = e // PER_WORD
        word = words[0]
        for i in range(1, len(words)):
            word = jnp.where(at == i, words[i], word)
        code = lax.rem(lax.shift_right_logical(word, 8 * lax.rem(e, PER_WORD)), 256)
        dispatch(code // CHUNKS, 0, len(ACTIONS), lax.rem(code, CHUNKS))

    @pl.when(helped)
    def _():
        for j in range(PARTS):
            send_help(j).wait_recv()
            back[j] += help_in[j].astype(jnp.float32)

    @pl.when(jnp.logical_and(s == 0, needed))
    def _():
        for i in range(2):
            send_source(2 * c + i).wait_send()

    @pl.when(lent)
    def _():
        for j in range(PARTS):
            for copy in send_lent(j):
                copy.wait_send()

    def order(first, i):
        return (2 * first + i) % PARTS if isinstance(first, int) else lax.rem(2 * first + i, PARTS)

    def sends_y(i):
        wanted = jnp.logical_or(paired, c == 1) if i < 2 else paired
        return wanted if i < 2 else jnp.logical_and(wanted, jnp.logical_not(ends))

    def takes_y(i):
        wanted = jnp.logical_or(paired, c == 0) if i < 2 else paired
        return wanted if i < 2 else jnp.logical_and(wanted, jnp.logical_not(ends))

    for i in range(PARTS):
        j = order(other, i)

        @pl.when(sends_y(i))
        def _(j=j):
            y_out[j] = back[j].astype(jnp.bfloat16)
            send_y(j).start()

    passes = jnp.logical_and(active, jnp.logical_not(ends))
    for i in range(PARTS):
        j = order(c, i)

        @pl.when(takes_y(i))
        def _(j=j):
            send_y(j).wait_recv()
            back[j] += y_in[j].astype(jnp.float32)

        @pl.when(passes)
        def _(j=j):
            prev_out[j] = back[j].astype(jnp.bfloat16)
            send_prev(j).start()

    for i in range(2):
        out[0, i * part : (i + 1) * part, :] = back[order(c, i)].T

    @pl.when(jnp.logical_and(lends, jnp.logical_not(ends)))
    def _():
        lend()

    @pl.when(helper)
    def _():
        back[...] = jnp.zeros_like(back)
        send_scale().wait_recv()
        for m in range(PARTS):
            send_corner(m).wait_recv()
            for copy in send_lent(m):
                copy.wait_recv()
            rows, cols = slice(m * chunk, (m + 1) * chunk), slice(0, (m + 1) * part)
            total = jnp.dot(corners[m][0], src_a[cols, :], preferred_element_type=jnp.float32)
            total += jnp.dot(corners[m][1], src_b[cols, :], preferred_element_type=jnp.float32)
            gather(m, total, corner_scale[:, rows], corners[m][0], corners[m][1])
        for j in range(PARTS):
            help_out[j] = back[j].astype(jnp.bfloat16)
            send_help(j).start()
        for j in range(PARTS):
            send_help(j).wait_send()

    @pl.when(lent)
    def _():
        for i in range(3):
            send_block(i).wait_send()

    @pl.when(helped)
    def _():
        send_scale().wait_send()
        for m in range(PARTS):
            send_corner(m).wait_send()
            for copy in send_lent(m):
                copy.wait_send()

    @pl.when(s > 0)
    def _():
        send_rhs().wait_send()
        send_coef().wait_send()

    for k in range(CHUNKS):
        @pl.when(r < last(k))
        def _(k=k):
            for h in range(SUBS):
                send_pre(k, h).wait_send()

        @pl.when(jnp.logical_and(r > 0, r <= last(k)))
        def _(k=k):
            for h in range(SUBS):
                send_suf(k, h).wait_send()

    for i in range(PARTS):
        @pl.when(sends_y(i))
        def _(i=i):
            send_y(order(other, i)).wait_send()

        @pl.when(passes)
        def _(i=i):
            send_prev(i).wait_send()


def sweep(n_sec, n_row, n_col, forcing, inverse_factor, diag_inverse, coupling):
    share, width = forcing.shape[1:]
    block_rows, block_cols = inverse_factor.shape[2:]
    chunk, part = block_rows // CHUNKS, block_cols // PARTS
    vmem = pl.BlockSpec(memory_space=pltpu.VMEM)
    bf16, f32 = jnp.bfloat16, jnp.float32
    dma = pltpu.SemaphoreType.DMA
    return pl.pallas_call(
        functools.partial(sweep_kernel, n_sec, n_row, n_col),
        out_shape=jax.ShapeDtypeStruct(forcing.shape, f32),
        in_specs=[vmem, vmem, vmem, pl.BlockSpec(memory_space=pl.ANY)],
        out_specs=vmem,
        scratch_shapes=[
            pltpu.VMEM((2, block_rows, block_cols), bf16),
            pltpu.VMEM((block_cols, width), bf16),
            pltpu.VMEM((block_cols, width), bf16),
            pltpu.VMEM((CHUNKS, chunk, width), f32),
            pltpu.VMEM((CHUNKS, chunk, width), bf16),
            pltpu.VMEM((CHUNKS, chunk, width), bf16),
            pltpu.VMEM((CHUNKS, chunk, width), bf16),
            pltpu.VMEM((CHUNKS, chunk, width), bf16),
            pltpu.VMEM((PARTS, width, part), f32),
            pltpu.VMEM((PARTS, width, part), bf16),
            pltpu.VMEM((PARTS, width, part), bf16),
            pltpu.VMEM((PARTS, width, part), bf16),
            pltpu.VMEM((PARTS, width, part), bf16),
            pltpu.VMEM((n_col, width, share), f32),
            pltpu.VMEM((n_col, 2, share), f32),
            dma((CHUNKS,)),
            dma((2,)), dma((2,)),
            dma((CHUNKS * SUBS,)), dma((CHUNKS * SUBS,)),
            dma((CHUNKS * SUBS,)), dma((CHUNKS * SUBS,)),
            dma((PARTS,)), dma((PARTS,)),
            dma((PARTS,)), dma((PARTS,)),
            dma, dma, dma, dma,
            pltpu.SemaphoreType.REGULAR,
            *[pltpu.VMEM((2, chunk, (m + 1) * part), bf16) for m in range(PARTS)],
            pltpu.VMEM((2, HALF * chunk), f32),
            pltpu.VMEM((PARTS, width, part), bf16),
            pltpu.VMEM((PARTS, width, part), bf16),
            dma((PARTS,)), dma((PARTS,)), dma, dma,
            dma((2, PARTS)), dma((2, PARTS)), dma((PARTS,)), dma((PARTS,)), dma((2,)), dma((2,)),
        ],
        compiler_params=pltpu.CompilerParams(
            collective_id=0, has_side_effects=True, vmem_limit_bytes=60 * 2**20
        ),
    )(forcing, diag_inverse, coupling, inverse_factor)


def solution(mesh):
    placed = (
        P("sec", ("row", "col"), None),
        P("sec", None, "col", "row"),
        P("sec", None, "col"),
        P("sec", None, ("row", "col")),
    )
    n_sec, n_row, n_col = (mesh.shape[axis] for axis in ("sec", "row", "col"))

    def body(forcing, inverse_factor, diag_inverse, coupling):
        share, width = forcing.shape[1:]
        fits = inverse_factor.size * 2 <= 32 * 2**20
        block = inverse_factor.shape[2] == 4 * share and inverse_factor.shape[3] == 2 * share
        if share % 256 or width % 128 or not fits or n_sec != 4 or (n_row, n_col) != (4, 2) or not block:
            return local(forcing, inverse_factor, diag_inverse, coupling)
        return sweep(n_sec, n_row, n_col, forcing, inverse_factor, diag_inverse, coupling)

    return jax.shard_map(
        body, mesh=mesh, in_specs=placed, out_specs=P("sec", ("row", "col"), None), check_vma=False
    )
```
